32 devices in a mesh: sec: 32 (over z, y, x, core).
Axes of the slice: x: 2, y: 2, z: 4, core: 2. Of those that a mesh axis runs over, the one named last changes fastest.
Arguments:
- front_reflect: float32 [32, 384, 384], P('sec'), may hold values from -0.125 to 0.125
- front_through: float32 [32, 384, 384], P('sec'), may hold values from -1 to 1
- back_reflect: float32 [32, 384, 384], P('sec'), may hold values from -0.125 to 0.125
- back_through: float32 [32, 384, 384], P('sec'), may hold values from -1 to 1
- depth_maps: float32 [32, 4, 384, 384], P('sec'), may hold values from -1 to 1
- incident: float32 [384, 128], replicated, may hold values from -6 to 6
Outputs:
- through_field: float32 [32, 384, 128], P('sec')
- reflected: float32 [32, 384, 128], P('sec')
- depth_fields: float32 [32, 4, 384, 128], P('sec')
The draws below stay inside these ranges and needn't reach their ends.
All inputs are finite; a program needn't handle non-finite values.
Results may differ from the reference program's by a relative error of at most 0.00013.
Values sent between devices are 32-bit elements; how exact they have to be, the bound alone decides.
No kernel may reach another device: no remote copies, remote signals or barrier semaphores. Data moves between devices by JAX's collectives and lax.ppermute only.
A program may use at most 64 MiB of HBM per device.

```python
import math
import jax
import jax.numpy as jnp
from jax import lax

M = 384
INC = 128
NEU = 3
SEGMENTS = 3
DEPTHS = 4
SECTIONS = 32
STRIDE = 4


def near_identity(key, extent):
    noise_key = jax.random.fold_in(key, 0)
    entries = jax.random.truncated_normal(noise_key, -2.0, 2.0, extent, jnp.float32)
    centre = jnp.full(extent[:-1] + (1,), 0.8, jnp.float32)
    identity = jnp.eye(M, dtype=jnp.float32)
    return centre * identity + 0.4 * entries / math.sqrt(M)


def draw_front_through(key, part):
    return near_identity(jax.random.fold_in(key, 101), (SECTIONS, M, M))


def draw_back_through(key, part):
    return near_identity(jax.random.fold_in(key, 202), (SECTIONS, M, M))


def draw_depth_maps(key, part):
    return near_identity(jax.random.fold_in(key, 303), (SECTIONS, DEPTHS, M, M))


def shard_levels(own_key, dims, shards, low, top_value):
    def one(position, shards_of):
        steps = jax.random.uniform(jax.random.fold_in(jax.random.fold_in(own_key, 6), position), (shards_of,), jnp.float32, low / len(shards), top_value / len(shards))
        return jnp.repeat(jnp.exp(steps), dims[position] // shards_of).reshape((-1,) + (1,) * (len(dims) - position - 1))

    gain = one(*shards[0])
    for cut in shards[1:]:
        gain = gain * one(*cut)
    return gain


def scatter_about(own_key, shape, width, most, cuts=(), kind=jnp.bfloat16):
    level = shard_levels(own_key, shape, cuts, -0.22, 0.18) if cuts else 1.0
    array = jax.random.normal(own_key, shape, jnp.float32) * width * level
    return jnp.minimum(jnp.maximum(array, -most), most).astype(kind)


def setup_inputs(seed: int = 0) -> dict:
    key_of = jax.random.split(jax.random.key(seed), 7)
    front_reflect = scatter_about(key_of[0], (SECTIONS, M, M), (5 * M) ** -0.5, 0.125, ((0, 32),), jnp.float32)
    front_through = draw_front_through(jax.random.fold_in(key_of[6], 71), 0)
    back_reflect = scatter_about(key_of[2], (SECTIONS, M, M), (5 * M) ** -0.5, 0.125, ((0, 32),), jnp.float32)
    back_through = draw_back_through(jax.random.fold_in(key_of[6], 71), 0)
    depth_maps = draw_depth_maps(jax.random.fold_in(key_of[6], 71), 0)
    incident = scatter_about(key_of[5], (M, INC), 1.0, 6.0, (), jnp.float32)
    return dict(front_reflect=front_reflect, front_through=front_through, back_reflect=back_reflect, back_through=back_through, depth_maps=depth_maps, incident=incident)


def product(former, latter):
    return jnp.matmul(former, latter, precision=lax.Precision.HIGHEST)


def series(bounce, identity):
    total = identity + bounce
    for _ in range(NEU - 1):
        total = identity + product(bounce, total)
    return total


def combine(upper, lower):
    upper_reflect, upper_through, upper_mirror, upper_return = upper
    lower_reflect, lower_through, lower_mirror, lower_return = lower
    identity = jnp.eye(M, dtype=jnp.float32)
    forward_sum = series(product(upper_mirror, lower_reflect), identity)
    reverse_sum = series(product(lower_reflect, upper_mirror), identity)
    g_through = product(forward_sum, upper_through)
    new_through = product(lower_through, g_through)
    new_reflect = upper_reflect + product(upper_return, product(lower_reflect, g_through))
    h_return = product(reverse_sum, lower_return)
    new_return = product(upper_return, h_return)
    new_mirror = lower_mirror + product(lower_through, product(upper_mirror, h_return))
    return (new_reflect, new_through, new_mirror, new_return)


def reference(front_reflect, front_through, back_reflect, back_through, depth_maps, incident):
    identity = jnp.eye(M, dtype=jnp.float32)
    current = (front_reflect, front_through, back_reflect, back_through)
    for level_index in range(SEGMENTS):
        distance = STRIDE * 2 ** level_index
        zeros = jnp.zeros((distance, M, M), jnp.float32)
        ones = jnp.broadcast_to(identity, (distance, M, M))
        upper = (
            jnp.concatenate([zeros, current[0][:-distance]], axis=0),
            jnp.concatenate([ones, current[1][:-distance]], axis=0),
            jnp.concatenate([zeros, current[2][:-distance]], axis=0),
            jnp.concatenate([ones, current[3][:-distance]], axis=0),
        )
        current = combine(upper, current)
    through_field = product(current[1], incident)
    reflected = product(current[0], incident)
    entering = jnp.concatenate([incident[None], through_field[:-1]], axis=0)
    depth_fields = jnp.einsum("sjmn,snc->sjmc", depth_maps, entering, precision=lax.Precision.HIGHEST)
    return (through_field, reflected, depth_fields)
```

```python
import jax
import jax.numpy as jnp
from jax import lax
from jax.sharding import PartitionSpec as P

SEGMENTS = 3
NODES = 2**SEGMENTS


def product(former, latter):
    return jnp.dot(
        former, latter, precision=lax.Precision.HIGH, preferred_element_type=jnp.float32
    )


def series(bounce, identity):
    partial_value = identity + bounce
    partial_value = identity + product(bounce, partial_value)
    return identity + product(bounce, partial_value)


def summed(bounce, value):
    total = value + product(bounce, value)
    total = value + product(bounce, total)
    return value + product(bounce, total)


def per_device(front_reflect, front_through, back_reflect, back_through, depth_maps, incident):
    length = lax.axis_size("sec")
    stride = length // NODES
    position = lax.axis_index("sec")
    node = position // stride

    def moved(value, routes):
        pairs = [(a * stride + r, b * stride + r) for a, b in routes for r in range(stride)]
        return lax.ppermute(value, "sec", pairs)

    def onward(value):
        return moved(value, [(k, k + 1) for k in range(NODES - 1)])

    identity = jnp.eye(front_reflect.shape[1], dtype=jnp.float32)
    r, t, q, u = front_reflect[0], front_through[0], back_reflect[0], back_through[0]
    first = node == 0

    q0, t0, u0, r0 = onward(q), onward(t), onward(u), onward(r)
    g = series(product(q0, r), identity)
    h = series(product(r, q0), identity)
    hu = product(h, u)
    q1 = q + product(t, product(q0, hu))
    gt = product(g, t0)
    t1 = jnp.where(first, t, product(t, gt))
    u1 = jnp.where(first, u, product(u0, hu))
    r1 = jnp.where(first, r, r0 + product(u0, product(r, gt)))

    low = [(0, 2), (1, 3)]
    f1 = product(t1, incident)
    s1 = product(r1, incident)
    rb = moved(r1, [(4, 2), (5, 3), (6, 4), (7, 5)])
    qa, ua, fa, sa = moved(q1, low), moved(u1, low), moved(f1, low), moved(s1, low)

    gt2 = summed(product(q1, rb), t1)
    r2 = r1 + product(u1, product(rb, gt2))
    rc = moved(r2, [(4, 2), (5, 3)])
    gtb = moved(gt2, [(2, 4), (3, 5), (4, 6), (5, 7)])

    hu2 = summed(product(r1, qa), u1)
    q2 = q1 + product(t1, product(qa, hu2))
    u2 = product(ua, hu2)
    g2 = summed(product(qa, r1), fa)
    f2 = product(t1, g2)
    s2 = sa + product(ua, product(r1, g2))

    g4 = summed(product(qa, r2), fa)
    s4 = sa + product(ua, product(r2, g4))
    t2 = product(t1, gtb)
    g4b, s4b = moved(g4, [(2, 4), (3, 5)]), moved(s4, [(2, 4), (3, 5)])

    g6 = summed(product(q2, rc), f2)
    g6b = moved(g6, [(2, 6), (3, 7)])
    s6 = s2 + product(u2, product(rc, g6))
    s6b = moved(s6, [(2, 6), (3, 7)])

    late = product(t2, g4b + g6b)
    through_field = jnp.where(node < 2, f1, jnp.where(node < 4, f2, late))
    reflected = jnp.where(node < 2, s1, jnp.where(node < 4, s2, s4b + s6b))
    entering = lax.ppermute(through_field, "sec", [(i, i + 1) for i in range(length - 1)])
    entering = jnp.where(position == 0, incident, entering)
    depth_fields = jnp.einsum(
        "jmn,nc->jmc",
        depth_maps[0],
        entering,
        precision=lax.Precision.HIGH,
        preferred_element_type=jnp.float32,
    )
    return (through_field[None], reflected[None], depth_fields[None])


def solution(mesh):
    in_specs = (
        P("sec", None, None),
        P("sec", None, None),
        P("sec", None, None),
        P("sec", None, None),
        P("sec", None, None, None),
        P(),
    )
    out_specs = (P("sec", None, None), P("sec", None, None), P("sec", None, None, None))
    return jax.shard_map(
        per_device, mesh=mesh, in_specs=in_specs, out_specs=out_specs, check_vma=False
    )
```

```python
import jax
import jax.numpy as jnp
from jax import lax
from jax.experimental import pallas as pl
from jax.experimental.pallas import tpu as pltpu
from jax.sharding import PartitionSpec as P

SEGMENTS = 3
NODES = 2**SEGMENTS
F32 = jnp.float32


def split(value):
    high = value.astype(jnp.bfloat16)
    return high, (value - high.astype(F32)).astype(jnp.bfloat16)


def left(value):
    high, low = split(value)
    return jnp.concatenate([high, high, low], axis=1)


def right(value):
    high, low = split(value)
    return jnp.concatenate([high, low, high], axis=0)


def product(former, latter):
    return jnp.dot(left(former), right(latter), preferred_element_type=F32)


def summed(bounce, value):
    factor = left(bounce)
    total = value
    for _ in range(3):
        total = value + jnp.dot(factor, right(total), preferred_element_type=F32)
    return total


def staged(body, node, inputs, outputs, products):
    def kernel(node_ref, *refs):
        refs[len(inputs)][0] = node_ref[0]
        body(node_ref[0], *refs[: len(inputs)], *refs[len(inputs) + 1 :])

    vmem, smem = pl.BlockSpec(memory_space=pltpu.VMEM), pl.BlockSpec(memory_space=pltpu.SMEM)
    side = inputs[0].shape[0]
    moved_bytes = 4 * side * side * (len(inputs) + len(outputs))
    results = pl.pallas_call(
        kernel,
        out_shape=[jax.ShapeDtypeStruct((1,), jnp.int32)]
        + [jax.ShapeDtypeStruct(shape, F32) for shape in outputs],
        in_specs=[smem] + [vmem] * len(inputs),
        out_specs=[smem] + [vmem] * len(outputs),
        cost_estimate=pl.CostEstimate(
            flops=int(products * 6 * side**3), bytes_accessed=moved_bytes, transcendentals=0
        ),
    )(node, *inputs)
    return results[0], results[1:]


def per_device(front_reflect, front_through, back_reflect, back_through, depth_maps, incident):
    length = lax.axis_size("sec")
    stride = length // NODES
    position = lax.axis_index("sec")
    k = position // stride
    node = k.astype(jnp.int32).reshape(1)
    square, field = front_reflect.shape[1:], incident.shape

    def moved(value, routes):
        pairs = [(a * stride + i, b * stride + i) for a, b in routes for i in range(stride)]
        return lax.ppermute(value, "sec", pairs)

    r, t, q, u = front_reflect[0], front_through[0], back_reflect[0], back_through[0]
    onward = [(0, 1), (1, 2), (2, 3), (3, 4), (4, 5)]
    low = [(0, 2), (1, 3)]
    back = [(4, 2), (5, 3)]

    q0 = moved(q, onward)
    swapped = moved(r, [(7, 6), (6, 7), (1, 0)])
    t0 = moved(t, onward)
    u0 = moved(u, onward)

    def pair_reflect(at):
        def body(k, came, r, t, q, u, *rest):
            out, gt_out = rest[-2:]

            @pl.when(k == at)
            def _():
                gt = summed(product(q[...], came[...]), t[...])
                gt_out[...] = gt
                out[...] = r[...] + product(u[...], product(came[...], gt))

            @pl.when(k != at)
            def _():
                out[...] = came[...]
                if len(rest) == 3:
                    gt_out[...] = rest[0][...]

        return body

    node, (relay, gt) = staged(pair_reflect(6), node, [swapped, r, t, q, u], [square] * 2, 6)
    hopped = moved(relay, [(6, 7), (7, 5), (0, 2)])

    def forward_q(k, q0, r, t, q, u, q1, hu_out):
        @pl.when(k == 0)
        def _():
            q1[...] = q[...]

        @pl.when((k > 0) & (k < 6))
        def _():
            hu = summed(product(r[...], q0[...]), u[...])
            hu_out[...] = hu
            q1[...] = q[...] + product(t[...], product(q0[...], hu))

    node, (q1, hu) = staged(forward_q, node, [q0, r, t, q, u], [square] * 2, 6)
    qa = moved(q1, low)

    r_late = moved(r, [(0, 1), (2, 3), (3, 2)])

    def forward_t(k, q0, t0, r, t, t1, rgt):
        @pl.when(k == 0)
        def _():
            t1[...] = t[...]

        @pl.when((k > 0) & (k < 6))
        def _():
            gt = summed(product(q0[...], r[...]), t0[...])
            rgt[...] = product(r[...], gt)
            t1[...] = product(t[...], gt)

    node, (t1, rgt) = staged(forward_t, node, [q0, t0, r, t], [square] * 2, 6)

    node, (relay, gt) = staged(pair_reflect(5), node, [hopped, r, t, q, u, gt], [square] * 2, 6)
    bounced = moved(relay, [(5, 4), (7, 5)])
    gt_came = moved(gt, [(5, 6), (6, 7)])
    r_next = moved(lax.optimization_barrier((r, relay))[0], [(4, 3)])

    def forward_u(k, u0, u, hu, rgt, u1, w):
        @pl.when(k == 0)
        def _():
            u1[...] = u[...]

        @pl.when((k > 0) & (k < 6))
        def _():
            factor = left(u0[...])
            w[...] = jnp.dot(factor, right(rgt[...]), preferred_element_type=F32)
            u1[...] = jnp.dot(factor, right(hu[...]), preferred_element_type=F32)

    node, (u1, w) = staged(forward_u, node, [u0, u, hu, rgt], [square] * 2, 2)
    w_came = moved(w, back)
    ua = moved(u1, low)

    def second_reflect(k, bounced, q1, t1, u1, w, total, gt_out):
        @pl.when((k == 4) | (k == 5))
        def _():
            gt = summed(product(q1[...], bounced[...]), t1[...])
            gt_out[...] = gt
            total[...] = w[...] + product(u1[...], product(bounced[...], gt))

    node, (total, gt2) = staged(
        second_reflect, node, [bounced, q1, t1, u1, w], [square] * 2, 6
    )
    total_came = moved(total, back)
    gt2_came = moved(gt2, [(4, 6), (5, 7)])

    def own_fields(k, r_late, hopped, r, w, t1, incident, r1, f1, s1):
        @pl.when(k == 0)
        def _():
            r1[...] = r[...]

        @pl.when(k == 2)
        def _():
            r1[...] = hopped[...] + w[...]

        @pl.when((k == 1) | (k == 3))
        def _():
            r1[...] = r_late[...] + w[...]

        @pl.when(k < 2)
        def _():
            f1[...] = product(t1[...], incident[...])
            s1[...] = product(r1[...], incident[...])

    node, (r1, f1, s1) = staged(
        own_fields, node, [r_late, hopped, r, w, t1, incident], [square, field, field], 1
    )
    fa, sa = moved(f1, low), moved(s1, low)

    def second_q(k, r1, qa, q1, t1, u1, q2, hu_out):
        @pl.when((k == 2) | (k == 3))
        def _():
            hu = summed(product(r1[...], qa[...]), u1[...])
            hu_out[...] = hu
            q2[...] = q1[...] + product(t1[...], product(qa[...], hu))

    node, (q2, hu2) = staged(second_q, node, [r1, qa, q1, t1, u1], [square] * 2, 6)

    def second_fields(k, qa, ua, fa, sa, hu2, r1, t1, u2, f2, s2):
        @pl.when((k == 2) | (k == 3))
        def _():
            g = summed(product(qa[...], r1[...]), fa[...])
            f2[...] = product(t1[...], g)
            s2[...] = sa[...] + product(ua[...], product(r1[...], g))
            u2[...] = product(ua[...], hu2[...])

    node, (u2, f2, s2) = staged(
        second_fields, node, [qa, ua, fa, sa, hu2, r1, t1], [square, field, field], 4
    )

    def third_fields(k, r_late, r_next, w_came, q1, t1, u1, r1, qa, ua, fa, sa, w4, s4):
        @pl.when((k == 2) | (k == 3))
        def _():
            came = jnp.where(k == 2, r_late[...], r_next[...]) + w_came[...]
            gt = summed(product(q1[...], came), t1[...])
            rc = r1[...] + product(u1[...], product(came, gt))
            g = summed(product(qa[...], rc), fa[...])
            w4[...] = product(gt, g)
            s4[...] = sa[...] + product(ua[...], product(rc, g))

    node, (w4, s4) = staged(
        third_fields,
        node,
        [r_late, r_next, w_came, q1, t1, u1, r1, qa, ua, fa, sa],
        [field] * 2,
        9,
    )
    w4_came, s4_came = moved(w4, [(2, 4), (3, 5)]), moved(s4, [(2, 4), (3, 5)])

    def second_through(k, t, gt_came, gt2_came, t2):
        @pl.when(k > 5)
        def _():
            t2[...] = product(product(t[...], gt_came[...]), gt2_came[...])

    node, (t2,) = staged(second_through, node, [t, gt_came, gt2_came], [square], 2)

    def last_fields(k, r_late, r_next, total_came, q2, f2, g6, rg6):
        @pl.when((k == 2) | (k == 3))
        def _():
            rc = jnp.where(k == 2, r_late[...], r_next[...]) + total_came[...]
            g = summed(product(q2[...], rc), f2[...])
            g6[...] = g
            rg6[...] = product(rc, g)

    node, (g6, rg6) = staged(
        last_fields, node, [r_late, r_next, total_came, q2, f2], [field] * 2, 3
    )
    g6_came = moved(g6, [(2, 6), (3, 7)])

    def last_reflected(k, s2, u2, rg6, s6):
        @pl.when((k == 2) | (k == 3))
        def _():
            s6[...] = s2[...] + product(u2[...], rg6[...])

    node, (s6,) = staged(last_reflected, node, [s2, u2, rg6], [field], 1)
    s6_came = moved(s6, [(2, 6), (3, 7)])

    def through(k, f1, f2, t1, w4, t2, g6, out):
        @pl.when(k < 2)
        def _():
            out[...] = f1[...]

        @pl.when((k == 2) | (k == 3))
        def _():
            out[...] = f2[...]

        @pl.when((k == 4) | (k == 5))
        def _():
            out[...] = product(t1[...], w4[...])

        @pl.when(k > 5)
        def _():
            out[...] = product(t2[...], g6[...])

    node, (through_field,) = staged(
        through, node, [f1, f2, t1, w4_came, t2, g6_came], [field], 1
    )
    entering = lax.ppermute(through_field, "sec", [(i, i + 1) for i in range(length - 1)])
    reflected = jnp.where(
        k < 2, s1, jnp.where(k < 4, s2, jnp.where(k < 6, s4_came, s6_came))
    )

    place = position.astype(jnp.int32).reshape(1)

    def depths(place, maps, entering, incident, out):
        value = right(jnp.where(place == 0, incident[...], entering[...]))
        for j in range(depth_maps.shape[1]):
            out[j] = jnp.dot(left(maps[j]), value, preferred_element_type=F32)

    _, (depth_fields,) = staged(
        depths,
        place,
        [depth_maps[0], entering, incident],
        [depth_maps.shape[1:3] + field[1:]],
        1,
    )
    return (through_field[None], reflected[None], depth_fields[None])


def solution(mesh):
    in_specs = (
        P("sec", None, None),
        P("sec", None, None),
        P("sec", None, None),
        P("sec", None, None),
        P("sec", None, None, None),
        P(),
    )
    out_specs = (P("sec", None, None), P("sec", None, None), P("sec", None, None, None))
    return jax.shard_map(
        per_device, mesh=mesh, in_specs=in_specs, out_specs=out_specs, check_vma=False
    )
```

```python
import jax
import jax.numpy as jnp
from jax import lax
from jax.experimental import pallas as pl
from jax.experimental.pallas import tpu as pltpu
from jax.sharding import PartitionSpec as P

SEGMENTS = 3
NODES = 2**SEGMENTS
F32 = jnp.float32


def split(value):
    high = value.astype(jnp.bfloat16)
    return high, (value - high.astype(F32)).astype(jnp.bfloat16)


def left(value):
    high, low = split(value)
    return jnp.concatenate([high, high, low], axis=1)


def right(value):
    high, low = split(value)
    return jnp.concatenate([high, low, high], axis=0)


def product(former, latter):
    return jnp.dot(left(former), right(latter), preferred_element_type=F32)


def summed(bounce, value):
    factor = left(bounce)
    total = value
    for _ in range(3):
        total = value + jnp.dot(factor, right(total), preferred_element_type=F32)
    return total


def staged(body, stride, inputs, outputs, products):
    def kernel(*refs):
        body(lax.axis_index("sec") // stride, *refs)

    vmem = pl.BlockSpec(memory_space=pltpu.VMEM)
    side = inputs[0].shape[0]
    moved_bytes = 4 * side * side * (len(inputs) + len(outputs))
    return pl.pallas_call(
        kernel,
        out_shape=[jax.ShapeDtypeStruct(shape, F32) for shape in outputs],
        in_specs=[vmem] * len(inputs),
        out_specs=[vmem] * len(outputs),
        compiler_params=pltpu.CompilerParams(vmem_limit_bytes=24 * 2**20),
        cost_estimate=pl.CostEstimate(flops=int(products * 6 * side**3), bytes_accessed=moved_bytes, transcendentals=0),
    )(*inputs)


def per_device(front_reflect, front_through, back_reflect, back_through, depth_maps, incident):
    length = lax.axis_size("sec")
    stride = length // NODES
    position = lax.axis_index("sec")
    k = position // stride
    square, field = front_reflect.shape[1:], incident.shape

    def moved(value, routes):
        pairs = [(a * stride + i, b * stride + i) for a, b in routes for i in range(stride)]
        return lax.ppermute(value, "sec", pairs)

    r, t, q, u = front_reflect[0], front_through[0], back_reflect[0], back_through[0]
    onward = [(0, 1), (1, 2), (2, 3), (3, 4), (4, 5)]
    low = [(0, 2), (1, 3)]
    back = [(4, 2), (5, 3)]

    q0 = moved(q, onward)
    swapped = moved(r, [(7, 6), (6, 7), (1, 0)])
    t0 = moved(t, onward)
    u0 = moved(u, onward)

    def pair_reflect(at):
        def body(k, came, r, t, q, u, *rest):
            out, gt_out = rest[-2:]

            @pl.when(k == at)
            def _():
                gt = summed(product(q[...], came[...]), t[...])
                gt_out[...] = gt
                out[...] = r[...] + product(u[...], product(came[...], gt))

            @pl.when(k != at)
            def _():
                out[...] = came[...]
                if len(rest) == 3:
                    gt_out[...] = rest[0][...]

        return body

    (relay, gt) = staged(pair_reflect(6), stride, [swapped, r, t, q, u], [square] * 2, 6)
    hopped = moved(relay, [(6, 7), (7, 5), (0, 2)])

    def forward_q(k, q0, r, t, q, u, q1, hu_out):
        @pl.when(k == 0)
        def _():
            q1[...] = q[...]

        @pl.when((k > 0) & (k < 6))
        def _():
            hu = summed(product(r[...], q0[...]), u[...])
            hu_out[...] = hu
            q1[...] = q[...] + product(t[...], product(q0[...], hu))

    (q1, hu) = staged(forward_q, stride, [q0, r, t, q, u], [square] * 2, 6)
    qa = moved(q1, low)

    r_late = moved(r, [(0, 1), (2, 3), (3, 2)])

    def forward_t(k, q0, t0, r, t, t1, rgt):
        @pl.when(k == 0)
        def _():
            t1[...] = t[...]

        @pl.when((k > 0) & (k < 6))
        def _():
            gt = summed(product(q0[...], r[...]), t0[...])
            rgt[...] = product(r[...], gt)
            t1[...] = product(t[...], gt)

    (t1, rgt) = staged(forward_t, stride, [q0, t0, r, t], [square] * 2, 6)

    (relay, gt) = staged(pair_reflect(5), stride, [hopped, r, t, q, u, gt], [square] * 2, 6)
    bounced = moved(relay, [(5, 4), (7, 5)])
    gt_came = moved(gt, [(5, 6), (6, 7)])
    r_next = moved(lax.optimization_barrier((r, relay))[0], [(4, 3)])

    def forward_u(k, u0, u, hu, rgt, u1, w):
        @pl.when(k == 0)
        def _():
            u1[...] = u[...]

        @pl.when((k > 0) & (k < 6))
        def _():
            factor = left(u0[...])
            w[...] = jnp.dot(factor, right(rgt[...]), preferred_element_type=F32)
            u1[...] = jnp.dot(factor, right(hu[...]), preferred_element_type=F32)

    (u1, w) = staged(forward_u, stride, [u0, u, hu, rgt], [square] * 2, 2)
    w_came = moved(w, back)
    ua = moved(u1, low)

    def second_reflect(k, bounced, q1, t1, u1, w, total, gt_out):
        @pl.when((k == 4) | (k == 5))
        def _():
            gt = summed(product(q1[...], bounced[...]), t1[...])
            gt_out[...] = gt
            total[...] = w[...] + product(u1[...], product(bounced[...], gt))

    (total, gt2) = staged(second_reflect, stride, [bounced, q1, t1, u1, w], [square] * 2, 6
    )
    total_came = moved(total, back)
    gt2_came = moved(gt2, [(4, 6), (5, 7)])

    def own_fields(k, r_late, hopped, r, w, t1, incident, r1, f1, s1):
        @pl.when(k == 0)
        def _():
            r1[...] = r[...]

        @pl.when(k == 2)
        def _():
            r1[...] = hopped[...] + w[...]

        @pl.when((k == 1) | (k == 3))
        def _():
            r1[...] = r_late[...] + w[...]

        @pl.when(k < 2)
        def _():
            f1[...] = product(t1[...], incident[...])
            s1[...] = product(r1[...], incident[...])

    (r1, f1, s1) = staged(own_fields, stride, [r_late, hopped, r, w, t1, incident], [square, field, field], 1
    )
    fa = moved(f1, low)
    sa = moved(s1, low)

    def second_q(k, r1, qa, q1, t1, u1, q2, hu_out):
        @pl.when((k == 2) | (k == 3))
        def _():
            hu = summed(product(r1[...], qa[...]), u1[...])
            hu_out[...] = hu
            q2[...] = q1[...] + product(t1[...], product(qa[...], hu))

    (q2, hu2) = staged(second_q, stride, [r1, qa, q1, t1, u1], [square] * 2, 6)

    def second_fields(k, qa, ua, fa, sa, hu2, r1, t1, u2, f2, s2):
        @pl.when((k == 2) | (k == 3))
        def _():
            g = summed(product(qa[...], r1[...]), fa[...])
            f2[...] = product(t1[...], g)
            s2[...] = sa[...] + product(ua[...], product(r1[...], g))
            u2[...] = product(ua[...], hu2[...])

    (u2, f2, s2) = staged(second_fields, stride, [qa, ua, fa, sa, hu2, r1, t1], [square, field, field], 4
    )

    def third_fields(k, r_late, r_next, w_came, q1, t1, u1, r1, qa, ua, fa, sa, w4, s4):
        @pl.when((k == 2) | (k == 3))
        def _():
            came = jnp.where(k == 2, r_late[...], r_next[...]) + w_came[...]
            gt = summed(product(q1[...], came), t1[...])
            rc = r1[...] + product(u1[...], product(came, gt))
            g = summed(product(qa[...], rc), fa[...])
            w4[...] = product(gt, g)
            s4[...] = sa[...] + product(ua[...], product(rc, g))

    (w4, s4) = staged(third_fields, stride,
        [r_late, r_next, w_came, q1, t1, u1, r1, qa, ua, fa, sa],
        [field] * 2,
        9,
    )
    w4_came = moved(w4, [(2, 4), (3, 5)])
    s4_came = moved(s4, [(2, 4), (3, 5)])

    def second_through(k, t, gt_came, gt2_came, t2):
        @pl.when(k > 5)
        def _():
            t2[...] = product(product(t[...], gt_came[...]), gt2_came[...])

    (t2,) = staged(second_through, stride, [t, gt_came, gt2_came], [square], 2)

    def last_fields(k, r_late, r_next, total_came, q2, f2, g6, rg6):
        @pl.when((k == 2) | (k == 3))
        def _():
            rc = jnp.where(k == 2, r_late[...], r_next[...]) + total_came[...]
            g = summed(product(q2[...], rc), f2[...])
            g6[...] = g
            rg6[...] = product(rc, g)

    (g6, rg6) = staged(last_fields, stride, [r_late, r_next, total_came, q2, f2], [field] * 2, 3
    )
    g6_came = moved(g6, [(2, 6), (3, 7)])

    def last_reflected(k, s2, u2, rg6, s6):
        @pl.when((k == 2) | (k == 3))
        def _():
            s6[...] = s2[...] + product(u2[...], rg6[...])

    (s6,) = staged(last_reflected, stride, [s2, u2, rg6], [field], 1)
    s6_came = moved(s6, [(2, 6), (3, 7)])

    def through(k, f1, f2, t1, w4, t2, g6, out):
        @pl.when(k < 2)
        def _():
            out[...] = f1[...]

        @pl.when((k == 2) | (k == 3))
        def _():
            out[...] = f2[...]

        @pl.when((k == 4) | (k == 5))
        def _():
            out[...] = product(t1[...], w4[...])

        @pl.when(k > 5)
        def _():
            out[...] = product(t2[...], g6[...])

    (through_field,) = staged(through, stride, [f1, f2, t1, w4_came, t2, g6_came], [field], 1
    )
    entering = lax.ppermute(through_field, "sec", [(i, i + 1) for i in range(length - 1)])
    reflected = jnp.where(
        k < 2, s1, jnp.where(k < 4, s2, jnp.where(k < 6, s4_came, s6_came))
    )

    def depths(place, maps, entering, incident, out):
        value = right(jnp.where(place == 0, incident[...], entering[...]))
        for j in range(depth_maps.shape[1]):
            out[j] = jnp.dot(left(maps[j]), value, preferred_element_type=F32)

    (depth_fields,) = staged(depths, 1, [depth_maps[0], entering, incident], [depth_maps.shape[1:3] + field[1:]], 1)
    return (through_field[None], reflected[None], depth_fields[None])


def solution(mesh):
    in_specs = (
        P("sec", None, None),
        P("sec", None, None),
        P("sec", None, None),
        P("sec", None, None),
        P("sec", None, None, None),
        P(),
    )
    out_specs = (P("sec", None, None), P("sec", None, None), P("sec", None, None, None))

    return jax.shard_map(per_device, mesh=mesh, in_specs=in_specs, out_specs=out_specs, check_vma=False)
```

```python
import jax
import jax.numpy as jnp
from jax import lax
from jax.experimental import pallas as pl
from jax.experimental.pallas import tpu as pltpu
from jax.sharding import PartitionSpec as P

SEGMENTS = 3
NODES = 2**SEGMENTS
F32 = jnp.float32


def split(value):
    high = value.astype(jnp.bfloat16)
    return high, (value - high.astype(F32)).astype(jnp.bfloat16)


def left(value):
    high, low = split(value)
    return jnp.concatenate([high, high, low], axis=1)


def right(value):
    high, low = split(value)
    return jnp.concatenate([high, low, high], axis=0)


def product(former, latter):
    return jnp.dot(left(former), right(latter), preferred_element_type=F32)


def summed(bounce, value):
    factor = left(bounce)
    total = value
    for _ in range(3):
        total = value + jnp.dot(factor, right(total), preferred_element_type=F32)
    return total


def staged(body, stride, inputs, outputs, products):
    def kernel(*refs):
        body(lax.axis_index("sec") // stride, *refs)

    vmem = pl.BlockSpec(memory_space=pltpu.VMEM)
    side = inputs[0].shape[0]
    moved_bytes = 4 * side * side * (len(inputs) + len(outputs))
    return pl.pallas_call(
        kernel,
        out_shape=[jax.ShapeDtypeStruct(shape, F32) for shape in outputs],
        in_specs=[vmem] * len(inputs),
        out_specs=[vmem] * len(outputs),
        compiler_params=pltpu.CompilerParams(vmem_limit_bytes=24 * 2**20),
        cost_estimate=pl.CostEstimate(flops=int(products * 6 * side**3), bytes_accessed=moved_bytes, transcendentals=0),
    )(*inputs)


def per_device(front_reflect, front_through, back_reflect, back_through, depth_maps, incident):
    length = lax.axis_size("sec")
    stride = length // NODES
    position = lax.axis_index("sec")
    k = position // stride
    square, field = front_reflect.shape[1:], incident.shape

    def moved(value, routes):
        pairs = [(a * stride + i, b * stride + i) for a, b in routes for i in range(stride)]
        return lax.ppermute(value, "sec", pairs)

    r, t, q, u = front_reflect[0], front_through[0], back_reflect[0], back_through[0]
    onward = [(0, 1), (1, 2), (2, 3), (3, 4), (4, 5)]
    low = [(0, 2), (1, 3)]
    back = [(4, 2), (5, 3)]

    q0 = moved(q, onward)
    swapped = moved(r, [(7, 6), (6, 7), (1, 0), (0, 1)])
    t0 = moved(t, onward)
    u0 = moved(u, onward)

    def load(k, *refs):
        for i in range(4):
            refs[4 + i][...] = refs[i][...]

    r_in, (r, t, q, u) = r, staged(load, stride, [r, t, q, u], [square] * 4, 0.1)

    def pair_reflect(at):
        def body(k, came, r, t, q, u, *rest):
            out, gt_out = rest[-2:]

            @pl.when(k == at)
            def _():
                gt = summed(product(q[...], came[...]), t[...])
                gt_out[...] = gt
                out[...] = r[...] + product(u[...], product(came[...], gt))

            @pl.when(k != at)
            def _():
                out[...] = came[...]
                if len(rest) == 3:
                    gt_out[...] = rest[0][...]

        return body

    (relay, gt) = staged(pair_reflect(6), stride, [swapped, r, t, q, u], [square] * 2, 6)
    hopped = moved(relay, [(6, 7), (7, 5), (0, 2)])

    def forward_q(k, q0, r, t, q, u, q1, hu_out):
        @pl.when(k == 0)
        def _():
            q1[...] = q[...]

        @pl.when((k > 0) & (k < 6))
        def _():
            hu = summed(product(r[...], q0[...]), u[...])
            hu_out[...] = hu
            q1[...] = q[...] + product(t[...], product(q0[...], hu))

    (q1, hu) = staged(forward_q, stride, [q0, r, t, q, u], [square] * 2, 6)
    qa = moved(q1, low)


    def forward_t(k, q0, t0, r, t, t1, rgt):
        @pl.when(k == 0)
        def _():
            t1[...] = t[...]

        @pl.when((k > 0) & (k < 6))
        def _():
            gt = summed(product(q0[...], r[...]), t0[...])
            rgt[...] = product(r[...], gt)
            t1[...] = product(t[...], gt)

    (t1, rgt) = staged(forward_t, stride, [q0, t0, r, t], [square] * 2, 6)

    (relay, gt) = staged(pair_reflect(5), stride, [hopped, r, t, q, u, gt], [square] * 2, 6)
    bounced = moved(relay, [(5, 4), (7, 5)])
    gt_came = moved(gt, [(5, 6), (6, 7)])
    r_late = moved(r_in, [(2, 3), (3, 2)])
    r_next = moved(r_in, [(4, 3)])

    def forward_u(k, u0, u, hu, rgt, u1, w):
        @pl.when(k == 0)
        def _():
            u1[...] = u[...]

        @pl.when((k > 0) & (k < 6))
        def _():
            factor = left(u0[...])
            w[...] = jnp.dot(factor, right(rgt[...]), preferred_element_type=F32)
            u1[...] = jnp.dot(factor, right(hu[...]), preferred_element_type=F32)

    (u1, w) = staged(forward_u, stride, [u0, u, hu, rgt], [square] * 2, 2)
    w_came = moved(w, back)
    ua = moved(u1, low)

    def low_fields(k, swapped, r, w, t1, incident, f1, s1):
        @pl.when(k < 2)
        def _():
            whole = jnp.where(k == 0, r[...], swapped[...] + w[...])
            value = right(incident[...])
            f1[...] = jnp.dot(left(t1[...]), value, preferred_element_type=F32)
            s1[...] = jnp.dot(left(whole), value, preferred_element_type=F32)

    (f1, s1) = staged(low_fields, stride, [swapped, r, w, t1, incident], [field, field], 1)
    fa = moved(f1, low)
    sa = moved(s1, low)

    def open_gate(k, w, out):
        out[...] = w[:8, :128]

    (gate,) = staged(open_gate, stride, [w], [(8, 128)], 0.1)

    def second_reflect(k, bounced, q1, t1, u1, w, gate, total, gt_out):
        @pl.when((k == 4) | (k == 5))
        def _():
            gt = summed(product(q1[...], bounced[...]), t1[...])
            gt_out[...] = gt
            total[...] = w[...] + product(u1[...], product(bounced[...], gt))

    (total, gt2) = staged(second_reflect, stride, [bounced, q1, t1, u1, w, gate], [square] * 2, 6
    )
    total_came = moved(total, back)
    gt2_came = moved(gt2, [(4, 6), (5, 7)])

    def own_fields(k, r_late, hopped, w, r1):
        @pl.when(k == 2)
        def _():
            r1[...] = hopped[...] + w[...]

        @pl.when(k == 3)
        def _():
            r1[...] = r_late[...] + w[...]

    (r1,) = staged(own_fields, stride, [r_late, hopped, w], [square], 0.1)

    def second_q(k, r1, qa, q1, t1, u1, q2, hu_out):
        @pl.when((k == 2) | (k == 3))
        def _():
            hu = summed(product(r1[...], qa[...]), u1[...])
            hu_out[...] = hu
            q2[...] = q1[...] + product(t1[...], product(qa[...], hu))

    (q2, hu2) = staged(second_q, stride, [r1, qa, q1, t1, u1], [square] * 2, 6)

    def second_fields(k, qa, ua, fa, sa, hu2, r1, t1, u2, f2, s2):
        @pl.when((k == 2) | (k == 3))
        def _():
            g = summed(product(qa[...], r1[...]), fa[...])
            f2[...] = product(t1[...], g)
            s2[...] = sa[...] + product(ua[...], product(r1[...], g))
            u2[...] = product(ua[...], hu2[...])

    (u2, f2, s2) = staged(second_fields, stride, [qa, ua, fa, sa, hu2, r1, t1], [square, field, field], 4
    )

    def third_fields(k, r_late, r_next, w_came, q1, t1, u1, r1, qa, ua, fa, sa, w4, s4):
        @pl.when((k == 2) | (k == 3))
        def _():
            came = jnp.where(k == 2, r_late[...], r_next[...]) + w_came[...]
            gt = summed(product(q1[...], came), t1[...])
            rc = r1[...] + product(u1[...], product(came, gt))
            g = summed(product(qa[...], rc), fa[...])
            w4[...] = product(gt, g)
            s4[...] = sa[...] + product(ua[...], product(rc, g))

    (w4, s4) = staged(third_fields, stride,
        [r_late, r_next, w_came, q1, t1, u1, r1, qa, ua, fa, sa],
        [field] * 2,
        9,
    )
    w4_came = moved(w4, [(2, 4), (3, 5)])
    s4_came = moved(s4, [(2, 4), (3, 5)])

    def second_through(k, t, gt_came, gt2_came, t2):
        @pl.when(k > 5)
        def _():
            t2[...] = product(product(t[...], gt_came[...]), gt2_came[...])

    (t2,) = staged(second_through, stride, [t, gt_came, gt2_came], [square], 2)

    def last_fields(k, r_late, r_next, total_came, q2, f2, g6, rg6):
        @pl.when((k == 2) | (k == 3))
        def _():
            rc = jnp.where(k == 2, r_late[...], r_next[...]) + total_came[...]
            g = summed(product(q2[...], rc), f2[...])
            g6[...] = g
            rg6[...] = product(rc, g)

    (g6, rg6) = staged(last_fields, stride, [r_late, r_next, total_came, q2, f2], [field] * 2, 3
    )
    g6_came = moved(g6, [(2, 6), (3, 7)])

    def last_reflected(k, s2, u2, rg6, s6):
        @pl.when((k == 2) | (k == 3))
        def _():
            s6[...] = s2[...] + product(u2[...], rg6[...])

    (s6,) = staged(last_reflected, stride, [s2, u2, rg6], [field], 1)
    s6_came = moved(s6, [(2, 6), (3, 7)])

    def through(k, f1, f2, t1, w4, t2, g6, out):
        @pl.when(k < 2)
        def _():
            out[...] = f1[...]

        @pl.when((k == 2) | (k == 3))
        def _():
            out[...] = f2[...]

        @pl.when((k == 4) | (k == 5))
        def _():
            out[...] = product(t1[...], w4[...])

        @pl.when(k > 5)
        def _():
            out[...] = product(t2[...], g6[...])

    (through_field,) = staged(through, stride, [f1, f2, t1, w4_came, t2, g6_came], [field], 1
    )
    entering = lax.ppermute(through_field, "sec", [(i, i + 1) for i in range(length - 1)])
    reflected = jnp.where(
        k < 2, s1, jnp.where(k < 4, s2, jnp.where(k < 6, s4_came, s6_came))
    )

    def depths(place, maps, entering, incident, out):
        value = right(jnp.where(place == 0, incident[...], entering[...]))
        for j in range(depth_maps.shape[1]):
            out[j] = jnp.dot(left(maps[j]), value, preferred_element_type=F32)

    (depth_fields,) = staged(depths, 1, [depth_maps[0], entering, incident], [depth_maps.shape[1:3] + field[1:]], 1)
    return (through_field[None], reflected[None], depth_fields[None])


def solution(mesh):
    in_specs = (
        P("sec", None, None),
        P("sec", None, None),
        P("sec", None, None),
        P("sec", None, None),
        P("sec", None, None, None),
        P(),
    )
    out_specs = (P("sec", None, None), P("sec", None, None), P("sec", None, None, None))

    return jax.shard_map(per_device, mesh=mesh, in_specs=in_specs, out_specs=out_specs, check_vma=False)
```

```python
import jax
import jax.numpy as jnp
from jax import lax
from jax.experimental import pallas as pl
from jax.experimental.pallas import tpu as pltpu
from jax.sharding import PartitionSpec as P

SEGMENTS = 3
NODES = 2**SEGMENTS
F32 = jnp.float32


def split(value):
    high = value.astype(jnp.bfloat16)
    return high, (value - high.astype(F32)).astype(jnp.bfloat16)


def left(value):
    high, low = split(value)
    return jnp.concatenate([high, high, low], axis=1)


def right(value):
    high, low = split(value)
    return jnp.concatenate([high, low, high], axis=0)


def product(former, latter):
    return jnp.dot(left(former), right(latter), preferred_element_type=F32)


def summed(bounce, value):
    factor = left(bounce)
    total = value
    for _ in range(3):
        total = value + jnp.dot(factor, right(total), preferred_element_type=F32)
    return total


def staged(body, stride, inputs, outputs, products):
    def kernel(*refs):
        body(lax.axis_index("sec") // stride, *refs)

    vmem = pl.BlockSpec(memory_space=pltpu.VMEM)
    side = inputs[0].shape[0]
    moved_bytes = 4 * side * side * (len(inputs) + len(outputs))
    return pl.pallas_call(
        kernel,
        out_shape=[jax.ShapeDtypeStruct(shape, F32) for shape in outputs],
        in_specs=[vmem] * len(inputs),
        out_specs=[vmem] * len(outputs),
        compiler_params=pltpu.CompilerParams(vmem_limit_bytes=24 * 2**20),
        cost_estimate=pl.CostEstimate(
            flops=int(products * 6 * side**3), bytes_accessed=moved_bytes, transcendentals=0
        ),
    )(*inputs)


def per_device(front_reflect, front_through, back_reflect, back_through, depth_maps, incident):
    length = lax.axis_size("sec")
    stride = length // NODES
    position = lax.axis_index("sec")
    k = position // stride
    square, field = front_reflect.shape[1:], incident.shape

    def moved(value, routes):
        pairs = [(a * stride + i, b * stride + i) for a, b in routes for i in range(stride)]
        return lax.ppermute(value, "sec", pairs)

    r, t, q, u = front_reflect[0], front_through[0], back_reflect[0], back_through[0]
    onward = [(0, 1), (1, 2), (2, 3), (3, 4), (4, 5)]
    low = [(0, 2), (1, 3)]
    back = [(4, 2), (5, 3)]

    q0 = moved(q, onward)
    swapped = moved(r, [(7, 6), (6, 7), (1, 0), (0, 1)])
    t0 = moved(t, onward)
    u0 = moved(u, onward)

    def load(k, *refs):
        for i in range(4):
            refs[4 + i][...] = refs[i][...]

    r_in, (r, t, q, u) = r, staged(load, stride, [r, t, q, u], [square] * 4, 0.1)

    def pair_reflect(at):
        def body(k, came, r, t, q, u, *rest):
            out, gt_out = rest[-2:]

            @pl.when(k == at)
            def _():
                gt = summed(product(q[...], came[...]), t[...])
                gt_out[...] = gt
                out[...] = r[...] + product(u[...], product(came[...], gt))

            @pl.when(k != at)
            def _():
                out[...] = came[...]
                if len(rest) == 3:
                    gt_out[...] = rest[0][...]

        return body

    (relay, gt) = staged(pair_reflect(6), stride, [swapped, r, t, q, u], [square] * 2, 6)
    hopped = moved(relay, [(6, 7), (7, 5), (0, 2)])

    def forward_q(k, q0, r, t, q, u, q1, hu_out):
        @pl.when(k == 0)
        def _():
            q1[...] = q[...]

        @pl.when((k > 0) & (k < 6))
        def _():
            hu = summed(product(r[...], q0[...]), u[...])
            hu_out[...] = hu
            q1[...] = q[...] + product(t[...], product(q0[...], hu))

    (q1, hu) = staged(forward_q, stride, [q0, r, t, q, u], [square] * 2, 6)
    qa = moved(q1, low)


    def forward_t(k, q0, t0, r, t, t1, rgt):
        @pl.when(k == 0)
        def _():
            t1[...] = t[...]

        @pl.when((k > 0) & (k < 6))
        def _():
            gt = summed(product(q0[...], r[...]), t0[...])
            rgt[...] = product(r[...], gt)
            t1[...] = product(t[...], gt)

    (t1, rgt) = staged(forward_t, stride, [q0, t0, r, t], [square] * 2, 6)

    (relay, gt) = staged(pair_reflect(5), stride, [hopped, r, t, q, u, gt], [square] * 2, 6)
    bounced = moved(relay, [(5, 4), (7, 5)])
    gt_came = moved(gt, [(5, 6), (6, 7)])
    r_late = moved(r_in, [(2, 3), (3, 2)])
    r_next = moved(r_in, [(4, 3)])

    def forward_u(k, u0, u, hu, rgt, u1, w):
        @pl.when(k == 0)
        def _():
            u1[...] = u[...]

        @pl.when((k > 0) & (k < 6))
        def _():
            factor = left(u0[...])
            w[...] = jnp.dot(factor, right(rgt[...]), preferred_element_type=F32)
            u1[...] = jnp.dot(factor, right(hu[...]), preferred_element_type=F32)

    (u1, w) = staged(forward_u, stride, [u0, u, hu, rgt], [square] * 2, 2)
    w_came = moved(w, back)
    ua = moved(u1, low)

    def low_fields(k, swapped, r, w, t1, incident, f1, s1):
        @pl.when(k < 2)
        def _():
            whole = jnp.where(k == 0, r[...], swapped[...] + w[...])
            value = right(incident[...])
            f1[...] = jnp.dot(left(t1[...]), value, preferred_element_type=F32)
            s1[...] = jnp.dot(left(whole), value, preferred_element_type=F32)

    (f1, s1) = staged(low_fields, stride, [swapped, r, w, t1, incident], [field, field], 1
    )
    fa = moved(f1, low)
    sa = moved(s1, low)

    def open_gate(k, w, out):
        out[...] = w[:8, :128]

    (gate,) = staged(open_gate, stride, [w], [(8, 128)], 0.1)

    def second_reflect(k, bounced, q1, t1, u1, w, gate, total, gt_out):
        @pl.when((k == 4) | (k == 5))
        def _():
            gt = summed(product(q1[...], bounced[...]), t1[...])
            gt_out[...] = gt
            total[...] = w[...] + product(u1[...], product(bounced[...], gt))

    (total, gt2) = staged(second_reflect, stride, [bounced, q1, t1, u1, w, gate], [square] * 2, 6
    )
    total_came = moved(total, back)
    gt2_came = moved(gt2, [(4, 6), (5, 7)])

    def own_fields(k, r_late, hopped, w, r1):
        @pl.when(k == 2)
        def _():
            r1[...] = hopped[...] + w[...]

        @pl.when(k == 3)
        def _():
            r1[...] = r_late[...] + w[...]

    (r1,) = staged(own_fields, stride, [r_late, hopped, w], [square], 0.1)

    def second_q(k, r1, qa, q1, t1, u1, q2, hu_out):
        @pl.when((k == 2) | (k == 3))
        def _():
            hu = summed(product(r1[...], qa[...]), u1[...])
            hu_out[...] = hu
            q2[...] = q1[...] + product(t1[...], product(qa[...], hu))

    (q2, hu2) = staged(second_q, stride, [r1, qa, q1, t1, u1], [square] * 2, 6)

    def second_fields(k, qa, fa, r1, t1, f2, rg2):
        @pl.when((k == 2) | (k == 3))
        def _():
            g = summed(product(qa[...], r1[...]), fa[...])
            f2[...] = product(t1[...], g)
            rg2[...] = product(r1[...], g)

    (f2, rg2) = staged(second_fields, stride, [qa, fa, r1, t1], [field, field], 2)

    def third_fields(k, r_late, r_next, w_came, q1, t1, u1, r1, qa, fa, w4, rg4):
        @pl.when((k == 2) | (k == 3))
        def _():
            came = jnp.where(k == 2, r_late[...], r_next[...]) + w_came[...]
            gt = summed(product(q1[...], came), t1[...])
            rc = r1[...] + product(u1[...], product(came, gt))
            g = summed(product(qa[...], rc), fa[...])
            w4[...] = product(gt, g)
            rg4[...] = product(rc, g)

    (w4, rg4) = staged(
        third_fields, stride, [r_late, r_next, w_came, q1, t1, u1, r1, qa, fa], [field] * 2, 9
    )
    w4_came = moved(w4, [(2, 4), (3, 5)])

    def second_through(k, t, gt_came, gt2_came, t2):
        @pl.when(k > 5)
        def _():
            t2[...] = product(product(t[...], gt_came[...]), gt2_came[...])

    (t2,) = staged(second_through, stride, [t, gt_came, gt2_came], [square], 2)

    def last_fields(k, r_late, r_next, total_came, q2, f2, g6, rg6):
        @pl.when((k == 2) | (k == 3))
        def _():
            rc = jnp.where(k == 2, r_late[...], r_next[...]) + total_came[...]
            g = summed(product(q2[...], rc), f2[...])
            g6[...] = g
            rg6[...] = product(rc, g)

    (g6, rg6) = staged(last_fields, stride, [r_late, r_next, total_came, q2, f2], [field] * 2, 3
    )
    g6_came = moved(g6, [(2, 6), (3, 7)])

    def all_reflected(k, sa, ua, rg2, rg4, rg6, hu2, s2, s4, s6):
        @pl.when((k == 2) | (k == 3))
        def _():
            sums = rg2[...] + product(hu2[...], rg6[...])
            value = product(ua[...], jnp.concatenate([rg2[...], rg4[...], sums], axis=1))
            width = sa.shape[1]
            for i, out in enumerate((s2, s4, s6)):
                out[...] = sa[...] + value[:, i * width : (i + 1) * width]

    (s2, s4, s6) = staged(all_reflected, stride, [sa, ua, rg2, rg4, rg6, hu2], [field] * 3, 2)
    s6_came = moved(s6, [(2, 6), (3, 7)])
    s4_came = moved(s4, [(2, 4), (3, 5)])

    def through(k, f1, f2, t1, w4, t2, g6, out):
        @pl.when(k < 2)
        def _():
            out[...] = f1[...]

        @pl.when((k == 2) | (k == 3))
        def _():
            out[...] = f2[...]

        @pl.when((k == 4) | (k == 5))
        def _():
            out[...] = product(t1[...], w4[...])

        @pl.when(k > 5)
        def _():
            out[...] = product(t2[...], g6[...])

    (through_field,) = staged(through, stride, [f1, f2, t1, w4_came, t2, g6_came], [field], 1
    )
    entering = lax.ppermute(through_field, "sec", [(i, i + 1) for i in range(length - 1)])
    reflected = jnp.where(
        k < 2, s1, jnp.where(k < 4, s2, jnp.where(k < 6, s4_came, s6_came))
    )

    def depths(place, maps, entering, incident, out):
        value = right(jnp.where(place == 0, incident[...], entering[...]))
        for j in range(depth_maps.shape[1]):
            out[j] = jnp.dot(left(maps[j]), value, preferred_element_type=F32)

    (depth_fields,) = staged(depths,
        1,
        [depth_maps[0], entering, incident],
        [depth_maps.shape[1:3] + field[1:]],
        1,
    )
    return (through_field[None], reflected[None], depth_fields[None])


def solution(mesh):
    in_specs = (
        P("sec", None, None),
        P("sec", None, None),
        P("sec", None, None),
        P("sec", None, None),
        P("sec", None, None, None),
        P(),
    )
    out_specs = (P("sec", None, None), P("sec", None, None), P("sec", None, None, None))

    return jax.shard_map(
        per_device, mesh=mesh, in_specs=in_specs, out_specs=out_specs, check_vma=False
    )
```

```python
import jax
import jax.numpy as jnp
from jax import lax
from jax.experimental import pallas as pl
from jax.experimental.pallas import tpu as pltpu
from jax.sharding import PartitionSpec as P

SEGMENTS = 3
NODES = 2**SEGMENTS
F32 = jnp.float32


def split(value):
    high = value.astype(jnp.bfloat16)
    return high, (value - high.astype(F32)).astype(jnp.bfloat16)


def left(value):
    high, low = split(value)
    return jnp.concatenate([high, high, low], axis=1)


def right(value):
    high, low = split(value)
    return jnp.concatenate([high, low, high], axis=0)


def product(former, latter):
    return jnp.dot(left(former), right(latter), preferred_element_type=F32)


def summed(bounce, value, rolled=False):
    factor = left(bounce)

    def step(_, total):
        return value + jnp.dot(factor, right(total), preferred_element_type=F32)

    return lax.fori_loop(0, 3, step, value, unroll=not rolled)


def staged(body, stride, inputs, outputs, products):
    def kernel(*refs):
        body(lax.axis_index("sec") // stride, *refs)

    vmem = pl.BlockSpec(memory_space=pltpu.VMEM)
    side = inputs[0].shape[0]
    moved_bytes = 4 * side * side * (len(inputs) + len(outputs))
    return pl.pallas_call(
        kernel,
        out_shape=[jax.ShapeDtypeStruct(shape, F32) for shape in outputs],
        in_specs=[vmem] * len(inputs),
        out_specs=[vmem] * len(outputs),
        compiler_params=pltpu.CompilerParams(vmem_limit_bytes=24 * 2**20),
        cost_estimate=pl.CostEstimate(
            flops=int(products * 6 * side**3), bytes_accessed=moved_bytes, transcendentals=0
        ),
    )(*inputs)


def per_device(front_reflect, front_through, back_reflect, back_through, depth_maps, incident):
    length = lax.axis_size("sec")
    stride = length // NODES
    position = lax.axis_index("sec")
    k = position // stride
    square, field = front_reflect.shape[1:], incident.shape

    def moved(value, routes):
        pairs = [(a * stride + i, b * stride + i) for a, b in routes for i in range(stride)]
        return lax.ppermute(value, "sec", pairs)

    r, t, q, u = front_reflect[0], front_through[0], back_reflect[0], back_through[0]
    width = field[1]
    fields = (field[0], 2 * width)
    low = [(0, 2), (1, 3)]
    back = [(4, 2), (5, 3)]
    middle = [(2, 3), (3, 4), (4, 5)]

    swapped = moved(r, [(7, 6), (6, 7), (1, 0)])
    r2_down = moved(r, [(2, 0)])
    q0 = moved(q, [(0, 1), (1, 2)] + middle)
    t0 = moved(t, [(1, 2)] + middle)
    u1_over = moved(u, [(1, 0)])
    u0 = moved(u, [(0, 1)] + middle)
    r_late = moved(r, [(3, 2)])
    r_next = moved(r, [(4, 3)])

    def load(k, r, t, q, u, incident, *out):
        for i, ref in enumerate((r, t, q, u)):
            out[i][...] = ref[...]

        @pl.when(k == 0)
        def _():
            value = right(incident[...])
            out[4][:, :width] = jnp.dot(left(t[...]), value, preferred_element_type=F32)
            out[4][:, width:] = jnp.dot(left(r[...]), value, preferred_element_type=F32)

    r, t, q, u, first = staged(load, stride, [r, t, q, u, incident], [square] * 4 + [fields], 1)
    first_came = moved(first, [(0, 1)])

    def pair_reflect(at):
        def body(k, came, r, t, q, u, *rest):
            out, gt_out = rest[-2:]

            @pl.when(k == at)
            def _():
                gt = summed(product(q[...], came[...]), t[...], True)
                gt_out[...] = gt
                out[...] = r[...] + product(u[...], product(came[...], gt))

            @pl.when(k != at)
            def _():
                out[...] = came[...]
                if len(rest) == 3:
                    gt_out[...] = rest[0][...]

        return body

    (relay, gt) = staged(pair_reflect(6), stride, [swapped, r, t, q, u], [square] * 2, 6)
    hopped = moved(relay, [(6, 7), (7, 5), (0, 2)])
    r2_over = moved(r2_down, [(0, 1)])
    u1_up = moved(u1_over, [(0, 2)])
    r2_up = moved(r2_over, [(1, 3)])

    def forward_q(k, q0, r, t, q, u, q1, hu_out):
        @pl.when(k == 0)
        def _():
            q1[...] = q[...]

        @pl.when((k > 0) & (k < 6))
        def _():
            hu = summed(product(r[...], q0[...]), u[...], True)
            hu_out[...] = hu
            q1[...] = q[...] + product(t[...], product(q0[...], hu))

    (q1, hu) = staged(forward_q, stride, [q0, r, t, q, u], [square] * 2, 6)
    qa = moved(q1, low)


    def forward_t(k, q0, t0, r, t, t1, rgt):
        @pl.when((k > 1) & (k < 6))
        def _():
            gt = summed(product(q0[...], r[...]), t0[...], True)
            rgt[...] = product(r[...], gt)
            t1[...] = product(t[...], gt)

    (t1, rgt) = staged(forward_t, stride, [q0, t0, r, t], [square] * 2, 6)

    (relay, gt) = staged(pair_reflect(5), stride, [hopped, r, t, q, u, gt], [square] * 2, 6)
    bounced = moved(relay, [(5, 4), (7, 5)])
    gt_came = moved(gt, [(5, 6), (6, 7)])

    def forward_u(k, u0, u1_up, u, hu, rgt, u1, w):
        @pl.when(k == 0)
        def _():
            u1[...] = u[...]

        @pl.when((k > 0) & (k < 6))
        def _():
            factor = left(jnp.where(k == 2, u1_up[...], u0[...]))
            u1[...] = jnp.dot(factor, right(hu[...]), preferred_element_type=F32)

            @pl.when(k > 1)
            def _():
                w[...] = jnp.dot(factor, right(rgt[...]), preferred_element_type=F32)

    (u1, w) = staged(forward_u, stride, [u0, u1_up, u, hu, rgt], [square] * 2, 2)
    w_came = moved(w, back)
    ua = moved(u1, low)

    def low_fields(k, first, came, q0, r, t, u0, out):
        @pl.when(k == 0)
        def _():
            out[...] = first[...]

        @pl.when(k == 1)
        def _():
            g = summed(product(q0[...], r[...]), came[:, :width], True)
            out[:, :width] = product(t[...], g)
            out[:, width:] = came[:, width:] + product(u0[...], product(r[...], g))

    (first,) = staged(low_fields, stride, [first, first_came, q0, r, t, u0], [fields], 2)
    fa = moved(first, low)

    def open_gate(k, w, out):
        out[...] = w[:8, :128]

    (gate,) = staged(open_gate, stride, [w], [(8, 128)], 0.1)

    def second_reflect(k, bounced, q1, t1, u1, w, gate, total, gt_out):
        @pl.when((k == 4) | (k == 5))
        def _():
            gt = summed(product(q1[...], bounced[...]), t1[...])
            gt_out[...] = gt
            total[...] = w[...] + product(u1[...], product(bounced[...], gt))

    (total, gt2) = staged(second_reflect, stride, [bounced, q1, t1, u1, w, gate], [square] * 2, 6
    )
    total_came = moved(total, back)
    gt2_came = moved(gt2, [(4, 6), (5, 7)])

    def own_fields(k, r2_up, hopped, w, r1):
        @pl.when(k == 2)
        def _():
            r1[...] = hopped[...] + w[...]

        @pl.when(k == 3)
        def _():
            r1[...] = r2_up[...] + w[...]

    (r1,) = staged(own_fields, stride, [r2_up, hopped, w], [square], 0.1)

    def second_q(k, r1, qa, q1, t1, u1, q2, hu_out):
        @pl.when((k == 2) | (k == 3))
        def _():
            hu = summed(product(r1[...], qa[...]), u1[...], True)
            hu_out[...] = hu
            q2[...] = q1[...] + product(t1[...], product(qa[...], hu))

    (q2, hu2) = staged(second_q, stride, [r1, qa, q1, t1, u1], [square] * 2, 6)

    def second_fields(k, qa, fa, r1, t1, f2, rg2):
        @pl.when((k == 2) | (k == 3))
        def _():
            g = summed(product(qa[...], r1[...]), fa[:, :width])
            f2[...] = product(t1[...], g)
            rg2[...] = product(r1[...], g)

    (f2, rg2) = staged(second_fields, stride, [qa, fa, r1, t1], [field, field], 2)

    def third_fields(k, r_late, r_next, w_came, q1, t1, u1, r1, qa, fa, w4, rg4):
        @pl.when((k == 2) | (k == 3))
        def _():
            came = jnp.where(k == 2, r_late[...], r_next[...]) + w_came[...]
            gt = summed(product(q1[...], came), t1[...])
            rc = r1[...] + product(u1[...], product(came, gt))
            g = summed(product(qa[...], rc), fa[:, :width])
            w4[...] = product(gt, g)
            rg4[...] = product(rc, g)

    (w4, rg4) = staged(
        third_fields, stride, [r_late, r_next, w_came, q1, t1, u1, r1, qa, fa], [field] * 2, 9
    )
    w4_came = moved(w4, [(2, 4), (3, 5)])

    def second_through(k, t, gt_came, gt2_came, t2):
        @pl.when(k > 5)
        def _():
            t2[...] = product(product(t[...], gt_came[...]), gt2_came[...])

    (t2,) = staged(second_through, stride, [t, gt_came, gt2_came], [square], 2)

    def last_fields(k, r_late, r_next, total_came, q2, f2, g6, rg6):
        @pl.when((k == 2) | (k == 3))
        def _():
            rc = jnp.where(k == 2, r_late[...], r_next[...]) + total_came[...]
            g = summed(product(q2[...], rc), f2[...])
            g6[...] = g
            rg6[...] = product(rc, g)

    (g6, rg6) = staged(last_fields, stride, [r_late, r_next, total_came, q2, f2], [field] * 2, 3
    )
    g6_came = moved(g6, [(2, 6), (3, 7)])

    def all_reflected(k, fa, ua, rg2, rg4, rg6, hu2, s2, s4, s6):
        @pl.when((k == 2) | (k == 3))
        def _():
            sums = rg2[...] + product(hu2[...], rg6[...])
            value = product(ua[...], jnp.concatenate([rg2[...], rg4[...], sums], axis=1))
            for i, out in enumerate((s2, s4, s6)):
                out[...] = fa[:, width:] + value[:, i * width : (i + 1) * width]

    (s2, s4, s6) = staged(all_reflected, stride, [fa, ua, rg2, rg4, rg6, hu2], [field] * 3, 2)
    s6_came = moved(s6, [(2, 6), (3, 7)])
    s4_came = moved(s4, [(2, 4), (3, 5)])

    def through(k, first, f2, t1, w4, t2, g6, out):
        @pl.when(k < 2)
        def _():
            out[...] = first[:, :width]

        @pl.when((k == 2) | (k == 3))
        def _():
            out[...] = f2[...]

        @pl.when((k == 4) | (k == 5))
        def _():
            out[...] = product(t1[...], w4[...])

        @pl.when(k > 5)
        def _():
            out[...] = product(t2[...], g6[...])

    (through_field,) = staged(through, stride, [first, f2, t1, w4_came, t2, g6_came], [field], 1
    )
    entering = lax.ppermute(through_field, "sec", [(i, i + 1) for i in range(length - 1)])
    reflected = jnp.where(
        k < 2, first[:, width:], jnp.where(k < 4, s2, jnp.where(k < 6, s4_came, s6_came))
    )

    def depths(place, maps, entering, incident, out):
        value = right(jnp.where(place == 0, incident[...], entering[...]))
        for j in range(depth_maps.shape[1]):
            out[j] = jnp.dot(left(maps[j]), value, preferred_element_type=F32)

    (depth_fields,) = staged(depths,
        1,
        [depth_maps[0], entering, incident],
        [depth_maps.shape[1:3] + field[1:]],
        1,
    )
    return (through_field[None], reflected[None], depth_fields[None])


def solution(mesh):
    in_specs = (
        P("sec", None, None),
        P("sec", None, None),
        P("sec", None, None),
        P("sec", None, None),
        P("sec", None, None, None),
        P(),
    )
    out_specs = (P("sec", None, None), P("sec", None, None), P("sec", None, None, None))

    return jax.shard_map(
        per_device, mesh=mesh, in_specs=in_specs, out_specs=out_specs, check_vma=False
    )
```

```python
import jax
import jax.numpy as jnp
from jax import lax
from jax.experimental import pallas as pl
from jax.experimental.pallas import tpu as pltpu
from jax.sharding import PartitionSpec as P

SEGMENTS = 3
NODES = 2**SEGMENTS
F32 = jnp.float32


def split(value):
    high = value.astype(jnp.bfloat16)
    return high, (value - high.astype(F32)).astype(jnp.bfloat16)


def left(value):
    high, low = split(value)
    return jnp.concatenate([high, high, low], axis=1)


def right(value):
    high, low = split(value)
    return jnp.concatenate([high, low, high], axis=0)


def product(former, latter):
    return jnp.dot(left(former), right(latter), preferred_element_type=F32)


def summed(bounce, value, rolled=False):
    factor = left(bounce)

    def step(_, total):
        return value + jnp.dot(factor, right(total), preferred_element_type=F32)

    return lax.fori_loop(0, 3, step, value, unroll=not rolled)


def staged(body, stride, inputs, outputs, products):
    def kernel(*refs):
        body(lax.axis_index("sec") // stride, *refs)

    vmem = pl.BlockSpec(memory_space=pltpu.VMEM)
    side = inputs[0].shape[0]
    moved_bytes = 4 * side * side * (len(inputs) + len(outputs))
    return pl.pallas_call(
        kernel,
        out_shape=[jax.ShapeDtypeStruct(shape, F32) for shape in outputs],
        in_specs=[vmem] * len(inputs),
        out_specs=[vmem] * len(outputs),
        compiler_params=pltpu.CompilerParams(vmem_limit_bytes=24 * 2**20),
        cost_estimate=pl.CostEstimate(
            flops=int(products * 6 * side**3), bytes_accessed=moved_bytes, transcendentals=0
        ),
    )(*inputs)


def per_device(front_reflect, front_through, back_reflect, back_through, depth_maps, incident):
    length = lax.axis_size("sec")
    stride = length // NODES
    position = lax.axis_index("sec")
    k = position // stride
    square, field = front_reflect.shape[1:], incident.shape

    def moved(value, routes):
        pairs = [(a * stride + i, b * stride + i) for a, b in routes for i in range(stride)]
        return lax.ppermute(value, "sec", pairs)

    r, t, q, u = front_reflect[0], front_through[0], back_reflect[0], back_through[0]
    width = field[1]
    fields = (field[0], 2 * width)
    low = [(0, 2), (1, 3)]
    back = [(4, 2), (5, 3)]
    middle = [(2, 3), (3, 4), (4, 5)]

    swapped = moved(r, [(7, 6), (6, 7), (1, 0)])
    r2_down = moved(r, [(2, 0)])
    q0 = moved(q, [(0, 1), (1, 2)] + middle)
    t0 = moved(t, [(1, 2)] + middle)
    u1_over = moved(u, [(1, 0)])
    u0 = moved(u, [(3, 4), (4, 5)])
    u0_low = moved(u, [(0, 1), (2, 3)])
    r_late = moved(r, [(3, 2)])
    r_next = moved(r, [(4, 3)])

    def load(k, r, t, q, u, incident, *out):
        for i, ref in enumerate((r, t, q, u)):
            out[i][...] = ref[...]

        @pl.when(k == 0)
        def _():
            value = right(incident[...])
            out[4][:, :width] = jnp.dot(left(t[...]), value, preferred_element_type=F32)
            out[4][:, width:] = jnp.dot(left(r[...]), value, preferred_element_type=F32)

    r, t, q, u, first = staged(load, stride, [r, t, q, u, incident], [square] * 4 + [fields], 1)
    first_came = moved(first, [(0, 1)])

    def pair_reflect(at):
        def body(k, came, r, t, q, u, *rest):
            out, gt_out = rest[-2:]

            @pl.when(k == at)
            def _():
                gt = summed(product(q[...], came[...]), t[...], True)
                gt_out[...] = gt
                out[...] = r[...] + product(u[...], product(came[...], gt))

            @pl.when(k != at)
            def _():
                out[...] = came[...]
                if len(rest) == 3:
                    gt_out[...] = rest[0][...]

        return body

    (relay, gt) = staged(pair_reflect(6), stride, [swapped, r, t, q, u], [square] * 2, 6)
    hopped = moved(relay, [(6, 7), (7, 5), (0, 2)])
    r2_over = moved(r2_down, [(0, 1)])
    u1_up = moved(u1_over, [(0, 2)])
    r2_up = moved(r2_over, [(1, 3)])

    def forward_q(k, q0, r, t, q, u, q1, hu_out):
        @pl.when(k == 0)
        def _():
            q1[...] = q[...]

        @pl.when((k > 0) & (k < 6))
        def _():
            hu = summed(product(r[...], q0[...]), u[...], True)
            hu_out[...] = hu
            q1[...] = q[...] + product(t[...], product(q0[...], hu))

    (q1, hu) = staged(forward_q, stride, [q0, r, t, q, u], [square] * 2, 6)
    qa = moved(q1, low)


    def forward_t(k, q0, t0, r, t, t1, rgt):
        @pl.when((k > 1) & (k < 6))
        def _():
            gt = summed(product(q0[...], r[...]), t0[...], True)
            rgt[...] = product(r[...], gt)
            t1[...] = product(t[...], gt)

    (t1, rgt) = staged(forward_t, stride, [q0, t0, r, t], [square] * 2, 6)

    (relay, gt) = staged(pair_reflect(5), stride, [hopped, r, t, q, u, gt], [square] * 2, 6)
    bounced = moved(relay, [(5, 4), (7, 5)])
    gt_came = moved(gt, [(5, 6), (6, 7)])

    def forward_u(k, u0, hu, rgt, u1, w):
        @pl.when((k == 4) | (k == 5))
        def _():
            factor = left(u0[...])
            w[...] = jnp.dot(factor, right(rgt[...]), preferred_element_type=F32)
            u1[...] = jnp.dot(factor, right(hu[...]), preferred_element_type=F32)

    (u1, w) = staged(forward_u, stride, [u0, hu, rgt], [square] * 2, 2)
    w_came = moved(w, back)

    def low_fields(k, first, came, q0, r, t, f1, rg):
        @pl.when(k == 0)
        def _():
            f1[...] = first[:, :width]

        @pl.when(k == 1)
        def _():
            g = summed(product(q0[...], r[...]), came[:, :width], True)
            f1[...] = product(t[...], g)
            rg[...] = product(r[...], g)

    (f1, rg) = staged(low_fields, stride, [first, first_came, q0, r, t], [field] * 2, 2)
    fa = moved(f1, low)

    def second_reflect(k, bounced, q1, t1, u1, w, total, gt_out):
        @pl.when((k == 4) | (k == 5))
        def _():
            gt = summed(product(q1[...], bounced[...]), t1[...])
            gt_out[...] = gt
            total[...] = w[...] + product(u1[...], product(bounced[...], gt))

    (total, gt2) = staged(second_reflect, stride, [bounced, q1, t1, u1, w], [square] * 2, 6
    )
    total_came = moved(total, back)
    gt2_came = moved(gt2, [(4, 6), (5, 7)])

    def low_u(k, u0, u1_up, u, hu, rgt, rg, first, came, both, w):
        side = u.shape[1]

        @pl.when(k == 0)
        def _():
            both[:, :side] = u[...]
            both[:, side:] = first[:, width:]

        @pl.when((k > 0) & (k < 4))
        def _():
            factor = left(jnp.where(k == 2, u1_up[...], u0[...]))
            both[:, :side] = jnp.dot(factor, right(hu[...]), preferred_element_type=F32)

            @pl.when(k == 1)
            def _():
                both[:, side:] = came[:, width:] + jnp.dot(
                    factor, right(rg[...]), preferred_element_type=F32
                )

            @pl.when(k > 1)
            def _():
                w[...] = jnp.dot(factor, right(rgt[...]), preferred_element_type=F32)

    (both, w_low) = staged(
        low_u,
        stride,
        [u0_low, u1_up, u, hu, rgt, rg, first, first_came],
        [(square[0], square[1] + width), square],
        2,
    )
    ua = moved(both, low)

    def own_fields(k, r2_up, hopped, w, r1):
        @pl.when(k == 2)
        def _():
            r1[...] = hopped[...] + w[...]

        @pl.when(k == 3)
        def _():
            r1[...] = r2_up[...] + w[...]

    (r1,) = staged(own_fields, stride, [r2_up, hopped, w_low], [square], 0.1)

    def second_q(k, r1, qa, q1, t1, both, q2, hu_out):
        @pl.when((k == 2) | (k == 3))
        def _():
            hu = summed(product(r1[...], qa[...]), both[:, : q1.shape[1]], True)
            hu_out[...] = hu
            q2[...] = q1[...] + product(t1[...], product(qa[...], hu))

    (q2, hu2) = staged(second_q, stride, [r1, qa, q1, t1, both], [square] * 2, 6)

    def second_fields(k, qa, fa, r1, t1, f2, rg2):
        @pl.when((k == 2) | (k == 3))
        def _():
            g = summed(product(qa[...], r1[...]), fa[...])
            f2[...] = product(t1[...], g)
            rg2[...] = product(r1[...], g)

    (f2, rg2) = staged(second_fields, stride, [qa, fa, r1, t1], [field, field], 2)

    def third_fields(k, r_late, r_next, w_came, q1, t1, both, r1, qa, fa, w4, rg4):
        @pl.when((k == 2) | (k == 3))
        def _():
            came = jnp.where(k == 2, r_late[...], r_next[...]) + w_came[...]
            gt = summed(product(q1[...], came), t1[...], True)
            rc = r1[...] + product(both[:, : q1.shape[1]], product(came, gt))
            g = summed(product(qa[...], rc), fa[...])
            w4[...] = product(gt, g)
            rg4[...] = product(rc, g)

    (w4, rg4) = staged(
        third_fields, stride, [r_late, r_next, w_came, q1, t1, both, r1, qa, fa], [field] * 2, 9
    )
    w4_came = moved(w4, [(2, 4), (3, 5)])

    def second_through(k, t, gt_came, gt2_came, t2):
        @pl.when(k > 5)
        def _():
            t2[...] = product(product(t[...], gt_came[...]), gt2_came[...])

    (t2,) = staged(second_through, stride, [t, gt_came, gt2_came], [square], 2)

    def last_fields(k, r_late, r_next, total_came, q2, f2, g6, rg6):
        @pl.when((k == 2) | (k == 3))
        def _():
            rc = jnp.where(k == 2, r_late[...], r_next[...]) + total_came[...]
            g = summed(product(q2[...], rc), f2[...])
            g6[...] = g
            rg6[...] = product(rc, g)

    (g6, rg6) = staged(last_fields, stride, [r_late, r_next, total_came, q2, f2], [field] * 2, 3
    )
    g6_came = moved(g6, [(2, 6), (3, 7)])

    def all_reflected(k, ua, rg2, rg4, rg6, hu2, s2, s4, s6):
        @pl.when((k == 2) | (k == 3))
        def _():
            sums = rg2[...] + product(hu2[...], rg6[...])
            value = product(ua[:, : hu2.shape[1]], jnp.concatenate([rg2[...], rg4[...], sums], axis=1))
            for i, out in enumerate((s2, s4, s6)):
                out[...] = ua[:, hu2.shape[1] :] + value[:, i * width : (i + 1) * width]

    (s2, s4, s6) = staged(all_reflected, stride, [ua, rg2, rg4, rg6, hu2], [field] * 3, 2)
    s6_came = moved(s6, [(2, 6), (3, 7)])
    s4_came = moved(s4, [(2, 4), (3, 5)])

    def through(k, f1, f2, t1, w4, t2, g6, out):
        @pl.when(k < 2)
        def _():
            out[...] = f1[...]

        @pl.when((k == 2) | (k == 3))
        def _():
            out[...] = f2[...]

        @pl.when((k == 4) | (k == 5))
        def _():
            out[...] = product(t1[...], w4[...])

        @pl.when(k > 5)
        def _():
            out[...] = product(t2[...], g6[...])

    (through_field,) = staged(through, stride, [f1, f2, t1, w4_came, t2, g6_came], [field], 1
    )
    entering = lax.ppermute(through_field, "sec", [(i, i + 1) for i in range(length - 1)])
    reflected = jnp.where(
        k < 2, both[:, square[1] :], jnp.where(k < 4, s2, jnp.where(k < 6, s4_came, s6_came))
    )

    def depths(place, maps, entering, incident, out):
        value = right(jnp.where(place == 0, incident[...], entering[...]))
        for j in range(depth_maps.shape[1]):
            out[j] = jnp.dot(left(maps[j]), value, preferred_element_type=F32)

    (depth_fields,) = staged(depths,
        1,
        [depth_maps[0], entering, incident],
        [depth_maps.shape[1:3] + field[1:]],
        1,
    )
    return (through_field[None], reflected[None], depth_fields[None])


def solution(mesh):
    in_specs = (
        P("sec", None, None),
        P("sec", None, None),
        P("sec", None, None),
        P("sec", None, None),
        P("sec", None, None, None),
        P(),
    )
    out_specs = (P("sec", None, None), P("sec", None, None), P("sec", None, None, None))

    return jax.shard_map(
        per_device, mesh=mesh, in_specs=in_specs, out_specs=out_specs, check_vma=False
    )
```

```python
import jax
import jax.numpy as jnp
from jax import lax
from jax.experimental import pallas as pl
from jax.experimental.pallas import tpu as pltpu
from jax.sharding import PartitionSpec as P

SEGMENTS = 3
NODES = 2**SEGMENTS
F32 = jnp.float32


def split(value):
    high = value.astype(jnp.bfloat16)
    return high, (value - high.astype(F32)).astype(jnp.bfloat16)


def left(value):
    high, low = split(value)
    return jnp.concatenate([high, high, low], axis=1)


def right(value):
    high, low = split(value)
    return jnp.concatenate([high, low, high], axis=0)


def product(former, latter):
    return jnp.dot(left(former), right(latter), preferred_element_type=F32)


def summed(bounce, value, rolled=False):
    factor = left(bounce)

    def step(_, total):
        return value + jnp.dot(factor, right(total), preferred_element_type=F32)

    return lax.fori_loop(0, 3, step, value, unroll=not rolled)


def staged(body, stride, inputs, outputs, products, dtype=F32):
    def kernel(*refs):
        body(lax.axis_index("sec") // stride, *refs)

    vmem = pl.BlockSpec(memory_space=pltpu.VMEM)
    side = inputs[0].shape[-1]
    moved_bytes = 4 * side * side * (len(inputs) + len(outputs))
    return pl.pallas_call(
        kernel,
        out_shape=[jax.ShapeDtypeStruct(shape, dtype) for shape in outputs],
        in_specs=[vmem] * len(inputs),
        out_specs=[vmem] * len(outputs),
        compiler_params=pltpu.CompilerParams(vmem_limit_bytes=24 * 2**20),
        cost_estimate=pl.CostEstimate(
            flops=int(products * 6 * side**3), bytes_accessed=moved_bytes, transcendentals=0
        ),
    )(*inputs)


def per_device(front_reflect, front_through, back_reflect, back_through, depth_maps, incident):
    length = lax.axis_size("sec")
    stride = length // NODES
    position = lax.axis_index("sec")
    k = position // stride
    square, field = front_reflect.shape[1:], incident.shape

    def moved(value, routes, start=0, step=1):
        pairs = [
            (a * stride + i, b * stride + i)
            for a, b in routes
            for i in range(start, stride, step)
        ]
        return lax.ppermute(value, "sec", pairs)

    r, t, q, u = front_reflect[0], front_through[0], back_reflect[0], back_through[0]
    width = field[1]
    fields = (field[0], 2 * width)
    low = [(0, 2), (1, 3)]
    back = [(4, 2), (5, 3)]
    middle = [(2, 3), (3, 4), (4, 5)]

    swapped = moved(r, [(7, 6), (6, 7), (1, 0)])
    r2_down = moved(r, [(2, 0)])
    q0 = moved(q, [(0, 1), (1, 2)] + middle)
    t0 = moved(t, [(1, 2)] + middle)
    u1_over = moved(u, [(1, 0)])
    u0 = moved(u, [(3, 4), (4, 5)])
    u0_low = moved(u, [(0, 1), (2, 3)])
    r_late = moved(r, [(3, 2)])
    r_next = moved(r, [(4, 3)])

    def load(k, r, t, q, u, incident, *out):
        for i, ref in enumerate((r, t, q, u)):
            out[i][...] = ref[...]

        @pl.when(k == 0)
        def _():
            value = right(incident[...])
            out[4][:, :width] = jnp.dot(left(t[...]), value, preferred_element_type=F32)
            out[4][:, width:] = jnp.dot(left(r[...]), value, preferred_element_type=F32)

    r, t, q, u, first = staged(load, stride, [r, t, q, u, incident], [square] * 4 + [fields], 1)
    first_came = moved(first, [(0, 1)])

    def pair_reflect(at):
        def body(k, came, r, t, q, u, *rest):
            out, gt_out = rest[-2:]

            @pl.when(k == at)
            def _():
                gt = summed(product(q[...], came[...]), t[...], True)
                gt_out[...] = gt
                out[...] = r[...] + product(u[...], product(came[...], gt))

            @pl.when(k != at)
            def _():
                out[...] = came[...]
                if len(rest) == 3:
                    gt_out[...] = rest[0][...]

        return body

    (relay, gt) = staged(pair_reflect(6), stride, [swapped, r, t, q, u], [square] * 2, 6)
    hopped = moved(relay, [(6, 7), (7, 5), (0, 2)])
    r2_over = moved(r2_down, [(0, 1)])
    u1_up = moved(u1_over, [(0, 2)])
    r2_up = moved(r2_over, [(1, 3)])

    def forward_q(k, q0, r, t, q, u, q1, hu_out):
        @pl.when(k == 0)
        def _():
            q1[...] = q[...]

        @pl.when((k > 0) & (k < 6))
        def _():
            hu = summed(product(r[...], q0[...]), u[...], True)
            hu_out[...] = hu
            q1[...] = q[...] + product(t[...], product(q0[...], hu))

    (q1, hu) = staged(forward_q, stride, [q0, r, t, q, u], [square] * 2, 6)
    qa = moved(q1, low)

    def split_maps(d, maps, out):
        @pl.loop(0, depth_maps.shape[1])
        def _(j):
            out[j] = left(maps[j])

    (maps,) = staged(
        split_maps,
        1,
        [depth_maps[0]],
        [depth_maps.shape[1:3] + (3 * square[1],)],
        0.1,
        jnp.bfloat16,
    )


    def forward_t(k, q0, t0, r, t, t1, rgt):
        @pl.when((k > 1) & (k < 6))
        def _():
            gt = summed(product(q0[...], r[...]), t0[...], True)
            rgt[...] = product(r[...], gt)
            t1[...] = product(t[...], gt)

    (t1, rgt) = staged(forward_t, stride, [q0, t0, r, t], [square] * 2, 6)

    (relay, gt) = staged(pair_reflect(5), stride, [hopped, r, t, q, u, gt], [square] * 2, 6)
    bounced = moved(relay, [(5, 4), (7, 5)])
    gt_came = moved(gt, [(5, 6), (6, 7)])

    def forward_u(k, u0, hu, rgt, u1, w):
        @pl.when((k == 4) | (k == 5))
        def _():
            factor = left(u0[...])
            w[...] = jnp.dot(factor, right(rgt[...]), preferred_element_type=F32)
            u1[...] = jnp.dot(factor, right(hu[...]), preferred_element_type=F32)

    (u1, w) = staged(forward_u, stride, [u0, hu, rgt], [square] * 2, 2)
    w_came = moved(w, back)

    def low_fields(k, first, came, q0, r, t, f1, rg):
        @pl.when(k == 0)
        def _():
            f1[...] = first[:, :width]

        @pl.when(k == 1)
        def _():
            g = summed(product(q0[...], r[...]), came[:, :width], True)
            f1[...] = product(t[...], g)
            rg[...] = product(r[...], g)

    (f1, rg) = staged(low_fields, stride, [first, first_came, q0, r, t], [field] * 2, 2)
    fa = moved(f1, low)

    def second_reflect(k, bounced, q1, t1, u1, w, total, gt_out):
        @pl.when((k == 4) | (k == 5))
        def _():
            gt = summed(product(q1[...], bounced[...]), t1[...])
            gt_out[...] = gt
            total[...] = w[...] + product(u1[...], product(bounced[...], gt))

    (total, gt2) = staged(second_reflect, stride, [bounced, q1, t1, u1, w], [square] * 2, 6
    )
    total_came = moved(total, back)
    gt2_came = moved(gt2, [(4, 6), (5, 7)])

    def low_u(k, u0, u1_up, u, hu, rgt, rg, first, came, both, w):
        side = u.shape[1]

        @pl.when(k == 0)
        def _():
            both[:, :side] = u[...]
            both[:, side:] = first[:, width:]

        @pl.when((k > 0) & (k < 4))
        def _():
            factor = left(jnp.where(k == 2, u1_up[...], u0[...]))
            both[:, :side] = jnp.dot(factor, right(hu[...]), preferred_element_type=F32)

            @pl.when(k == 1)
            def _():
                both[:, side:] = came[:, width:] + jnp.dot(
                    factor, right(rg[...]), preferred_element_type=F32
                )

            @pl.when(k > 1)
            def _():
                w[...] = jnp.dot(factor, right(rgt[...]), preferred_element_type=F32)

    (both, w_low) = staged(
        low_u,
        stride,
        [u0_low, u1_up, u, hu, rgt, rg, first, first_came],
        [(square[0], square[1] + width), square],
        2,
    )
    ua = moved(both, low)

    def own_fields(k, r2_up, hopped, w, r1):
        @pl.when(k == 2)
        def _():
            r1[...] = hopped[...] + w[...]

        @pl.when(k == 3)
        def _():
            r1[...] = r2_up[...] + w[...]

    (r1,) = staged(own_fields, stride, [r2_up, hopped, w_low], [square], 0.1)

    def second_q(k, r1, qa, q1, t1, both, q2, hu_out):
        @pl.when((k == 2) | (k == 3))
        def _():
            hu = summed(product(r1[...], qa[...]), both[:, : q1.shape[1]], True)
            hu_out[...] = hu
            q2[...] = q1[...] + product(t1[...], product(qa[...], hu))

    (q2, hu2) = staged(second_q, stride, [r1, qa, q1, t1, both], [square] * 2, 6)

    def second_fields(k, qa, fa, r1, t1, f2, g2):
        @pl.when((k == 2) | (k == 3))
        def _():
            g = summed(product(qa[...], r1[...]), fa[...], True)
            g2[...] = g
            f2[...] = product(t1[...], g)

    (f2, g2) = staged(second_fields, stride, [qa, fa, r1, t1], [field, field], 2)

    def third_fields(k, r_late, r_next, w_came, q1, t1, both, r1, qa, fa, w4, g4, rc4):
        @pl.when((k == 2) | (k == 3))
        def _():
            came = jnp.where(k == 2, r_late[...], r_next[...]) + w_came[...]
            gt = summed(product(q1[...], came), t1[...], True)
            rc = r1[...] + product(both[:, : q1.shape[1]], product(came, gt))
            rc4[...] = rc
            g = summed(product(qa[...], rc), fa[...], True)
            g4[...] = g
            w4[...] = product(gt, g)

    (w4, g4, rc4) = staged(
        third_fields,
        stride,
        [r_late, r_next, w_came, q1, t1, both, r1, qa, fa],
        [field, field, square],
        9,
    )
    w4_came = moved(w4, [(2, 4), (3, 5)])

    def second_through(k, t, gt_came, gt2_came, t2):
        @pl.when(k > 5)
        def _():
            t2[...] = product(product(t[...], gt_came[...]), gt2_came[...])

    (t2,) = staged(second_through, stride, [t, gt_came, gt2_came], [square], 2)

    def last_fields(k, r_late, r_next, total_came, q2, f2, g6):
        @pl.when((k == 2) | (k == 3))
        def _():
            rc = jnp.where(k == 2, r_late[...], r_next[...]) + total_came[...]
            g6[...] = summed(product(q2[...], rc), f2[...])

    (g6,) = staged(last_fields, stride, [r_late, r_next, total_came, q2, f2], [field], 3)
    g6_odd = moved(g6, [(2, 6), (3, 7)], 1, 2)
    g6_even = moved(g6, [(2, 6), (3, 7)], 0, 2)

    def passed(value, choose):
        pairs = [(i, i + 1) for i in range(length - 1) if choose(i)]
        return lax.ppermute(value, "sec", pairs)

    half = NODES // 2 * stride
    next_low = passed(jnp.where(k < 2, f1, f2), lambda i: i < half)

    def all_reflected(
        k, ua, r1, g2, rc4, g4, r_late, r_next, total_came, g6, hu2, s2, s4, s6
    ):
        @pl.when((k == 2) | (k == 3))
        def _():
            rc = jnp.where(k == 2, r_late[...], r_next[...]) + total_came[...]
            rg2 = product(r1[...], g2[...])
            rg4 = product(rc4[...], g4[...])
            sums = rg2 + product(hu2[...], product(rc, g6[...]))
            value = product(ua[:, : hu2.shape[1]], jnp.concatenate([rg2, rg4, sums], axis=1))
            for i, out in enumerate((s2, s4, s6)):
                out[...] = ua[:, hu2.shape[1] :] + value[:, i * width : (i + 1) * width]

    (s2, s4, s6) = staged(
        all_reflected,
        stride,
        [ua, r1, g2, rc4, g4, r_late, r_next, total_came, g6, hu2],
        [field] * 3,
        3,
    )
    s6_came = moved(s6, [(2, 6), (3, 7)])
    s4_came = moved(s4, [(2, 4), (3, 5)])

    def through_odd(d, f1, f2, t1, w4, t2, g6, out):
        k = d // stride

        @pl.when(k < 2)
        def _():
            out[...] = f1[...]

        @pl.when((k == 2) | (k == 3))
        def _():
            out[...] = f2[...]

        @pl.when((k == 4) | (k == 5))
        def _():
            out[...] = product(t1[...], w4[...])

        @pl.when((k > 5) & (d % 2 == 1))
        def _():
            out[...] = product(t2[...], g6[...])

    (odd,) = staged(through_odd, 1, [f1, f2, t1, w4_came, t2, g6_odd], [field], 1)
    next_odd = passed(odd, lambda i: i >= half and i % 2 == 1)

    def through_even(d, odd, t2, g6, out):
        k = d // stride
        late = (k > 5) & (d % 2 == 0)

        @pl.when(late)
        def _():
            out[...] = product(t2[...], g6[...])

        @pl.when(jnp.logical_not(late))
        def _():
            out[...] = odd[...]

    (through_field,) = staged(through_even, 1, [odd, t2, g6_even], [field], 1)
    next_even = passed(through_field, lambda i: i >= half and i % 2 == 0)
    reflected = jnp.where(
        k < 2, both[:, square[1] :], jnp.where(k < 4, s2, jnp.where(k < 6, s4_came, s6_came))
    )

    def depths(d, maps, low, odd, even, incident, out):
        came = jnp.where(d % 2 == 1, even[...], odd[...])
        came = jnp.where(d <= half, low[...], came)
        value = right(jnp.where(d == 0, incident[...], came))

        @pl.loop(0, depth_maps.shape[1])
        def _(j):
            out[j] = jnp.dot(maps[j], value, preferred_element_type=F32)

    (depth_fields,) = staged(
        depths,
        1,
        [maps, next_low, next_odd, next_even, incident],
        [depth_maps.shape[1:3] + field[1:]],
        1,
    )
    return (through_field[None], reflected[None], depth_fields[None])


def solution(mesh):
    in_specs = (
        P("sec", None, None),
        P("sec", None, None),
        P("sec", None, None),
        P("sec", None, None),
        P("sec", None, None, None),
        P(),
    )
    out_specs = (P("sec", None, None), P("sec", None, None), P("sec", None, None, None))

    return jax.shard_map(
        per_device, mesh=mesh, in_specs=in_specs, out_specs=out_specs, check_vma=False
    )
```

```python
import jax
import jax.numpy as jnp
from jax import lax
from jax.experimental import pallas as pl
from jax.experimental.pallas import tpu as pltpu
from jax.sharding import PartitionSpec as P

SEGMENTS = 3
NODES = 2**SEGMENTS
F32 = jnp.float32


def split(value):
    high = value.astype(jnp.bfloat16)
    return high, (value - high.astype(F32)).astype(jnp.bfloat16)


def left(value):
    high, low = split(value)
    return jnp.concatenate([high, high, low], axis=1)


def right(value):
    high, low = split(value)
    return jnp.concatenate([high, low, high], axis=0)


def product(former, latter):
    return jnp.dot(left(former), right(latter), preferred_element_type=F32)


def summed(bounce, value, rolled=False):
    factor = left(bounce)

    def step(_, total):
        return value + jnp.dot(factor, right(total), preferred_element_type=F32)

    return lax.fori_loop(0, 3, step, value, unroll=not rolled)


def staged(body, stride, inputs, outputs, products, dtype=F32):
    def kernel(*refs):
        body(lax.axis_index("sec") // stride, *refs)

    vmem = pl.BlockSpec(memory_space=pltpu.VMEM)
    side = inputs[0].shape[-1]
    moved_bytes = 4 * side * side * (len(inputs) + len(outputs))
    return pl.pallas_call(
        kernel,
        out_shape=[jax.ShapeDtypeStruct(shape, dtype) for shape in outputs],
        in_specs=[vmem] * len(inputs),
        out_specs=[vmem] * len(outputs),
        compiler_params=pltpu.CompilerParams(vmem_limit_bytes=24 * 2**20),
        cost_estimate=pl.CostEstimate(
            flops=int(products * 6 * side**3), bytes_accessed=moved_bytes, transcendentals=0
        ),
    )(*inputs)


def per_device(front_reflect, front_through, back_reflect, back_through, depth_maps, incident):
    length = lax.axis_size("sec")
    stride = length // NODES
    position = lax.axis_index("sec")
    k = position // stride
    square, field = front_reflect.shape[1:], incident.shape

    def moved(value, routes, start=0, step=1):
        pairs = [
            (a * stride + i, b * stride + i)
            for a, b in routes
            for i in range(start, stride, step)
        ]
        return lax.ppermute(value, "sec", pairs)

    r, t, q, u = front_reflect[0], front_through[0], back_reflect[0], back_through[0]
    width = field[1]
    fields = (field[0], 2 * width)
    low = [(0, 2), (1, 3)]
    back = [(4, 2), (5, 3)]
    middle = [(2, 3), (3, 4), (4, 5)]

    swapped = moved(r, [(7, 6), (6, 7), (1, 0)])
    r2_down = moved(r, [(2, 0)])
    q0 = moved(q, [(0, 1), (1, 2)] + middle)
    t0 = moved(t, [(1, 2)] + middle)
    u1_over = moved(u, [(1, 0)])
    u0 = moved(u, [(3, 4), (4, 5)])
    u0_low = moved(u, [(0, 1), (2, 3)])
    r_late = moved(r, [(3, 2)])
    r_next = moved(r, [(4, 3)])

    def load(k, r, t, q, u, incident, *out):
        for i, ref in enumerate((r, t, q, u)):
            out[i][...] = ref[...]

        @pl.when(k == 0)
        def _():
            value = right(incident[...])
            out[4][:, :width] = jnp.dot(left(t[...]), value, preferred_element_type=F32)
            out[4][:, width:] = jnp.dot(left(r[...]), value, preferred_element_type=F32)

    r, t, q, u, first = staged(load, stride, [r, t, q, u, incident], [square] * 4 + [fields], 1)
    first_came = moved(first, [(0, 1)])

    def pair_reflect(at):
        def body(k, came, r, t, q, u, *rest):
            out, gt_out = rest[-2:]

            @pl.when(k == at)
            def _():
                gt = summed(product(q[...], came[...]), t[...], True)
                gt_out[...] = gt
                out[...] = r[...] + product(u[...], product(came[...], gt))

            @pl.when(k != at)
            def _():
                out[...] = came[...]
                if len(rest) == 3:
                    gt_out[...] = rest[0][...]

        return body

    (relay, gt) = staged(pair_reflect(6), stride, [swapped, r, t, q, u], [square] * 2, 6)
    hopped = moved(relay, [(6, 7), (7, 5), (0, 2)])
    r2_over = moved(r2_down, [(0, 1)])
    u1_up = moved(u1_over, [(0, 2)])
    r2_up = moved(r2_over, [(1, 3)])

    def forward_q(k, q0, r, t, q, u, q1, hu_out):
        @pl.when(k == 0)
        def _():
            q1[...] = q[...]

        @pl.when((k > 0) & (k < 6))
        def _():
            hu = summed(product(r[...], q0[...]), u[...], True)
            hu_out[...] = hu
            q1[...] = q[...] + product(t[...], product(q0[...], hu))

    (q1, hu) = staged(forward_q, stride, [q0, r, t, q, u], [square] * 2, 6)
    qa = moved(q1, low)

    maps = depth_maps[0]

    def forward_t(k, q0, t0, r, t, t1, rgt):
        @pl.when((k > 1) & (k < 6))
        def _():
            gt = summed(product(q0[...], r[...]), t0[...], True)
            rgt[...] = product(r[...], gt)
            t1[...] = product(t[...], gt)

    (t1, rgt) = staged(forward_t, stride, [q0, t0, r, t], [square] * 2, 6)

    (relay, gt) = staged(pair_reflect(5), stride, [hopped, r, t, q, u, gt], [square] * 2, 6)
    bounced = moved(relay, [(5, 4), (7, 5)])
    gt_came = moved(gt, [(5, 6), (6, 7)])

    def forward_u(k, u0, hu, rgt, u1, w):
        @pl.when((k == 4) | (k == 5))
        def _():
            factor = left(u0[...])
            w[...] = jnp.dot(factor, right(rgt[...]), preferred_element_type=F32)
            u1[...] = jnp.dot(factor, right(hu[...]), preferred_element_type=F32)

    (u1, w) = staged(forward_u, stride, [u0, hu, rgt], [square] * 2, 2)
    w_came = moved(w, back)

    def low_fields(k, first, came, q0, r, t, f1, rg):
        @pl.when(k == 0)
        def _():
            f1[...] = first[:, :width]

        @pl.when(k == 1)
        def _():
            g = summed(product(q0[...], r[...]), came[:, :width], True)
            f1[...] = product(t[...], g)
            rg[...] = product(r[...], g)

    (f1, rg) = staged(low_fields, stride, [first, first_came, q0, r, t], [field] * 2, 2)
    fa = moved(f1, low)

    def second_reflect(k, bounced, q1, t1, u1, w, total, gt_out):
        @pl.when((k == 4) | (k == 5))
        def _():
            gt = summed(product(q1[...], bounced[...]), t1[...])
            gt_out[...] = gt
            total[...] = w[...] + product(u1[...], product(bounced[...], gt))

    (total, gt2) = staged(second_reflect, stride, [bounced, q1, t1, u1, w], [square] * 2, 6
    )
    total_came = moved(total, back)
    gt2_came = moved(gt2, [(4, 6), (5, 7)])

    def low_u(k, u0, u1_up, u, hu, rgt, rg, first, came, both, w):
        side = u.shape[1]

        @pl.when(k == 0)
        def _():
            both[:, :side] = u[...]
            both[:, side:] = first[:, width:]

        @pl.when((k > 0) & (k < 4))
        def _():
            factor = left(jnp.where(k == 2, u1_up[...], u0[...]))
            both[:, :side] = jnp.dot(factor, right(hu[...]), preferred_element_type=F32)

            @pl.when(k == 1)
            def _():
                both[:, side:] = came[:, width:] + jnp.dot(
                    factor, right(rg[...]), preferred_element_type=F32
                )

            @pl.when(k > 1)
            def _():
                w[...] = jnp.dot(factor, right(rgt[...]), preferred_element_type=F32)

    (both, w_low) = staged(
        low_u,
        stride,
        [u0_low, u1_up, u, hu, rgt, rg, first, first_came],
        [(square[0], square[1] + width), square],
        2,
    )
    ua = moved(both, low)

    def own_fields(k, r2_up, hopped, w, r1):
        @pl.when(k == 2)
        def _():
            r1[...] = hopped[...] + w[...]

        @pl.when(k == 3)
        def _():
            r1[...] = r2_up[...] + w[...]

    (r1,) = staged(own_fields, stride, [r2_up, hopped, w_low], [square], 0.1)

    def second_q(k, r1, qa, q1, t1, both, q2, hu_out):
        @pl.when((k == 2) | (k == 3))
        def _():
            hu = summed(product(r1[...], qa[...]), both[:, : q1.shape[1]], True)
            hu_out[...] = hu
            q2[...] = q1[...] + product(t1[...], product(qa[...], hu))

    (q2, hu2) = staged(second_q, stride, [r1, qa, q1, t1, both], [square] * 2, 6)

    def second_fields(k, f1, qa, fa, r1, t1, f2, g2):
        @pl.when(k < 2)
        def _():
            f2[...] = f1[...]

        @pl.when((k == 2) | (k == 3))
        def _():
            g = summed(product(qa[...], r1[...]), fa[...], True)
            g2[...] = g
            f2[...] = product(t1[...], g)

    (f2, g2) = staged(second_fields, stride, [f1, qa, fa, r1, t1], [field, field], 2)

    def third_fields(k, r_late, r_next, w_came, q1, t1, both, r1, qa, fa, w4, g4, rc4):
        @pl.when((k == 2) | (k == 3))
        def _():
            came = jnp.where(k == 2, r_late[...], r_next[...]) + w_came[...]
            gt = summed(product(q1[...], came), t1[...], True)
            rc = r1[...] + product(both[:, : q1.shape[1]], product(came, gt))
            rc4[...] = rc
            g = summed(product(qa[...], rc), fa[...], True)
            g4[...] = g
            w4[...] = product(gt, g)

    (w4, g4, rc4) = staged(
        third_fields,
        stride,
        [r_late, r_next, w_came, q1, t1, both, r1, qa, fa],
        [field, field, square],
        9,
    )
    w4_came = moved(w4, [(2, 4), (3, 5)])

    def second_through(k, t, gt_came, gt2_came, t2):
        @pl.when(k > 5)
        def _():
            t2[...] = product(product(t[...], gt_came[...]), gt2_came[...])

    (t2,) = staged(second_through, stride, [t, gt_came, gt2_came], [square], 2)

    def last_fields(k, r_late, r_next, total_came, q2, f2, g6):
        @pl.when((k == 2) | (k == 3))
        def _():
            rc = jnp.where(k == 2, r_late[...], r_next[...]) + total_came[...]
            g6[...] = summed(product(q2[...], rc), f2[...])

    (g6,) = staged(last_fields, stride, [r_late, r_next, total_came, q2, f2], [field], 3)
    g6_odd = moved(g6, [(2, 6), (3, 7)], 1, 2)
    g6_even = moved(g6, [(2, 6), (3, 7)], 0, 2)

    def passed(value, choose):
        pairs = [(i, i + 1) for i in range(length - 1) if choose(i)]
        return lax.ppermute(value, "sec", pairs)

    half = NODES // 2 * stride
    next_low = passed(f2, lambda i: i < half)

    def all_reflected(
        k, ua, r1, g2, rc4, g4, r_late, r_next, total_came, g6, hu2, s2, s4, s6
    ):
        @pl.when((k == 2) | (k == 3))
        def _():
            rc = jnp.where(k == 2, r_late[...], r_next[...]) + total_came[...]
            rg2 = product(r1[...], g2[...])
            rg4 = product(rc4[...], g4[...])
            sums = rg2 + product(hu2[...], product(rc, g6[...]))
            value = product(ua[:, : hu2.shape[1]], jnp.concatenate([rg2, rg4, sums], axis=1))
            for i, out in enumerate((s2, s4, s6)):
                out[...] = ua[:, hu2.shape[1] :] + value[:, i * width : (i + 1) * width]

    (s2, s4, s6) = staged(
        all_reflected,
        stride,
        [ua, r1, g2, rc4, g4, r_late, r_next, total_came, g6, hu2],
        [field] * 3,
        3,
    )
    s6_came = moved(s6, [(2, 6), (3, 7)])
    s4_came = moved(s4, [(2, 4), (3, 5)])

    def through_odd(d, f2, t1, w4, t2, g6, out):
        k = d // stride

        @pl.when(k < 4)
        def _():
            out[...] = f2[...]

        @pl.when((k == 4) | (k == 5))
        def _():
            out[...] = product(t1[...], w4[...])

        @pl.when((k > 5) & (d % 2 == 1))
        def _():
            out[...] = product(t2[...], g6[...])

    (odd,) = staged(through_odd, 1, [f2, t1, w4_came, t2, g6_odd], [field], 1)
    next_odd = passed(odd, lambda i: i >= half and i % 2 == 1)

    def through_even(d, odd, t2, g6, out):
        k = d // stride
        late = (k > 5) & (d % 2 == 0)

        @pl.when(late)
        def _():
            out[...] = product(t2[...], g6[...])

        @pl.when(jnp.logical_not(late))
        def _():
            out[...] = odd[...]

    (through_field,) = staged(through_even, 1, [odd, t2, g6_even], [field], 1)
    next_even = passed(through_field, lambda i: i >= half and i % 2 == 0)
    reflected = jnp.where(
        k < 2, both[:, square[1] :], jnp.where(k < 4, s2, jnp.where(k < 6, s4_came, s6_came))
    )

    def depths(d, maps, low, odd, even, incident, out):
        came = jnp.where(d % 2 == 1, even[...], odd[...])
        came = jnp.where(d <= half, low[...], came)
        value = right(jnp.where(d == 0, incident[...], came))

        @pl.loop(0, depth_maps.shape[1])
        def _(j):
            out[j] = jnp.dot(left(maps[j]), value, preferred_element_type=F32)

    (depth_fields,) = staged(
        depths,
        1,
        [maps, next_low, next_odd, next_even, incident],
        [depth_maps.shape[1:3] + field[1:]],
        1,
    )
    return (through_field[None], reflected[None], depth_fields[None])


def solution(mesh):
    in_specs = (
        P("sec", None, None),
        P("sec", None, None),
        P("sec", None, None),
        P("sec", None, None),
        P("sec", None, None, None),
        P(),
    )
    out_specs = (P("sec", None, None), P("sec", None, None), P("sec", None, None, None))

    return jax.shard_map(
        per_device, mesh=mesh, in_specs=in_specs, out_specs=out_specs, check_vma=False
    )
```

```python
import jax
import jax.numpy as jnp
from jax import lax
from jax.experimental import pallas as pl
from jax.experimental.pallas import tpu as pltpu
from jax.sharding import PartitionSpec as P

SEGMENTS = 3
NODES = 2**SEGMENTS
F32 = jnp.float32


def split(value):
    high = value.astype(jnp.bfloat16)
    return high, (value - high.astype(F32)).astype(jnp.bfloat16)


def left(value):
    high, low = split(value)
    return jnp.concatenate([high, high, low], axis=1)


def right(value):
    high, low = split(value)
    return jnp.concatenate([high, low, high], axis=0)


def product(former, latter):
    return jnp.dot(left(former), right(latter), preferred_element_type=F32)


def summed(bounce, value, rolled=False):
    factor = left(bounce)

    def step(_, total):
        return value + jnp.dot(factor, right(total), preferred_element_type=F32)

    return lax.fori_loop(0, 3, step, value, unroll=not rolled)


def staged(body, stride, inputs, outputs, products, dtype=F32):
    def kernel(*refs):
        body(lax.axis_index("sec") // stride, *refs)

    vmem = pl.BlockSpec(memory_space=pltpu.VMEM)
    side = inputs[0].shape[-1]
    moved_bytes = 4 * side * side * (len(inputs) + len(outputs))
    return pl.pallas_call(
        kernel,
        out_shape=[jax.ShapeDtypeStruct(shape, dtype) for shape in outputs],
        in_specs=[vmem] * len(inputs),
        out_specs=[vmem] * len(outputs),
        compiler_params=pltpu.CompilerParams(vmem_limit_bytes=24 * 2**20),
        cost_estimate=pl.CostEstimate(
            flops=int(products * 6 * side**3), bytes_accessed=moved_bytes, transcendentals=0
        ),
    )(*inputs)


def per_device(front_reflect, front_through, back_reflect, back_through, depth_maps, incident):
    length = lax.axis_size("sec")
    stride = length // NODES
    square, field = front_reflect.shape[1:], incident.shape

    def moved(value, routes, start=0, step=1):
        pairs = [
            (a * stride + i, b * stride + i)
            for a, b in routes
            for i in range(start, stride, step)
        ]
        return lax.ppermute(value, "sec", pairs)

    r, t, q, u = front_reflect[0], front_through[0], back_reflect[0], back_through[0]
    width = field[1]
    fields = (field[0], 2 * width)
    low = [(0, 2), (1, 3)]
    back = [(4, 2), (5, 3)]
    middle = [(2, 3), (3, 4), (4, 5)]

    swapped = moved(r, [(7, 6), (6, 7), (1, 0)])
    r2_down = moved(r, [(2, 0)])
    q0 = moved(q, [(0, 1), (1, 2)] + middle)
    t0 = moved(t, [(1, 2)] + middle)
    u1_over = moved(u, [(1, 0)])
    u0 = moved(u, [(3, 4), (4, 5)])
    u0_low = moved(u, [(0, 1), (2, 3)])
    r_late = moved(r, [(3, 2)])
    r_next = moved(r, [(4, 3)])

    def load(k, r, t, q, u, incident, *out):
        for i, ref in enumerate((r, t, q, u)):
            out[i][...] = ref[...]

        @pl.when(k == 0)
        def _():
            value = right(incident[...])
            out[4][:, :width] = jnp.dot(left(t[...]), value, preferred_element_type=F32)
            out[4][:, width:] = jnp.dot(left(r[...]), value, preferred_element_type=F32)

    r, t, q, u, first = staged(load, stride, [r, t, q, u, incident], [square] * 4 + [fields], 1)
    first_came = moved(first, [(0, 1)])

    def pair_reflect(at):
        def body(k, came, r, t, q, u, *rest):
            out, gt_out = rest[-2:]

            @pl.when(k == at)
            def _():
                gt = summed(product(q[...], came[...]), t[...], True)
                gt_out[...] = gt
                out[...] = r[...] + product(u[...], product(came[...], gt))

            @pl.when(k != at)
            def _():
                out[...] = came[...]
                if len(rest) == 3:
                    gt_out[...] = rest[0][...]

        return body

    (relay, gt) = staged(pair_reflect(6), stride, [swapped, r, t, q, u], [square] * 2, 6)
    hopped = moved(relay, [(6, 7), (7, 5), (0, 2)])
    r2_over = moved(r2_down, [(0, 1)])
    u1_up = moved(u1_over, [(0, 2)])
    r2_up = moved(r2_over, [(1, 3)])

    def forward_q(k, q0, r, t, q, u, q1, hu_out):
        @pl.when(k == 0)
        def _():
            q1[...] = q[...]

        @pl.when((k > 0) & (k < 6))
        def _():
            hu = summed(product(r[...], q0[...]), u[...], True)
            hu_out[...] = hu
            q1[...] = q[...] + product(t[...], product(q0[...], hu))

    (q1, hu) = staged(forward_q, stride, [q0, r, t, q, u], [square] * 2, 6)
    qa = moved(q1, low)

    maps = depth_maps[0]

    def forward_t(k, q0, t0, r, t, t1, rgt):
        @pl.when((k > 1) & (k < 6))
        def _():
            gt = summed(product(q0[...], r[...]), t0[...], True)
            rgt[...] = product(r[...], gt)
            t1[...] = product(t[...], gt)

    (t1, rgt) = staged(forward_t, stride, [q0, t0, r, t], [square] * 2, 6)

    (relay, gt) = staged(pair_reflect(5), stride, [hopped, r, t, q, u, gt], [square] * 2, 6)
    bounced = moved(relay, [(5, 4), (7, 5)])
    gt_came = moved(gt, [(5, 6), (6, 7)])

    def forward_u(k, u0, hu, rgt, u1, w):
        @pl.when((k == 4) | (k == 5))
        def _():
            factor = left(u0[...])
            w[...] = jnp.dot(factor, right(rgt[...]), preferred_element_type=F32)
            u1[...] = jnp.dot(factor, right(hu[...]), preferred_element_type=F32)

    (u1, w) = staged(forward_u, stride, [u0, hu, rgt], [square] * 2, 2)
    w_came = moved(w, back)

    def low_fields(k, first, came, q0, r, t, f1, rg):
        @pl.when(k == 0)
        def _():
            f1[...] = first[:, :width]

        @pl.when(k == 1)
        def _():
            g = summed(product(q0[...], r[...]), came[:, :width], True)
            f1[...] = product(t[...], g)
            rg[...] = product(r[...], g)

    (f1, rg) = staged(low_fields, stride, [first, first_came, q0, r, t], [field] * 2, 2)
    fa = moved(f1, low)

    def second_reflect(k, bounced, q1, t1, u1, w, total, gt_out):
        @pl.when((k == 4) | (k == 5))
        def _():
            gt = summed(product(q1[...], bounced[...]), t1[...])
            gt_out[...] = gt
            total[...] = w[...] + product(u1[...], product(bounced[...], gt))

    (total, gt2) = staged(second_reflect, stride, [bounced, q1, t1, u1, w], [square] * 2, 6
    )
    total_came = moved(total, back)
    gt2_came = moved(gt2, [(4, 6), (5, 7)])

    def low_u(k, u0, u1_up, u, hu, rgt, rg, first, came, both, w):
        side = u.shape[1]

        @pl.when(k == 0)
        def _():
            both[:, :side] = u[...]
            both[:, side:] = first[:, width:]

        @pl.when((k > 0) & (k < 4))
        def _():
            factor = left(jnp.where(k == 2, u1_up[...], u0[...]))
            both[:, :side] = jnp.dot(factor, right(hu[...]), preferred_element_type=F32)

            @pl.when(k == 1)
            def _():
                both[:, side:] = came[:, width:] + jnp.dot(
                    factor, right(rg[...]), preferred_element_type=F32
                )

            @pl.when(k > 1)
            def _():
                w[...] = jnp.dot(factor, right(rgt[...]), preferred_element_type=F32)

    (both, w_low) = staged(
        low_u,
        stride,
        [u0_low, u1_up, u, hu, rgt, rg, first, first_came],
        [(square[0], square[1] + width), square],
        2,
    )
    ua = moved(both, low)

    def own_fields(k, r2_up, hopped, w, r1):
        @pl.when(k == 2)
        def _():
            r1[...] = hopped[...] + w[...]

        @pl.when(k == 3)
        def _():
            r1[...] = r2_up[...] + w[...]

    (r1,) = staged(own_fields, stride, [r2_up, hopped, w_low], [square], 0.1)

    def second_q(k, r1, qa, q1, t1, both, q2, hu_out):
        @pl.when((k == 2) | (k == 3))
        def _():
            hu = summed(product(r1[...], qa[...]), both[:, : q1.shape[1]], True)
            hu_out[...] = hu
            q2[...] = q1[...] + product(t1[...], product(qa[...], hu))

    (q2, hu2) = staged(second_q, stride, [r1, qa, q1, t1, both], [square] * 2, 6)

    def second_fields(k, f1, qa, fa, r1, t1, f2, g2):
        @pl.when(k < 2)
        def _():
            f2[...] = f1[...]

        @pl.when((k == 2) | (k == 3))
        def _():
            g = summed(product(qa[...], r1[...]), fa[...], True)
            g2[...] = g
            f2[...] = product(t1[...], g)

    (f2, g2) = staged(second_fields, stride, [f1, qa, fa, r1, t1], [field, field], 2)

    def third_fields(k, r_late, r_next, w_came, q1, t1, both, r1, qa, fa, w4, g4, rc4):
        @pl.when((k == 2) | (k == 3))
        def _():
            came = jnp.where(k == 2, r_late[...], r_next[...]) + w_came[...]
            gt = summed(product(q1[...], came), t1[...], True)
            rc = r1[...] + product(both[:, : q1.shape[1]], product(came, gt))
            rc4[...] = rc
            g = summed(product(qa[...], rc), fa[...], True)
            g4[...] = g
            w4[...] = product(gt, g)

    (w4, g4, rc4) = staged(
        third_fields,
        stride,
        [r_late, r_next, w_came, q1, t1, both, r1, qa, fa],
        [field, field, square],
        9,
    )
    w4_came = moved(w4, [(2, 4), (3, 5)])

    def second_through(k, t, gt_came, gt2_came, t2):
        @pl.when(k > 5)
        def _():
            t2[...] = product(product(t[...], gt_came[...]), gt2_came[...])

    (t2,) = staged(second_through, stride, [t, gt_came, gt2_came], [square], 2)

    def last_fields(k, r_late, r_next, total_came, q2, f2, g6):
        @pl.when((k == 2) | (k == 3))
        def _():
            rc = jnp.where(k == 2, r_late[...], r_next[...]) + total_came[...]
            g6[...] = summed(product(q2[...], rc), f2[...])

    (g6,) = staged(last_fields, stride, [r_late, r_next, total_came, q2, f2], [field], 3)
    g6_odd = moved(g6, [(2, 6), (3, 7)], 1, 2)
    g6_even = moved(g6, [(2, 6), (3, 7)], 0, 2)

    def passed(value, choose):
        pairs = [(i, i + 1) for i in range(length - 1) if choose(i)]
        return lax.ppermute(value, "sec", pairs)

    half = NODES // 2 * stride
    next_low = passed(f2, lambda i: i < half)

    def all_reflected(
        k, ua, r1, g2, rc4, g4, r_late, r_next, total_came, g6, hu2, s2, s4, s6
    ):
        @pl.when((k == 2) | (k == 3))
        def _():
            rc = jnp.where(k == 2, r_late[...], r_next[...]) + total_came[...]
            rg2 = product(r1[...], g2[...])
            rg4 = product(rc4[...], g4[...])
            sums = rg2 + product(hu2[...], product(rc, g6[...]))
            value = product(ua[:, : hu2.shape[1]], jnp.concatenate([rg2, rg4, sums], axis=1))
            for i, out in enumerate((s2, s4, s6)):
                out[...] = ua[:, hu2.shape[1] :] + value[:, i * width : (i + 1) * width]

    (s2, s4, s6) = staged(
        all_reflected,
        stride,
        [ua, r1, g2, rc4, g4, r_late, r_next, total_came, g6, hu2],
        [field] * 3,
        3,
    )
    s6_came = moved(s6, [(2, 6), (3, 7)])
    s4_came = moved(s4, [(2, 4), (3, 5)])

    def through_odd(d, f2, t1, w4, t2, g6, out):
        k = d // stride

        @pl.when(k < 4)
        def _():
            out[...] = f2[...]

        @pl.when((k == 4) | (k == 5))
        def _():
            out[...] = product(t1[...], w4[...])

        @pl.when((k > 5) & (d % 2 == 1))
        def _():
            out[...] = product(t2[...], g6[...])

    (odd,) = staged(through_odd, 1, [f2, t1, w4_came, t2, g6_odd], [field], 1)
    next_odd = passed(odd, lambda i: i >= half and i % 2 == 1)

    def through_even(d, odd, t2, g6, out):
        k = d // stride
        late = (k > 5) & (d % 2 == 0)

        @pl.when(late)
        def _():
            out[...] = product(t2[...], g6[...])

        @pl.when(jnp.logical_not(late))
        def _():
            out[...] = odd[...]

    (through_field,) = staged(through_even, 1, [odd, t2, g6_even], [field], 1)
    next_even = passed(through_field, lambda i: i >= half and i % 2 == 0)

    def depths(d, maps, low, odd, even, incident, out):
        came = jnp.where(d % 2 == 1, even[...], odd[...])
        came = jnp.where(d <= half, low[...], came)
        value = right(jnp.where(d == 0, incident[...], came))
        for j in range(depth_maps.shape[1]):
            out[j] = jnp.dot(left(maps[j]), value, preferred_element_type=F32)

    (depth_fields,) = staged(
        depths,
        1,
        [maps, next_low, next_odd, next_even, incident],
        [depth_maps.shape[1:3] + field[1:]],
        1,
    )

    def reflected_out(k, both, s2, s4, s6, out):
        @pl.when(k < 2)
        def _():
            out[...] = both[:, square[1] :]

        @pl.when((k == 2) | (k == 3))
        def _():
            out[...] = s2[...]

        @pl.when((k == 4) | (k == 5))
        def _():
            out[...] = s4[...]

        @pl.when(k > 5)
        def _():
            out[...] = s6[...]

    (reflected,) = staged(reflected_out, stride, [both, s2, s4_came, s6_came], [field], 0.1)
    return (through_field[None], reflected[None], depth_fields[None])


def solution(mesh):
    in_specs = (
        P("sec", None, None),
        P("sec", None, None),
        P("sec", None, None),
        P("sec", None, None),
        P("sec", None, None, None),
        P(),
    )
    out_specs = (P("sec", None, None), P("sec", None, None), P("sec", None, None, None))

    return jax.shard_map(
        per_device, mesh=mesh, in_specs=in_specs, out_specs=out_specs, check_vma=False
    )
```

```python
import jax
import jax.numpy as jnp
from jax import lax
from jax.experimental import pallas as pl
from jax.experimental.pallas import tpu as pltpu
from jax.sharding import PartitionSpec as P

SEGMENTS = 3
NODES = 2**SEGMENTS
F32 = jnp.float32


def split(value):
    high = value.astype(jnp.bfloat16)
    return high, (value - high.astype(F32)).astype(jnp.bfloat16)


def left(value):
    high, low = split(value)
    return jnp.concatenate([high, high, low], axis=1)


def right(value):
    high, low = split(value)
    return jnp.concatenate([high, low, high], axis=0)


def product(former, latter):
    return jnp.dot(left(former), right(latter), preferred_element_type=F32)


def summed(bounce, value, rolled=False):
    factor = left(bounce)

    def step(_, total):
        return value + jnp.dot(factor, right(total), preferred_element_type=F32)

    return lax.fori_loop(0, 3, step, value, unroll=not rolled)


def staged(body, stride, inputs, outputs, products, dtype=F32):
    def kernel(*refs):
        body(lax.axis_index("sec") // stride, *refs)

    vmem = pl.BlockSpec(memory_space=pltpu.VMEM)
    side = inputs[0].shape[-1]
    moved_bytes = 4 * side * side * (len(inputs) + len(outputs))
    return pl.pallas_call(
        kernel,
        out_shape=[jax.ShapeDtypeStruct(shape, dtype) for shape in outputs],
        in_specs=[vmem] * len(inputs),
        out_specs=[vmem] * len(outputs),
        compiler_params=pltpu.CompilerParams(vmem_limit_bytes=24 * 2**20),
        cost_estimate=pl.CostEstimate(
            flops=int(products * 6 * side**3), bytes_accessed=moved_bytes, transcendentals=0
        ),
    )(*inputs)


def per_device(front_reflect, front_through, back_reflect, back_through, depth_maps, incident):
    length = lax.axis_size("sec")
    stride = length // NODES
    square, field = front_reflect.shape[1:], incident.shape

    def moved(value, routes, start=0, step=1):
        pairs = [
            (a * stride + i, b * stride + i)
            for a, b in routes
            for i in range(start, stride, step)
        ]
        return lax.ppermute(value, "sec", pairs)

    r, t, q, u = front_reflect[0], front_through[0], back_reflect[0], back_through[0]
    width = field[1]
    fields = (field[0], 2 * width)
    low = [(0, 2), (1, 3)]
    back = [(4, 2), (5, 3)]
    middle = [(2, 3), (3, 4), (4, 5)]

    swapped = moved(r, [(7, 6), (6, 7), (1, 0)])
    r2_down = moved(r, [(2, 0)])
    q0 = moved(q, [(0, 1), (1, 2)] + middle)
    t0 = moved(t, [(1, 2)] + middle)
    u1_over = moved(u, [(1, 0)])
    u0 = moved(u, [(3, 4), (4, 5)])
    u0_low = moved(u, [(0, 1), (2, 3)])
    qa_raw = moved(q, [(0, 2)])
    r_late = moved(r, [(3, 2)])
    r_next = moved(r, [(4, 3)])

    def load(k, r, t, q, u, incident, *out):
        for i, ref in enumerate((r, t, q, u)):
            out[i][...] = ref[...]

        @pl.when(k == 0)
        def _():
            value = right(incident[...])
            out[4][:, :width] = jnp.dot(left(t[...]), value, preferred_element_type=F32)
            out[4][:, width:] = jnp.dot(left(r[...]), value, preferred_element_type=F32)

    r, t, q, u, first = staged(load, stride, [r, t, q, u, incident], [square] * 4 + [fields], 1)
    first_came = moved(first, [(0, 1)])

    def pair_reflect(at):
        def body(k, came, r, t, q, u, *rest):
            out, gt_out = rest[-2:]

            @pl.when(k == at)
            def _():
                gt = summed(product(q[...], came[...]), t[...], True)
                gt_out[...] = gt
                out[...] = r[...] + product(u[...], product(came[...], gt))

            @pl.when(k != at)
            def _():
                out[...] = came[...]
                if len(rest) == 3:
                    gt_out[...] = rest[0][...]

        return body

    (relay, gt) = staged(pair_reflect(6), stride, [swapped, r, t, q, u], [square] * 2, 6)
    hopped = moved(relay, [(6, 7), (7, 5), (0, 2)])
    r2_over = moved(r2_down, [(0, 1)])
    u1_up = moved(u1_over, [(0, 2)])
    r2_up = moved(r2_over, [(1, 3)])

    def forward_q(k, q0, r, t, q, u, q1, hu_out):
        @pl.when(k == 0)
        def _():
            q1[...] = q[...]

        @pl.when((k > 0) & (k < 6))
        def _():
            hu = summed(product(r[...], q0[...]), u[...], True)
            hu_out[...] = hu
            q1[...] = q[...] + product(t[...], product(q0[...], hu))

    (q1, hu) = staged(forward_q, stride, [q0, r, t, q, u], [square] * 2, 6)
    qa = moved(q1, [(1, 3)])

    maps = depth_maps[0]

    def forward_t(k, q0, t0, r, t, t1, rgt):
        @pl.when((k > 1) & (k < 6))
        def _():
            gt = summed(product(q0[...], r[...]), t0[...], True)
            rgt[...] = product(r[...], gt)
            t1[...] = product(t[...], gt)

    (t1, rgt) = staged(forward_t, stride, [q0, t0, r, t], [square] * 2, 6)

    (relay, gt) = staged(pair_reflect(5), stride, [hopped, r, t, q, u, gt], [square] * 2, 6)
    bounced = moved(relay, [(5, 4), (7, 5)])
    gt_came = moved(gt, [(5, 6), (6, 7)])

    def forward_u(k, u0, hu, rgt, u1, w):
        @pl.when((k == 4) | (k == 5))
        def _():
            factor = left(u0[...])
            w[...] = jnp.dot(factor, right(rgt[...]), preferred_element_type=F32)
            u1[...] = jnp.dot(factor, right(hu[...]), preferred_element_type=F32)

    (u1, w) = staged(forward_u, stride, [u0, hu, rgt], [square] * 2, 2)
    w_came = moved(w, back)

    def low_fields(k, first, came, q0, r, t, f1, rg):
        @pl.when(k == 0)
        def _():
            f1[...] = first[:, :width]

        @pl.when(k == 1)
        def _():
            g = summed(product(q0[...], r[...]), came[:, :width], True)
            f1[...] = product(t[...], g)
            rg[...] = product(r[...], g)

    (f1, rg) = staged(low_fields, stride, [first, first_came, q0, r, t], [field] * 2, 2)
    fa = moved(f1, low)

    def second_reflect(k, bounced, q1, t1, u1, w, total, gt_out):
        @pl.when((k == 4) | (k == 5))
        def _():
            gt = summed(product(q1[...], bounced[...]), t1[...])
            gt_out[...] = gt
            total[...] = w[...] + product(u1[...], product(bounced[...], gt))

    (total, gt2) = staged(second_reflect, stride, [bounced, q1, t1, u1, w], [square] * 2, 6
    )
    total_came = moved(total, back)
    gt2_came = moved(gt2, [(4, 6), (5, 7)])

    def low_u(k, u0, u1_up, u, hu, rgt, rg, first, came, both, w):
        side = u.shape[1]

        @pl.when(k == 0)
        def _():
            both[:, :side] = u[...]
            both[:, side:] = first[:, width:]

        @pl.when((k > 0) & (k < 4))
        def _():
            factor = left(jnp.where(k == 2, u1_up[...], u0[...]))
            both[:, :side] = jnp.dot(factor, right(hu[...]), preferred_element_type=F32)

            @pl.when(k == 1)
            def _():
                both[:, side:] = came[:, width:] + jnp.dot(
                    factor, right(rg[...]), preferred_element_type=F32
                )

            @pl.when(k > 1)
            def _():
                w[...] = jnp.dot(factor, right(rgt[...]), preferred_element_type=F32)

    (both, w_low) = staged(
        low_u,
        stride,
        [u0_low, u1_up, u, hu, rgt, rg, first, first_came],
        [(square[0], square[1] + width), square],
        2,
    )
    ua = moved(both, low)

    def own_fields(k, r2_up, hopped, w, r1):
        @pl.when(k == 2)
        def _():
            r1[...] = hopped[...] + w[...]

        @pl.when(k == 3)
        def _():
            r1[...] = r2_up[...] + w[...]

    (r1,) = staged(own_fields, stride, [r2_up, hopped, w_low], [square], 0.1)

    def second_q(k, r1, qa_raw, qa, q1, t1, both, q2, hu_out):
        @pl.when((k == 2) | (k == 3))
        def _():
            came = jnp.where(k == 2, qa_raw[...], qa[...])
            hu = summed(product(r1[...], came), both[:, : q1.shape[1]], True)
            hu_out[...] = hu
            q2[...] = q1[...] + product(t1[...], product(came, hu))

    (q2, hu2) = staged(second_q, stride, [r1, qa_raw, qa, q1, t1, both], [square] * 2, 6)

    def second_fields(k, f1, qa_raw, qa, fa, r1, t1, f2, g2):
        @pl.when(k < 2)
        def _():
            f2[...] = f1[...]

        @pl.when((k == 2) | (k == 3))
        def _():
            came = jnp.where(k == 2, qa_raw[...], qa[...])
            g = summed(product(came, r1[...]), fa[...], True)
            g2[...] = g
            f2[...] = product(t1[...], g)

    (f2, g2) = staged(second_fields, stride, [f1, qa_raw, qa, fa, r1, t1], [field, field], 2)

    def third_fields(k, r_late, r_next, w_came, q1, t1, both, r1, qa_raw, qa, fa, w4, g4, rc4):
        @pl.when((k == 2) | (k == 3))
        def _():
            came = jnp.where(k == 2, r_late[...], r_next[...]) + w_came[...]
            gt = summed(product(q1[...], came), t1[...], True)
            rc = r1[...] + product(both[:, : q1.shape[1]], product(came, gt))
            rc4[...] = rc
            g = summed(product(jnp.where(k == 2, qa_raw[...], qa[...]), rc), fa[...], True)
            g4[...] = g
            w4[...] = product(gt, g)

    (w4, g4, rc4) = staged(
        third_fields,
        stride,
        [r_late, r_next, w_came, q1, t1, both, r1, qa_raw, qa, fa],
        [field, field, square],
        9,
    )
    w4_came = moved(w4, [(2, 4), (3, 5)])

    def second_through(k, t, gt_came, gt2_came, t2):
        @pl.when(k > 5)
        def _():
            t2[...] = product(product(t[...], gt_came[...]), gt2_came[...])

    (t2,) = staged(second_through, stride, [t, gt_came, gt2_came], [square], 2)

    def last_fields(k, r_late, r_next, total_came, q2, f2, g6):
        @pl.when((k == 2) | (k == 3))
        def _():
            rc = jnp.where(k == 2, r_late[...], r_next[...]) + total_came[...]
            g6[...] = summed(product(q2[...], rc), f2[...])

    (g6,) = staged(last_fields, stride, [r_late, r_next, total_came, q2, f2], [field], 3)
    g6_odd = moved(g6, [(2, 6), (3, 7)], 1, 2)
    g6_even = moved(g6, [(2, 6), (3, 7)], 0, 2)

    def passed(value, choose):
        pairs = [(i, i + 1) for i in range(length - 1) if choose(i)]
        return lax.ppermute(value, "sec", pairs)

    half = NODES // 2 * stride
    next_low = passed(f2, lambda i: i < half)

    def all_reflected(
        k, ua, r1, g2, rc4, g4, r_late, r_next, total_came, g6, hu2, s2, s4, s6
    ):
        @pl.when((k == 2) | (k == 3))
        def _():
            rc = jnp.where(k == 2, r_late[...], r_next[...]) + total_came[...]
            rg2 = product(r1[...], g2[...])
            rg4 = product(rc4[...], g4[...])
            sums = rg2 + product(hu2[...], product(rc, g6[...]))
            value = product(ua[:, : hu2.shape[1]], jnp.concatenate([rg2, rg4, sums], axis=1))
            for i, out in enumerate((s2, s4, s6)):
                out[...] = ua[:, hu2.shape[1] :] + value[:, i * width : (i + 1) * width]

    (s2, s4, s6) = staged(
        all_reflected,
        stride,
        [ua, r1, g2, rc4, g4, r_late, r_next, total_came, g6, hu2],
        [field] * 3,
        3,
    )
    s6_came = moved(s6, [(2, 6), (3, 7)])
    s4_came = moved(s4, [(2, 4), (3, 5)])

    def through_odd(d, f2, t1, w4, t2, g6, out):
        k = d // stride

        @pl.when(k < 4)
        def _():
            out[...] = f2[...]

        @pl.when((k == 4) | (k == 5))
        def _():
            out[...] = product(t1[...], w4[...])

        @pl.when((k > 5) & (d % 2 == 1))
        def _():
            out[...] = product(t2[...], g6[...])

    (odd,) = staged(through_odd, 1, [f2, t1, w4_came, t2, g6_odd], [field], 1)
    next_odd = passed(odd, lambda i: i >= half and i % 2 == 1)

    def through_even(d, odd, t2, g6, out):
        k = d // stride
        late = (k > 5) & (d % 2 == 0)

        @pl.when(late)
        def _():
            out[...] = product(t2[...], g6[...])

        @pl.when(jnp.logical_not(late))
        def _():
            out[...] = odd[...]

    (through_field,) = staged(through_even, 1, [odd, t2, g6_even], [field], 1)
    next_even = passed(through_field, lambda i: i >= half and i % 2 == 0)

    def depths(d, maps, low, odd, even, incident, out):
        came = jnp.where(d % 2 == 1, even[...], odd[...])
        came = jnp.where(d <= half, low[...], came)
        value = right(jnp.where(d == 0, incident[...], came))
        for j in range(depth_maps.shape[1]):
            out[j] = jnp.dot(left(maps[j]), value, preferred_element_type=F32)

    (depth_fields,) = staged(
        depths,
        1,
        [maps, next_low, next_odd, next_even, incident],
        [depth_maps.shape[1:3] + field[1:]],
        1,
    )

    def reflected_out(k, both, s2, s4, s6, out):
        @pl.when(k < 2)
        def _():
            out[...] = both[:, square[1] :]

        @pl.when((k == 2) | (k == 3))
        def _():
            out[...] = s2[...]

        @pl.when((k == 4) | (k == 5))
        def _():
            out[...] = s4[...]

        @pl.when(k > 5)
        def _():
            out[...] = s6[...]

    (reflected,) = staged(reflected_out, stride, [both, s2, s4_came, s6_came], [field], 0.1)
    return (through_field[None], reflected[None], depth_fields[None])


def solution(mesh):
    in_specs = (
        P("sec", None, None),
        P("sec", None, None),
        P("sec", None, None),
        P("sec", None, None),
        P("sec", None, None, None),
        P(),
    )
    out_specs = (P("sec", None, None), P("sec", None, None), P("sec", None, None, None))

    return jax.shard_map(
        per_device, mesh=mesh, in_specs=in_specs, out_specs=out_specs, check_vma=False
    )
```

```python
import jax
import jax.numpy as jnp
from jax import lax
from jax.experimental import pallas as pl
from jax.experimental.pallas import tpu as pltpu
from jax.sharding import PartitionSpec as P

SEGMENTS = 3
NODES = 2**SEGMENTS
F32 = jnp.float32


def split(value):
    high = value.astype(jnp.bfloat16)
    return high, (value - high.astype(F32)).astype(jnp.bfloat16)


def left(value):
    high, low = split(value)
    return jnp.concatenate([high, high, low], axis=1)


def right(value):
    high, low = split(value)
    return jnp.concatenate([high, low, high], axis=0)


def product(former, latter):
    return jnp.dot(left(former), right(latter), preferred_element_type=F32)


def summed(bounce, value):
    side = bounce.shape[1]
    both = product(bounce, jnp.concatenate([bounce, value], axis=1))
    total = value + both[:, side:]
    return total + product(both[:, :side], total)


def rolled_sum(bounce, value):
    factor = left(bounce)

    def step(_, total):
        return value + jnp.dot(factor, right(total), preferred_element_type=F32)

    return lax.fori_loop(0, 3, step, value)


def staged(body, stride, inputs, outputs, products, dtype=F32):
    def kernel(*refs):
        body(lax.axis_index("sec") // stride, *refs)

    vmem = pl.BlockSpec(memory_space=pltpu.VMEM)
    side = inputs[0].shape[-1]
    moved_bytes = 4 * side * side * (len(inputs) + len(outputs))
    return pl.pallas_call(
        kernel,
        out_shape=[jax.ShapeDtypeStruct(shape, dtype) for shape in outputs],
        in_specs=[vmem] * len(inputs),
        out_specs=[vmem] * len(outputs),
        compiler_params=pltpu.CompilerParams(vmem_limit_bytes=24 * 2**20),
        cost_estimate=pl.CostEstimate(
            flops=int(products * 6 * side**3), bytes_accessed=moved_bytes, transcendentals=0
        ),
    )(*inputs)


def per_device(front_reflect, front_through, back_reflect, back_through, depth_maps, incident):
    length = lax.axis_size("sec")
    stride = length // NODES
    square, field = front_reflect.shape[1:], incident.shape

    def moved(value, routes, start=0, step=1):
        pairs = [
            (a * stride + i, b * stride + i)
            for a, b in routes
            for i in range(start, stride, step)
        ]
        return lax.ppermute(value, "sec", pairs)

    r, t, q, u = front_reflect[0], front_through[0], back_reflect[0], back_through[0]
    width = field[1]
    fields = (field[0], 2 * width)
    low = [(0, 2), (1, 3)]
    back = [(4, 2), (5, 3)]
    middle = [(2, 3), (3, 4), (4, 5)]

    swapped = moved(r, [(7, 6), (6, 7), (1, 0)])
    r2_down = moved(r, [(2, 0)])
    q0 = moved(q, [(0, 1), (1, 2)] + middle)
    t0 = moved(t, [(1, 2)] + middle)
    u1_over = moved(u, [(1, 0)])
    u0 = moved(u, [(3, 4), (4, 5)])
    u0_low = moved(u, [(0, 1), (2, 3)])
    qa_raw = moved(q, [(0, 2)])
    r_late = moved(r, [(3, 2)])
    r_next = moved(r, [(4, 3)])

    def load(k, r, t, q, u, incident, *out):
        for i, ref in enumerate((r, t, q, u)):
            out[i][...] = ref[...]

        @pl.when(k == 0)
        def _():
            value = right(incident[...])
            out[4][:, :width] = jnp.dot(left(t[...]), value, preferred_element_type=F32)
            out[4][:, width:] = jnp.dot(left(r[...]), value, preferred_element_type=F32)

    r, t, q, u, first = staged(load, stride, [r, t, q, u, incident], [square] * 4 + [fields], 1)
    first_came = moved(first, [(0, 1)])

    def pair_reflect(at):
        def body(k, came, r, t, q, u, *rest):
            out, gt_out = rest[-2:]

            @pl.when(k == at)
            def _():
                gt = rolled_sum(product(q[...], came[...]), t[...])
                gt_out[...] = gt
                out[...] = r[...] + product(u[...], product(came[...], gt))

            @pl.when(k != at)
            def _():
                out[...] = came[...]
                if len(rest) == 3:
                    gt_out[...] = rest[0][...]

        return body

    (relay, gt) = staged(pair_reflect(6), stride, [swapped, r, t, q, u], [square] * 2, 6)
    hopped = moved(relay, [(6, 7), (7, 5), (0, 2)])
    r2_over = moved(r2_down, [(0, 1)])
    u1_up = moved(u1_over, [(0, 2)])
    r2_up = moved(r2_over, [(1, 3)])

    def forward_q(k, q0, r, t, q, u, q1, hu_out):
        @pl.when(k == 0)
        def _():
            q1[...] = q[...]

        @pl.when((k > 0) & (k < 6))
        def _():
            hu = rolled_sum(product(r[...], q0[...]), u[...])
            hu_out[...] = hu
            q1[...] = q[...] + product(t[...], product(q0[...], hu))

    (q1, hu) = staged(forward_q, stride, [q0, r, t, q, u], [square] * 2, 6)
    qa = moved(q1, [(1, 3)])

    maps = depth_maps[0]

    def forward_t(k, q0, t0, r, t, t1, rgt):
        @pl.when((k > 1) & (k < 6))
        def _():
            gt = rolled_sum(product(q0[...], r[...]), t0[...])
            rgt[...] = product(r[...], gt)
            t1[...] = product(t[...], gt)

    (t1, rgt) = staged(forward_t, stride, [q0, t0, r, t], [square] * 2, 6)

    (relay, gt) = staged(pair_reflect(5), stride, [hopped, r, t, q, u, gt], [square] * 2, 6)
    bounced = moved(relay, [(5, 4), (7, 5)])
    gt_came = moved(gt, [(5, 6), (6, 7)])

    def forward_u(k, u0, hu, rgt, u1, w):
        @pl.when((k == 4) | (k == 5))
        def _():
            factor = left(u0[...])
            w[...] = jnp.dot(factor, right(rgt[...]), preferred_element_type=F32)
            u1[...] = jnp.dot(factor, right(hu[...]), preferred_element_type=F32)

    (u1, w) = staged(forward_u, stride, [u0, hu, rgt], [square] * 2, 2)
    w_came = moved(w, back)

    def low_fields(k, first, came, q0, r, t, f1, rg):
        @pl.when(k == 0)
        def _():
            f1[...] = first[:, :width]

        @pl.when(k == 1)
        def _():
            g = rolled_sum(product(q0[...], r[...]), came[:, :width])
            f1[...] = product(t[...], g)
            rg[...] = product(r[...], g)

    (f1, rg) = staged(low_fields, stride, [first, first_came, q0, r, t], [field] * 2, 2)
    fa = moved(f1, low)

    def second_reflect(k, bounced, q1, t1, u1, w, total, gt_out):
        @pl.when((k == 4) | (k == 5))
        def _():
            gt = summed(product(q1[...], bounced[...]), t1[...])
            gt_out[...] = gt
            total[...] = w[...] + product(u1[...], product(bounced[...], gt))

    (total, gt2) = staged(second_reflect, stride, [bounced, q1, t1, u1, w], [square] * 2, 6
    )
    total_came = moved(total, back)
    gt2_came = moved(gt2, [(4, 6), (5, 7)])

    def low_u(k, u0, u1_up, u, hu, rgt, rg, first, came, both, w):
        side = u.shape[1]

        @pl.when(k == 0)
        def _():
            both[:, :side] = u[...]
            both[:, side:] = first[:, width:]

        @pl.when((k > 0) & (k < 4))
        def _():
            factor = left(jnp.where(k == 2, u1_up[...], u0[...]))
            both[:, :side] = jnp.dot(factor, right(hu[...]), preferred_element_type=F32)

            @pl.when(k == 1)
            def _():
                both[:, side:] = came[:, width:] + jnp.dot(
                    factor, right(rg[...]), preferred_element_type=F32
                )

            @pl.when(k > 1)
            def _():
                w[...] = jnp.dot(factor, right(rgt[...]), preferred_element_type=F32)

    (both, w_low) = staged(
        low_u,
        stride,
        [u0_low, u1_up, u, hu, rgt, rg, first, first_came],
        [(square[0], square[1] + width), square],
        2,
    )
    ua = moved(both, low)

    def own_fields(k, r2_up, hopped, w, r1):
        @pl.when(k == 2)
        def _():
            r1[...] = hopped[...] + w[...]

        @pl.when(k == 3)
        def _():
            r1[...] = r2_up[...] + w[...]

    (r1,) = staged(own_fields, stride, [r2_up, hopped, w_low], [square], 0.1)

    def second_q(k, r1, qa_raw, qa, q1, t1, both, q2, hu_out):
        @pl.when((k == 2) | (k == 3))
        def _():
            came = jnp.where(k == 2, qa_raw[...], qa[...])
            hu = summed(product(r1[...], came), both[:, : q1.shape[1]])
            hu_out[...] = hu
            q2[...] = q1[...] + product(t1[...], product(came, hu))

    (q2, hu2) = staged(second_q, stride, [r1, qa_raw, qa, q1, t1, both], [square] * 2, 6)

    def second_fields(k, f1, qa_raw, qa, fa, r1, t1, f2, g2):
        @pl.when(k < 2)
        def _():
            f2[...] = f1[...]

        @pl.when((k == 2) | (k == 3))
        def _():
            came = jnp.where(k == 2, qa_raw[...], qa[...])
            g = summed(product(came, r1[...]), fa[...])
            g2[...] = g
            f2[...] = product(t1[...], g)

    (f2, g2) = staged(second_fields, stride, [f1, qa_raw, qa, fa, r1, t1], [field, field], 2)

    def third_fields(k, r_late, r_next, w_came, q1, t1, both, r1, qa_raw, qa, fa, w4, g4, rc4):
        @pl.when((k == 2) | (k == 3))
        def _():
            came = jnp.where(k == 2, r_late[...], r_next[...]) + w_came[...]
            gt = summed(product(q1[...], came), t1[...])
            rc = r1[...] + product(both[:, : q1.shape[1]], product(came, gt))
            rc4[...] = rc
            g = summed(product(jnp.where(k == 2, qa_raw[...], qa[...]), rc), fa[...])
            g4[...] = g
            w4[...] = product(gt, g)

    (w4, g4, rc4) = staged(
        third_fields,
        stride,
        [r_late, r_next, w_came, q1, t1, both, r1, qa_raw, qa, fa],
        [field, field, square],
        9,
    )
    w4_came = moved(w4, [(2, 4), (3, 5)])

    def second_through(k, t, gt_came, gt2_came, t2):
        @pl.when(k > 5)
        def _():
            t2[...] = product(product(t[...], gt_came[...]), gt2_came[...])

    (t2,) = staged(second_through, stride, [t, gt_came, gt2_came], [square], 2)

    def last_fields(k, r_late, r_next, total_came, q2, f2, g6):
        @pl.when((k == 2) | (k == 3))
        def _():
            rc = jnp.where(k == 2, r_late[...], r_next[...]) + total_came[...]
            g6[...] = summed(product(q2[...], rc), f2[...])

    (g6,) = staged(last_fields, stride, [r_late, r_next, total_came, q2, f2], [field], 3)
    g6_odd = moved(g6, [(2, 6), (3, 7)], 1, 2)
    g6_even = moved(g6, [(2, 6), (3, 7)], 0, 2)

    def passed(value, choose):
        pairs = [(i, i + 1) for i in range(length - 1) if choose(i)]
        return lax.ppermute(value, "sec", pairs)

    half = NODES // 2 * stride
    next_low = passed(f2, lambda i: i < half)

    def all_reflected(
        k, ua, r1, g2, rc4, g4, r_late, r_next, total_came, g6, hu2, s2, s4, s6
    ):
        @pl.when((k == 2) | (k == 3))
        def _():
            rc = jnp.where(k == 2, r_late[...], r_next[...]) + total_came[...]
            rg2 = product(r1[...], g2[...])
            rg4 = product(rc4[...], g4[...])
            sums = rg2 + product(hu2[...], product(rc, g6[...]))
            value = product(ua[:, : hu2.shape[1]], jnp.concatenate([rg2, rg4, sums], axis=1))
            for i, out in enumerate((s2, s4, s6)):
                out[...] = ua[:, hu2.shape[1] :] + value[:, i * width : (i + 1) * width]

    (s2, s4, s6) = staged(
        all_reflected,
        stride,
        [ua, r1, g2, rc4, g4, r_late, r_next, total_came, g6, hu2],
        [field] * 3,
        3,
    )
    s6_came = moved(s6, [(2, 6), (3, 7)])
    s4_came = moved(s4, [(2, 4), (3, 5)])

    def through_mid(k, f2, t1, w4, out):
        @pl.when(k < 4)
        def _():
            out[...] = f2[...]

        @pl.when((k == 4) | (k == 5))
        def _():
            out[...] = product(t1[...], w4[...])

    (mid,) = staged(through_mid, stride, [f2, t1, w4_came], [field], 0.3)
    top = half + half // 2
    next_mid = passed(mid, lambda i: half <= i < top)

    def through_odd(d, mid, t2, g6, out):
        late = (d >= top) & (d % 2 == 1)

        @pl.when(late)
        def _():
            out[...] = product(t2[...], g6[...])

        @pl.when(jnp.logical_not(late))
        def _():
            out[...] = mid[...]

    (odd,) = staged(through_odd, 1, [mid, t2, g6_odd], [field], 0.3)
    next_odd = passed(odd, lambda i: i >= top and i % 2 == 1)

    def through_even(d, odd, t2, g6, out):
        late = (d >= top) & (d % 2 == 0)

        @pl.when(late)
        def _():
            out[...] = product(t2[...], g6[...])

        @pl.when(jnp.logical_not(late))
        def _():
            out[...] = odd[...]

    (through_field,) = staged(through_even, 1, [odd, t2, g6_even], [field], 0.3)
    next_even = passed(through_field, lambda i: i >= top and i % 2 == 0)

    def depths(d, maps, low, mid, odd, even, incident, out):
        came = jnp.where(d % 2 == 1, even[...], odd[...])
        came = jnp.where(d <= top, mid[...], came)
        came = jnp.where(d <= half, low[...], came)
        value = right(jnp.where(d == 0, incident[...], came))
        for j in range(depth_maps.shape[1]):
            out[j] = jnp.dot(left(maps[j]), value, preferred_element_type=F32)

    (depth_fields,) = staged(
        depths,
        1,
        [maps, next_low, next_mid, next_odd, next_even, incident],
        [depth_maps.shape[1:3] + field[1:]],
        1,
    )

    def reflected_out(k, both, s2, s4, s6, out):
        @pl.when(k < 2)
        def _():
            out[...] = both[:, square[1] :]

        @pl.when((k == 2) | (k == 3))
        def _():
            out[...] = s2[...]

        @pl.when((k == 4) | (k == 5))
        def _():
            out[...] = s4[...]

        @pl.when(k > 5)
        def _():
            out[...] = s6[...]

    (reflected,) = staged(reflected_out, stride, [both, s2, s4_came, s6_came], [field], 0.1)
    return (through_field[None], reflected[None], depth_fields[None])


def solution(mesh):
    in_specs = (
        P("sec", None, None),
        P("sec", None, None),
        P("sec", None, None),
        P("sec", None, None),
        P("sec", None, None, None),
        P(),
    )
    out_specs = (P("sec", None, None), P("sec", None, None), P("sec", None, None, None))

    return jax.shard_map(
        per_device, mesh=mesh, in_specs=in_specs, out_specs=out_specs, check_vma=False
    )
```

```python
import jax
import jax.numpy as jnp
from jax import lax
from jax.experimental import pallas as pl
from jax.experimental.pallas import tpu as pltpu
from jax.sharding import PartitionSpec as P

SEGMENTS = 3
NODES = 2**SEGMENTS
F32 = jnp.float32


def split(value):
    high = value.astype(jnp.bfloat16)
    return high, (value - high.astype(F32)).astype(jnp.bfloat16)


def left(value):
    high, low = split(value)
    return jnp.concatenate([high, high, low], axis=1)


def right(value):
    high, low = split(value)
    return jnp.concatenate([high, low, high], axis=0)


def product(former, latter):
    return jnp.dot(left(former), right(latter), preferred_element_type=F32)


def summed(bounce, value):
    side = bounce.shape[1]
    both = product(bounce, jnp.concatenate([bounce, value], axis=1))
    total = value + both[:, side:]
    return total + product(both[:, :side], total)


def rolled_sum(bounce, value):
    factor = left(bounce)

    def step(_, total):
        return value + jnp.dot(factor, right(total), preferred_element_type=F32)

    return lax.fori_loop(0, 3, step, value)


def staged(body, stride, inputs, outputs, products, dtype=F32):
    def kernel(*refs):
        body(lax.axis_index("sec") // stride, *refs)

    vmem = pl.BlockSpec(memory_space=pltpu.VMEM)
    side = inputs[0].shape[-1]
    moved_bytes = 4 * side * side * (len(inputs) + len(outputs))
    return pl.pallas_call(
        kernel,
        out_shape=[jax.ShapeDtypeStruct(shape, dtype) for shape in outputs],
        in_specs=[vmem] * len(inputs),
        out_specs=[vmem] * len(outputs),
        compiler_params=pltpu.CompilerParams(vmem_limit_bytes=24 * 2**20),
        cost_estimate=pl.CostEstimate(
            flops=int(products * 6 * side**3), bytes_accessed=moved_bytes, transcendentals=0
        ),
    )(*inputs)


def per_device(front_reflect, front_through, back_reflect, back_through, depth_maps, incident):
    length = lax.axis_size("sec")
    stride = length // NODES
    square, field = front_reflect.shape[1:], incident.shape

    def moved(value, routes, start=0, step=1):
        pairs = [
            (a * stride + i, b * stride + i)
            for a, b in routes
            for i in range(start, stride, step)
        ]
        return lax.ppermute(value, "sec", pairs)

    r, t, q, u = front_reflect[0], front_through[0], back_reflect[0], back_through[0]
    width = field[1]
    fields = (field[0], 2 * width)
    low = [(0, 2), (1, 3)]
    back = [(4, 2), (5, 3)]
    middle = [(2, 3), (3, 4), (4, 5)]

    swapped = moved(r, [(7, 6), (6, 7), (1, 0)])
    r2_down = moved(r, [(2, 0)])
    q0 = moved(q, [(0, 1), (1, 2)] + middle)
    t0 = moved(t, [(1, 2)] + middle)
    u1_over = moved(u, [(1, 0)])
    u0 = moved(u, [(3, 4), (4, 5)])
    u0_low = moved(u, [(0, 1), (2, 3)])
    qa_raw = moved(q, [(0, 2)])
    r_late = moved(r, [(3, 2)])
    r_next = moved(r, [(4, 3)])

    def load(k, r, t, q, u, incident, *out):
        for i, ref in enumerate((r, t, q, u)):
            out[i][...] = ref[...]

        @pl.when(k == 0)
        def _():
            value = right(incident[...])
            out[4][:, :width] = jnp.dot(left(t[...]), value, preferred_element_type=F32)
            out[4][:, width:] = jnp.dot(left(r[...]), value, preferred_element_type=F32)

    r, t, q, u, first = staged(load, stride, [r, t, q, u, incident], [square] * 4 + [fields], 1)
    first_came = moved(first, [(0, 1)])

    def pair_reflect(at):
        def body(k, came, r, t, q, u, *rest):
            out, gt_out = rest[-2:]

            @pl.when(k == at)
            def _():
                gt = rolled_sum(product(q[...], came[...]), t[...])
                gt_out[...] = gt
                out[...] = r[...] + product(u[...], product(came[...], gt))

            @pl.when(k != at)
            def _():
                out[...] = came[...]
                if len(rest) == 3:
                    gt_out[...] = rest[0][...]

        return body

    (relay, gt) = staged(pair_reflect(6), stride, [swapped, r, t, q, u], [square] * 2, 6)
    hopped = moved(relay, [(6, 7), (7, 5), (0, 2)])
    r2_over = moved(r2_down, [(0, 1)])
    u1_up = moved(u1_over, [(0, 2)])
    r2_up = moved(r2_over, [(1, 3)])

    def forward_q(k, q0, r, t, q, u, q1, hu_out):
        @pl.when(k == 0)
        def _():
            q1[...] = q[...]

        @pl.when((k > 0) & (k < 6))
        def _():
            hu = rolled_sum(product(r[...], q0[...]), u[...])
            hu_out[...] = hu
            q1[...] = q[...] + product(t[...], product(q0[...], hu))

    (q1, hu) = staged(forward_q, stride, [q0, r, t, q, u], [square] * 2, 6)
    qa = moved(q1, [(1, 3)])

    maps = depth_maps[0]

    def forward_t(k, q0, t0, r, t, t1, rgt):
        @pl.when((k > 1) & (k < 6))
        def _():
            gt = rolled_sum(product(q0[...], r[...]), t0[...])
            rgt[...] = product(r[...], gt)
            t1[...] = product(t[...], gt)

    (t1, rgt) = staged(forward_t, stride, [q0, t0, r, t], [square] * 2, 6)

    (relay, gt) = staged(pair_reflect(5), stride, [hopped, r, t, q, u, gt], [square] * 2, 6)
    bounced = moved(relay, [(5, 4), (7, 5)])
    gt_came = moved(gt, [(5, 6), (6, 7)])

    def forward_u(k, u0, hu, rgt, u1, w):
        @pl.when((k == 4) | (k == 5))
        def _():
            factor = left(u0[...])
            w[...] = jnp.dot(factor, right(rgt[...]), preferred_element_type=F32)
            u1[...] = jnp.dot(factor, right(hu[...]), preferred_element_type=F32)

    (u1, w) = staged(forward_u, stride, [u0, hu, rgt], [square] * 2, 2)
    w_came = moved(w, back)

    def low_fields(k, first, came, q0, r, t, f1, rg):
        @pl.when(k == 0)
        def _():
            f1[...] = first[:, :width]

        @pl.when(k == 1)
        def _():
            g = rolled_sum(product(q0[...], r[...]), came[:, :width])
            f1[...] = product(t[...], g)
            rg[...] = product(r[...], g)

    (f1, rg) = staged(low_fields, stride, [first, first_came, q0, r, t], [field] * 2, 2)
    fa = moved(f1, low)

    cut = square[1] // 3 * 2

    def second_reflect(k, bounced, q1, t1, u1, w, total, gt_out, bounce_out, twice_out):
        side = q1.shape[1]

        @pl.when((k == 4) | (k == 5))
        def _():
            bounce = product(q1[...], bounced[...])
            both = product(bounce, jnp.concatenate([bounce, t1[:, :cut]], axis=1))
            start = t1[:, :cut] + both[:, side:]
            gt = start + product(both[:, :side], start)
            total[...] = w[:, :cut] + product(u1[...], product(bounced[...], gt))
            gt_out[...] = gt
            bounce_out[...] = bounce
            twice_out[...] = both[:, :side]

    (total, gt_cut, bounce, twice) = staged(
        second_reflect, stride, [bounced, q1, t1, u1, w], [(square[0], cut)] * 2 + [square] * 2, 4
    )
    total_came = moved(total, back)

    def second_rest(k, bounced, bounce, twice, t1, u1, w, gt_cut, total, gt_out):
        @pl.when((k == 4) | (k == 5))
        def _():
            start = t1[:, cut:] + product(bounce[...], t1[:, cut:])
            gt = start + product(twice[...], start)
            total[...] = w[:, cut:] + product(u1[...], product(bounced[...], gt))
            gt_out[:, :cut] = gt_cut[...]
            gt_out[:, cut:] = gt

    (total_s, gt2) = staged(
        second_rest,
        stride,
        [bounced, bounce, twice, t1, u1, w, gt_cut],
        [(square[0], square[1] - cut), square],
        2,
    )
    total_s_came = moved(total_s, back)
    gt2_came = moved(gt2, [(4, 6), (5, 7)])

    def low_u(k, u0, u1_up, u, hu, rgt, rg, first, came, both, w):
        side = u.shape[1]

        @pl.when(k == 0)
        def _():
            both[:, :side] = u[...]
            both[:, side:] = first[:, width:]

        @pl.when((k > 0) & (k < 4))
        def _():
            factor = left(jnp.where(k == 2, u1_up[...], u0[...]))
            both[:, :side] = jnp.dot(factor, right(hu[...]), preferred_element_type=F32)

            @pl.when(k == 1)
            def _():
                both[:, side:] = came[:, width:] + jnp.dot(
                    factor, right(rg[...]), preferred_element_type=F32
                )

            @pl.when(k > 1)
            def _():
                w[...] = jnp.dot(factor, right(rgt[...]), preferred_element_type=F32)

    (both, w_low) = staged(
        low_u,
        stride,
        [u0_low, u1_up, u, hu, rgt, rg, first, first_came],
        [(square[0], square[1] + width), square],
        2,
    )
    ua = moved(both, low)

    def own_fields(k, r2_up, hopped, w, r1):
        @pl.when(k == 2)
        def _():
            r1[...] = hopped[...] + w[...]

        @pl.when(k == 3)
        def _():
            r1[...] = r2_up[...] + w[...]

    (r1,) = staged(own_fields, stride, [r2_up, hopped, w_low], [square], 0.1)

    def second_q(k, r1, qa_raw, qa, q1, t1, both, q2, hu_out):
        @pl.when((k == 2) | (k == 3))
        def _():
            came = jnp.where(k == 2, qa_raw[...], qa[...])
            hu = summed(product(r1[...], came), both[:, : q1.shape[1]])
            hu_out[...] = hu
            q2[...] = q1[...] + product(t1[...], product(came, hu))

    (q2, hu2) = staged(second_q, stride, [r1, qa_raw, qa, q1, t1, both], [square] * 2, 6)

    def second_fields(k, f1, qa_raw, qa, fa, r1, t1, f2, g2):
        @pl.when(k < 2)
        def _():
            f2[...] = f1[...]

        @pl.when((k == 2) | (k == 3))
        def _():
            came = jnp.where(k == 2, qa_raw[...], qa[...])
            g = summed(product(came, r1[...]), fa[...])
            g2[...] = g
            f2[...] = product(t1[...], g)

    (f2, g2) = staged(second_fields, stride, [f1, qa_raw, qa, fa, r1, t1], [field, field], 2)

    def third_fields(k, r_late, r_next, w_came, q1, t1, both, r1, qa_raw, qa, fa, w4, g4, rc4):
        @pl.when((k == 2) | (k == 3))
        def _():
            came = jnp.where(k == 2, r_late[...], r_next[...]) + w_came[...]
            gt = summed(product(q1[...], came), t1[...])
            rc = r1[...] + product(both[:, : q1.shape[1]], product(came, gt))
            rc4[...] = rc
            g = summed(product(jnp.where(k == 2, qa_raw[...], qa[...]), rc), fa[...])
            g4[...] = g
            w4[...] = product(gt, g)

    (w4, g4, rc4) = staged(
        third_fields,
        stride,
        [r_late, r_next, w_came, q1, t1, both, r1, qa_raw, qa, fa],
        [field, field, square],
        9,
    )
    w4_came = moved(w4, [(2, 4), (3, 5)])

    def second_through(k, t, gt_came, gt2_came, t2):
        @pl.when(k > 5)
        def _():
            t2[...] = product(product(t[...], gt_came[...]), gt2_came[...])

    (t2,) = staged(second_through, stride, [t, gt_came, gt2_came], [square], 2)

    def last_fields(k, r_late, r_next, total_came, total_s_came, q2, f2, g6):
        @pl.when((k == 2) | (k == 3))
        def _():
            whole = jnp.concatenate([total_came[...], total_s_came[...]], axis=1)
            rc = jnp.where(k == 2, r_late[...], r_next[...]) + whole
            g6[...] = summed(product(q2[...], rc), f2[...])

    (g6,) = staged(last_fields, stride, [r_late, r_next, total_came, total_s_came, q2, f2], [field], 3)
    g6_odd = moved(g6, [(2, 6), (3, 7)], 1, 2)
    g6_even = moved(g6, [(2, 6), (3, 7)], 0, 2)

    def passed(value, choose):
        pairs = [(i, i + 1) for i in range(length - 1) if choose(i)]
        return lax.ppermute(value, "sec", pairs)

    half = NODES // 2 * stride
    next_low = passed(f2, lambda i: i < half)

    def all_reflected(
        k, ua, r1, g2, rc4, g4, r_late, r_next, total_came, total_s_came, g6, hu2, s2, s4, s6
    ):
        @pl.when((k == 2) | (k == 3))
        def _():
            whole = jnp.concatenate([total_came[...], total_s_came[...]], axis=1)
            rc = jnp.where(k == 2, r_late[...], r_next[...]) + whole
            rg2 = product(r1[...], g2[...])
            rg4 = product(rc4[...], g4[...])
            sums = rg2 + product(hu2[...], product(rc, g6[...]))
            value = product(ua[:, : hu2.shape[1]], jnp.concatenate([rg2, rg4, sums], axis=1))
            for i, out in enumerate((s2, s4, s6)):
                out[...] = ua[:, hu2.shape[1] :] + value[:, i * width : (i + 1) * width]

    (s2, s4, s6) = staged(
        all_reflected,
        stride,
        [ua, r1, g2, rc4, g4, r_late, r_next, total_came, total_s_came, g6, hu2],
        [field] * 3,
        3,
    )
    s6_came = moved(s6, [(2, 6), (3, 7)])
    s4_came = moved(s4, [(2, 4), (3, 5)])

    def through_mid(k, f2, t1, w4, out):
        @pl.when(k < 4)
        def _():
            out[...] = f2[...]

        @pl.when((k == 4) | (k == 5))
        def _():
            out[...] = product(t1[...], w4[...])

    (mid,) = staged(through_mid, stride, [f2, t1, w4_came], [field], 0.3)
    top = half + half // 2
    next_mid = passed(mid, lambda i: half <= i < top)

    def through_odd(d, mid, t2, g6, out):
        late = (d >= top) & (d % 2 == 1)

        @pl.when(late)
        def _():
            out[...] = product(t2[...], g6[...])

        @pl.when(jnp.logical_not(late))
        def _():
            out[...] = mid[...]

    (odd,) = staged(through_odd, 1, [mid, t2, g6_odd], [field], 0.3)
    next_odd = passed(odd, lambda i: i >= top and i % 2 == 1)

    def through_even(d, odd, t2, g6, out):
        late = (d >= top) & (d % 2 == 0)

        @pl.when(late)
        def _():
            out[...] = product(t2[...], g6[...])

        @pl.when(jnp.logical_not(late))
        def _():
            out[...] = odd[...]

    (through_field,) = staged(through_even, 1, [odd, t2, g6_even], [field], 0.3)
    next_even = passed(through_field, lambda i: i >= top and i % 2 == 0)

    def depths(d, maps, low, mid, odd, even, incident, out):
        came = jnp.where(d % 2 == 1, even[...], odd[...])
        came = jnp.where(d <= top, mid[...], came)
        came = jnp.where(d <= half, low[...], came)
        value = right(jnp.where(d == 0, incident[...], came))
        for j in range(depth_maps.shape[1]):
            out[j] = jnp.dot(left(maps[j]), value, preferred_element_type=F32)

    (depth_fields,) = staged(
        depths,
        1,
        [maps, next_low, next_mid, next_odd, next_even, incident],
        [depth_maps.shape[1:3] + field[1:]],
        1,
    )

    def reflected_out(k, both, s2, s4, s6, out):
        @pl.when(k < 2)
        def _():
            out[...] = both[:, square[1] :]

        @pl.when((k == 2) | (k == 3))
        def _():
            out[...] = s2[...]

        @pl.when((k == 4) | (k == 5))
        def _():
            out[...] = s4[...]

        @pl.when(k > 5)
        def _():
            out[...] = s6[...]

    (reflected,) = staged(reflected_out, stride, [both, s2, s4_came, s6_came], [field], 0.1)
    return (through_field[None], reflected[None], depth_fields[None])


def solution(mesh):
    in_specs = (
        P("sec", None, None),
        P("sec", None, None),
        P("sec", None, None),
        P("sec", None, None),
        P("sec", None, None, None),
        P(),
    )
    out_specs = (P("sec", None, None), P("sec", None, None), P("sec", None, None, None))

    return jax.shard_map(
        per_device, mesh=mesh, in_specs=in_specs, out_specs=out_specs, check_vma=False
    )
```

```python
import jax
import jax.numpy as jnp
from jax import lax
from jax.experimental import pallas as pl
from jax.experimental.pallas import tpu as pltpu
from jax.sharding import PartitionSpec as P

SEGMENTS = 3
NODES = 2**SEGMENTS
F32 = jnp.float32


def split(value):
    high = value.astype(jnp.bfloat16)
    return high, (value - high.astype(F32)).astype(jnp.bfloat16)


def left(value):
    high, low = split(value)
    return jnp.concatenate([high, high, low], axis=1)


def right(value):
    high, low = split(value)
    return jnp.concatenate([high, low, high], axis=0)


def product(former, latter):
    return jnp.dot(left(former), right(latter), preferred_element_type=F32)


def summed(bounce, value):
    side = bounce.shape[1]
    both = product(bounce, jnp.concatenate([bounce, value], axis=1))
    total = value + both[:, side:]
    return total + product(both[:, :side], total)


def rolled_sum(bounce, value):
    factor = left(bounce)

    def step(_, total):
        return value + jnp.dot(factor, right(total), preferred_element_type=F32)

    return lax.fori_loop(0, 3, step, value)


def staged(body, stride, inputs, outputs, products, dtype=F32):
    def kernel(*refs):
        body(lax.axis_index("sec") // stride, *refs)

    vmem = pl.BlockSpec(memory_space=pltpu.VMEM)
    side = inputs[0].shape[-1]
    moved_bytes = 4 * side * side * (len(inputs) + len(outputs))
    return pl.pallas_call(
        kernel,
        out_shape=[jax.ShapeDtypeStruct(shape, dtype) for shape in outputs],
        in_specs=[vmem] * len(inputs),
        out_specs=[vmem] * len(outputs),
        compiler_params=pltpu.CompilerParams(vmem_limit_bytes=24 * 2**20),
        cost_estimate=pl.CostEstimate(
            flops=int(products * 6 * side**3), bytes_accessed=moved_bytes, transcendentals=0
        ),
    )(*inputs)


def per_device(front_reflect, front_through, back_reflect, back_through, depth_maps, incident):
    length = lax.axis_size("sec")
    stride = length // NODES
    square, field = front_reflect.shape[1:], incident.shape

    def moved(value, routes, start=0, step=1):
        pairs = [
            (a * stride + i, b * stride + i)
            for a, b in routes
            for i in range(start, stride, step)
        ]
        return lax.ppermute(value, "sec", pairs)

    r, t, q, u = front_reflect[0], front_through[0], back_reflect[0], back_through[0]
    width = field[1]
    fields = (field[0], 2 * width)
    low = [(0, 2), (1, 3)]
    back = [(4, 2), (5, 3)]
    middle = [(2, 3), (3, 4), (4, 5)]

    swapped = moved(r, [(7, 6), (6, 7), (1, 0)])
    r2_down = moved(r, [(2, 0)])
    q0 = moved(q, [(0, 1), (1, 2)] + middle)
    t0 = moved(t, [(1, 2)] + middle)
    u1_over = moved(u, [(1, 0)])
    u0 = moved(u, [(4, 5)])
    u0_low = moved(u, [(0, 1), (2, 3), (3, 2)])
    qa_raw = moved(q, [(0, 2)])
    r_late = moved(r, [(3, 2)])
    r_next = moved(r, [(4, 3)])

    def load(k, r, t, q, u, incident, *out):
        for i, ref in enumerate((r, t, q, u)):
            out[i][...] = ref[...]

        @pl.when(k == 0)
        def _():
            value = right(incident[...])
            out[4][:, :width] = jnp.dot(left(t[...]), value, preferred_element_type=F32)
            out[4][:, width:] = jnp.dot(left(r[...]), value, preferred_element_type=F32)

    r, t, q, u, first = staged(load, stride, [r, t, q, u, incident], [square] * 4 + [fields], 1)
    first_came = moved(first, [(0, 1)])

    def pair_reflect(at):
        def body(k, came, r, t, q, u, *rest):
            out, gt_out = rest[-2:]

            @pl.when(k == at)
            def _():
                gt = rolled_sum(product(q[...], came[...]), t[...])
                gt_out[...] = gt
                out[...] = r[...] + product(u[...], product(came[...], gt))

            @pl.when(k != at)
            def _():
                if len(rest) == 3:
                    gt_out[...] = rest[0][...]
                else:
                    out[...] = came[...]

        return body

    (relay, gt) = staged(pair_reflect(6), stride, [swapped, r, t, q, u], [square] * 2, 6)
    hopped = moved(relay, [(6, 7), (7, 5), (0, 2)])
    r2_over = moved(r2_down, [(0, 1)])
    u1_up = moved(u1_over, [(0, 2)])
    r2_up = moved(r2_over, [(1, 3)])

    def forward_q(k, q0, r, t, q, u, q1, hu_out):
        @pl.when(k == 0)
        def _():
            q1[...] = q[...]

        @pl.when((k > 0) & (k < 6))
        def _():
            hu = rolled_sum(product(r[...], q0[...]), u[...])
            hu_out[...] = hu
            q1[...] = q[...] + product(t[...], product(q0[...], hu))

    (q1, hu) = staged(forward_q, stride, [q0, r, t, q, u], [square] * 2, 6)
    qa = moved(q1, [(1, 3)])

    maps = depth_maps[0]

    def forward_t(k, q0, t0, r, t, t1, rgt):
        @pl.when((k > 1) & (k < 6))
        def _():
            gt = rolled_sum(product(q0[...], r[...]), t0[...])
            rgt[...] = product(r[...], gt)
            t1[...] = product(t[...], gt)

    (t1, rgt) = staged(forward_t, stride, [q0, t0, r, t], [square] * 2, 6)

    (relay, gt) = staged(pair_reflect(5), stride, [hopped, r, t, q, u, gt], [square] * 2, 6)
    bounced = moved(relay, [(5, 4)])
    bounced_s = moved(hopped, [(7, 5)])
    gt_came = moved(gt, [(5, 6), (6, 7)])

    def forward_u(k, u0, hu, rgt, u1, w):
        @pl.when(k == 4)
        def _():
            w[...] = rgt[...]
            u1[...] = hu[...]

        @pl.when(k == 5)
        def _():
            factor = left(u0[...])
            w[...] = jnp.dot(factor, right(rgt[...]), preferred_element_type=F32)
            u1[...] = jnp.dot(factor, right(hu[...]), preferred_element_type=F32)

    (u1, w) = staged(forward_u, stride, [u0, hu, rgt], [square] * 2, 2)
    w_came = moved(w, back)

    def low_fields(k, first, came, q0, r, t, f1, rg):
        @pl.when(k == 0)
        def _():
            f1[...] = first[:, :width]

        @pl.when(k == 1)
        def _():
            g = rolled_sum(product(q0[...], r[...]), came[:, :width])
            f1[...] = product(t[...], g)
            rg[...] = product(r[...], g)

    (f1, rg) = staged(low_fields, stride, [first, first_came, q0, r, t], [field] * 2, 2)
    fa = moved(f1, low)

    def second_reflect(k, bounced, bounced_s, q1, t1, u1, w, total, gt_out):
        @pl.when((k == 4) | (k == 5))
        def _():
            came = jnp.where(k == 4, bounced[...], bounced_s[...])
            gt = summed(product(q1[...], came), t1[...])
            gt_out[...] = gt
            total[...] = w[...] + product(u1[...], product(came, gt))

    (total, gt2) = staged(second_reflect, stride, [bounced, bounced_s, q1, t1, u1, w], [square] * 2, 6
    )
    total_came = moved(total, back)
    gt2_came = moved(gt2, [(4, 6), (5, 7)])

    def low_u(k, u0, u1_up, u, hu, rgt, rg, first, came, both, w):
        side = u.shape[1]

        @pl.when(k == 0)
        def _():
            both[:, :side] = u[...]
            both[:, side:] = first[:, width:]

        @pl.when((k > 0) & (k < 4))
        def _():
            factor = left(jnp.where(k == 2, u1_up[...], u0[...]))
            both[:, :side] = jnp.dot(factor, right(hu[...]), preferred_element_type=F32)

            @pl.when(k == 1)
            def _():
                both[:, side:] = came[:, width:] + jnp.dot(
                    factor, right(rg[...]), preferred_element_type=F32
                )

            @pl.when(k > 1)
            def _():
                w[...] = jnp.dot(factor, right(rgt[...]), preferred_element_type=F32)

    (both, w_low) = staged(
        low_u,
        stride,
        [u0_low, u1_up, u, hu, rgt, rg, first, first_came],
        [(square[0], square[1] + width), square],
        2,
    )
    ua = moved(both, low)

    def own_fields(k, r2_up, hopped, w, r1):
        @pl.when(k == 2)
        def _():
            r1[...] = hopped[...] + w[...]

        @pl.when(k == 3)
        def _():
            r1[...] = r2_up[...] + w[...]

    (r1,) = staged(own_fields, stride, [r2_up, hopped, w_low], [square], 0.1)

    def second_q(k, r1, qa_raw, qa, q1, t1, both, q2, hu_out):
        @pl.when((k == 2) | (k == 3))
        def _():
            came = jnp.where(k == 2, qa_raw[...], qa[...])
            hu = summed(product(r1[...], came), both[:, : q1.shape[1]])
            hu_out[...] = hu
            q2[...] = q1[...] + product(t1[...], product(came, hu))

    (q2, hu2) = staged(second_q, stride, [r1, qa_raw, qa, q1, t1, both], [square] * 2, 6)

    def second_fields(k, f1, qa_raw, qa, fa, r1, t1, f2, g2):
        @pl.when(k < 2)
        def _():
            f2[...] = f1[...]

        @pl.when((k == 2) | (k == 3))
        def _():
            came = jnp.where(k == 2, qa_raw[...], qa[...])
            g = summed(product(came, r1[...]), fa[...])
            g2[...] = g
            f2[...] = product(t1[...], g)

    (f2, g2) = staged(second_fields, stride, [f1, qa_raw, qa, fa, r1, t1], [field, field], 2)

    def third_fields(k, r_late, r_next, u3, w_came, q1, t1, both, r1, qa_raw, qa, fa, w4, g4, rc4):
        @pl.when(k == 2)
        def _():
            rc4[...] = r_late[...] + product(u3[...], w_came[...])

        @pl.when(k == 3)
        def _():
            rc4[...] = r_next[...] + w_came[...]

        @pl.when((k == 2) | (k == 3))
        def _():
            came = rc4[...]
            gt = summed(product(q1[...], came), t1[...])
            rc = r1[...] + product(both[:, : q1.shape[1]], product(came, gt))
            rc4[...] = rc
            g = summed(product(jnp.where(k == 2, qa_raw[...], qa[...]), rc), fa[...])
            g4[...] = g
            w4[...] = product(gt, g)

    (w4, g4, rc4) = staged(
        third_fields,
        stride,
        [r_late, r_next, u0_low, w_came, q1, t1, both, r1, qa_raw, qa, fa],
        [field, field, square],
        9,
    )
    w4_came = moved(w4, [(2, 4), (3, 5)])

    def second_through(k, t, gt_came, gt2_came, t2):
        @pl.when(k > 5)
        def _():
            t2[...] = product(product(t[...], gt_came[...]), gt2_came[...])

    (t2,) = staged(second_through, stride, [t, gt_came, gt2_came], [square], 2)

    def last_fields(k, r_late, r_next, u3, total_came, q2, f2, g6, rc6):
        @pl.when(k == 2)
        def _():
            rc6[...] = r_late[...] + product(u3[...], total_came[...])

        @pl.when(k == 3)
        def _():
            rc6[...] = r_next[...] + total_came[...]

        @pl.when((k == 2) | (k == 3))
        def _():
            g6[...] = summed(product(q2[...], rc6[...]), f2[...])

    (g6, rc6) = staged(
        last_fields, stride, [r_late, r_next, u0_low, total_came, q2, f2], [field, square], 3
    )
    g6_odd = moved(g6, [(2, 6), (3, 7)], 1, 2)
    g6_even = moved(g6, [(2, 6), (3, 7)], 0, 2)

    def passed(value, choose):
        pairs = [(i, i + 1) for i in range(length - 1) if choose(i)]
        return lax.ppermute(value, "sec", pairs)

    half = NODES // 2 * stride
    next_low = passed(f2, lambda i: i < half)

    def all_reflected(
        k, ua, r1, g2, rc4, g4, rc6, g6, hu2, s2, s4, s6
    ):
        @pl.when((k == 2) | (k == 3))
        def _():
            rg2 = product(r1[...], g2[...])
            rg4 = product(rc4[...], g4[...])
            sums = rg2 + product(hu2[...], product(rc6[...], g6[...]))
            value = product(ua[:, : hu2.shape[1]], jnp.concatenate([rg2, rg4, sums], axis=1))
            for i, out in enumerate((s2, s4, s6)):
                out[...] = ua[:, hu2.shape[1] :] + value[:, i * width : (i + 1) * width]

    (s2, s4, s6) = staged(
        all_reflected, stride, [ua, r1, g2, rc4, g4, rc6, g6, hu2], [field] * 3, 3
    )
    s6_came = moved(s6, [(2, 6), (3, 7)])
    s4_came = moved(s4, [(2, 4), (3, 5)])

    def through_mid(k, f2, t1, w4, out):
        @pl.when(k < 4)
        def _():
            out[...] = f2[...]

        @pl.when((k == 4) | (k == 5))
        def _():
            out[...] = product(t1[...], w4[...])

    (mid,) = staged(through_mid, stride, [f2, t1, w4_came], [field], 0.3)
    top = half + half // 2
    next_mid = passed(mid, lambda i: half <= i < top)

    def through_odd(d, mid, t2, g6, out):
        late = (d >= top) & (d % 2 == 1)

        @pl.when(late)
        def _():
            out[...] = product(t2[...], g6[...])

        @pl.when(jnp.logical_not(late))
        def _():
            out[...] = mid[...]

    (odd,) = staged(through_odd, 1, [mid, t2, g6_odd], [field], 0.3)
    next_odd = passed(odd, lambda i: i >= top and i % 2 == 1)

    def through_even(d, t2, g6, out):
        @pl.when((d >= top) & (d % 2 == 0))
        def _():
            out[...] = product(t2[...], g6[...])

    (even,) = staged(through_even, 1, [t2, g6_even], [field], 0.3)
    next_even = passed(even, lambda i: i >= top and i % 2 == 0)

    def depths(d, maps, low, mid, odd, even, incident, out):
        came = jnp.where(d % 2 == 1, even[...], odd[...])
        came = jnp.where(d <= top, mid[...], came)
        came = jnp.where(d <= half, low[...], came)
        value = right(jnp.where(d == 0, incident[...], came))
        for j in range(depth_maps.shape[1]):
            out[j] = jnp.dot(left(maps[j]), value, preferred_element_type=F32)

    (depth_fields,) = staged(
        depths,
        1,
        [maps, next_low, next_mid, next_odd, next_even, incident],
        [depth_maps.shape[1:3] + field[1:]],
        1,
    )

    def fields_out(d, odd, even, both, s2, s4, s6, through, reflected):
        k = d // stride
        late = (d >= top) & (d % 2 == 0)

        @pl.when(late)
        def _():
            through[...] = even[...]

        @pl.when(jnp.logical_not(late))
        def _():
            through[...] = odd[...]

        @pl.when(k < 2)
        def _():
            reflected[...] = both[:, square[1] :]

        @pl.when((k == 2) | (k == 3))
        def _():
            reflected[...] = s2[...]

        @pl.when((k == 4) | (k == 5))
        def _():
            reflected[...] = s4[...]

        @pl.when(k > 5)
        def _():
            reflected[...] = s6[...]

    (through_field, reflected) = staged(
        fields_out, 1, [odd, even, both, s2, s4_came, s6_came], [field] * 2, 0.1
    )
    return (through_field[None], reflected[None], depth_fields[None])


def solution(mesh):
    in_specs = (
        P("sec", None, None),
        P("sec", None, None),
        P("sec", None, None),
        P("sec", None, None),
        P("sec", None, None, None),
        P(),
    )
    out_specs = (P("sec", None, None), P("sec", None, None), P("sec", None, None, None))

    return jax.shard_map(
        per_device, mesh=mesh, in_specs=in_specs, out_specs=out_specs, check_vma=False
    )
```

```python
import jax
import jax.numpy as jnp
from jax import lax
from jax.experimental import pallas as pl
from jax.experimental.pallas import tpu as pltpu
from jax.sharding import PartitionSpec as P

SEGMENTS = 3
NODES = 2**SEGMENTS
F32 = jnp.float32


def split(value):
    high = value.astype(jnp.bfloat16)
    return high, (value - high.astype(F32)).astype(jnp.bfloat16)


def left(value):
    high, low = split(value)
    return jnp.concatenate([high, high, low], axis=1)


def right(value):
    high, low = split(value)
    return jnp.concatenate([high, low, high], axis=0)


def product(former, latter):
    return jnp.dot(left(former), right(latter), preferred_element_type=F32)


def summed(bounce, value):
    side = bounce.shape[1]
    both = product(bounce, jnp.concatenate([bounce, value], axis=1))
    total = value + both[:, side:]
    return total + product(both[:, :side], total)


def rolled_sum(bounce, value):
    factor = left(bounce)

    def step(_, total):
        return value + jnp.dot(factor, right(total), preferred_element_type=F32)

    return lax.fori_loop(0, 3, step, value)


def staged(body, stride, inputs, outputs, products, dtype=F32):
    def kernel(*refs):
        body(lax.axis_index("sec") // stride, *refs)

    vmem = pl.BlockSpec(memory_space=pltpu.VMEM)
    side = inputs[0].shape[-1]
    moved_bytes = 4 * side * side * (len(inputs) + len(outputs))
    return pl.pallas_call(
        kernel,
        out_shape=[jax.ShapeDtypeStruct(shape, dtype) for shape in outputs],
        in_specs=[vmem] * len(inputs),
        out_specs=[vmem] * len(outputs),
        compiler_params=pltpu.CompilerParams(vmem_limit_bytes=24 * 2**20),
        cost_estimate=pl.CostEstimate(
            flops=int(products * 6 * side**3), bytes_accessed=moved_bytes, transcendentals=0
        ),
    )(*inputs)


def per_device(front_reflect, front_through, back_reflect, back_through, depth_maps, incident):
    length = lax.axis_size("sec")
    stride = length // NODES
    square, field = front_reflect.shape[1:], incident.shape

    def moved(value, routes, start=0, step=1):
        pairs = [
            (a * stride + i, b * stride + i)
            for a, b in routes
            for i in range(start, stride, step)
        ]
        return lax.ppermute(value, "sec", pairs)

    r, t, q, u = front_reflect[0], front_through[0], back_reflect[0], back_through[0]
    width = field[1]
    fields = (field[0], 2 * width)
    low = [(0, 2), (1, 3)]
    back = [(4, 2), (5, 3)]
    middle = [(2, 3), (3, 4), (4, 5)]

    swapped = moved(r, [(7, 6), (6, 7), (1, 0)])
    r2_down = moved(r, [(2, 0)])
    q0 = moved(q, [(0, 1), (1, 2)] + middle)
    t0 = moved(t, [(1, 2)] + middle)
    u1_over = moved(u, [(1, 0)])
    u0 = moved(u, [(4, 5)])
    u0_low = moved(u, [(0, 1), (2, 3), (3, 2)])
    qa_raw = moved(q, [(0, 2)])
    r_late = moved(r, [(3, 2)])
    r_next = moved(r, [(4, 3)])

    def load(k, r, t, q, u, incident, *out):
        for i, ref in enumerate((r, t, q, u)):
            out[i][...] = ref[...]

        @pl.when(k == 0)
        def _():
            value = right(incident[...])
            out[4][:, :width] = jnp.dot(left(t[...]), value, preferred_element_type=F32)
            out[4][:, width:] = jnp.dot(left(r[...]), value, preferred_element_type=F32)

    r, t, q, u, first = staged(load, stride, [r, t, q, u, incident], [square] * 4 + [fields], 1)
    first_came = moved(first, [(0, 1)])

    def pair_reflect(at):
        def body(k, came, r, t, q, u, *rest):
            out, gt_out = rest[-2:]

            @pl.when(k == at)
            def _():
                gt = rolled_sum(product(q[...], came[...]), t[...])
                gt_out[...] = gt
                out[...] = r[...] + product(u[...], product(came[...], gt))

            @pl.when(k != at)
            def _():
                if len(rest) == 3:
                    gt_out[...] = rest[0][...]
                else:
                    out[...] = came[...]

        return body

    (relay, gt) = staged(pair_reflect(6), stride, [swapped, r, t, q, u], [square] * 2, 6)
    hopped = moved(relay, [(6, 7), (7, 5), (0, 2)])
    r2_over = moved(r2_down, [(0, 1)])
    u1_up = moved(u1_over, [(0, 2)])
    r2_up = moved(r2_over, [(1, 3)])

    def forward_q(k, q0, r, t, q, u, q1, hu_out):
        @pl.when(k == 0)
        def _():
            q1[...] = q[...]

        @pl.when((k > 0) & (k < 6))
        def _():
            hu = rolled_sum(product(r[...], q0[...]), u[...])
            hu_out[...] = hu
            q1[...] = q[...] + product(t[...], product(q0[...], hu))

    (q1, hu) = staged(forward_q, stride, [q0, r, t, q, u], [square] * 2, 6)
    qa = moved(q1, [(1, 3)])

    maps = depth_maps[0]

    def forward_t(k, q0, t0, r, t, t1, rgt):
        @pl.when((k > 1) & (k < 6))
        def _():
            gt = rolled_sum(product(q0[...], r[...]), t0[...])
            rgt[...] = product(r[...], gt)
            t1[...] = product(t[...], gt)

    (t1, rgt) = staged(forward_t, stride, [q0, t0, r, t], [square] * 2, 6)

    (relay, gt) = staged(pair_reflect(5), stride, [hopped, r, t, q, u, gt], [square] * 2, 6)
    bounced = moved(relay, [(5, 4)])
    bounced_s = moved(hopped, [(7, 5)])
    gt_came = moved(gt, [(5, 6), (6, 7)])

    def forward_u(k, u0, hu, rgt, u1, w):
        @pl.when(k == 4)
        def _():
            w[...] = rgt[...]
            u1[...] = hu[...]

        @pl.when(k == 5)
        def _():
            factor = left(u0[...])
            w[...] = jnp.dot(factor, right(rgt[...]), preferred_element_type=F32)
            u1[...] = jnp.dot(factor, right(hu[...]), preferred_element_type=F32)

    (u1, w) = staged(forward_u, stride, [u0, hu, rgt], [square] * 2, 2)
    w_came = moved(w, back)

    def low_fields(k, first, came, q0, r, t, f1, rg):
        @pl.when(k == 0)
        def _():
            f1[...] = first[:, :width]

        @pl.when(k == 1)
        def _():
            g = rolled_sum(product(q0[...], r[...]), came[:, :width])
            f1[...] = product(t[...], g)
            rg[...] = product(r[...], g)

    (f1, rg) = staged(low_fields, stride, [first, first_came, q0, r, t], [field] * 2, 2)
    fa = moved(f1, low)

    def second_reflect(k, bounced, bounced_s, q1, t1, u1, w, total, gt_out):
        @pl.when((k == 4) | (k == 5))
        def _():
            came = jnp.where(k == 4, bounced[...], bounced_s[...])
            gt = summed(product(q1[...], came), t1[...])
            gt_out[...] = gt
            total[...] = w[...] + product(u1[...], product(came, gt))

    (total, gt2) = staged(second_reflect, stride, [bounced, bounced_s, q1, t1, u1, w], [square] * 2, 6
    )
    total_came = moved(total, back)
    gt2_came = moved(gt2, [(4, 6), (5, 7)])

    def low_u(k, u0, u1_up, u, hu, rgt, rg, first, came, both, w):
        side = u.shape[1]

        @pl.when(k == 0)
        def _():
            both[:, :side] = u[...]
            both[:, side:] = first[:, width:]

        @pl.when((k > 0) & (k < 4))
        def _():
            factor = left(jnp.where(k == 2, u1_up[...], u0[...]))
            both[:, :side] = jnp.dot(factor, right(hu[...]), preferred_element_type=F32)

            @pl.when(k == 1)
            def _():
                both[:, side:] = came[:, width:] + jnp.dot(
                    factor, right(rg[...]), preferred_element_type=F32
                )

            @pl.when(k > 1)
            def _():
                w[...] = jnp.dot(factor, right(rgt[...]), preferred_element_type=F32)

    (both, w_low) = staged(
        low_u,
        stride,
        [u0_low, u1_up, u, hu, rgt, rg, first, first_came],
        [(square[0], square[1] + width), square],
        2,
    )
    ua = moved(both, low)

    def own_fields(k, r2_up, hopped, w, r1):
        @pl.when(k == 2)
        def _():
            r1[...] = hopped[...] + w[...]

        @pl.when(k == 3)
        def _():
            r1[...] = r2_up[...] + w[...]

    (r1,) = staged(own_fields, stride, [r2_up, hopped, w_low], [square], 0.1)

    def second_q(k, r1, qa_raw, qa, q1, t1, both, q2, hu_out):
        @pl.when((k == 2) | (k == 3))
        def _():
            came = jnp.where(k == 2, qa_raw[...], qa[...])
            hu = summed(product(r1[...], came), both[:, : q1.shape[1]])
            hu_out[...] = hu
            q2[...] = q1[...] + product(t1[...], product(came, hu))

    (q2, hu2) = staged(second_q, stride, [r1, qa_raw, qa, q1, t1, both], [square] * 2, 6)

    def second_fields(k, f1, qa_raw, qa, fa, r1, t1, f2, g2):
        @pl.when(k < 2)
        def _():
            f2[...] = f1[...]

        @pl.when((k == 2) | (k == 3))
        def _():
            came = jnp.where(k == 2, qa_raw[...], qa[...])
            g = summed(product(came, r1[...]), fa[...])
            g2[...] = g
            f2[...] = product(t1[...], g)

    (f2, g2) = staged(second_fields, stride, [f1, qa_raw, qa, fa, r1, t1], [field, field], 2)

    def third_fields(k, r_late, r_next, u3, w_came, q1, t1, both, r1, qa_raw, qa, fa, w4, g4, rc4):
        @pl.when(k == 2)
        def _():
            rc4[...] = r_late[...] + product(u3[...], w_came[...])

        @pl.when(k == 3)
        def _():
            rc4[...] = r_next[...] + w_came[...]

        @pl.when((k == 2) | (k == 3))
        def _():
            came = rc4[...]
            gt = summed(product(q1[...], came), t1[...])
            rc = r1[...] + product(both[:, : q1.shape[1]], product(came, gt))
            rc4[...] = rc
            g = summed(product(jnp.where(k == 2, qa_raw[...], qa[...]), rc), fa[...])
            g4[...] = g
            w4[...] = product(gt, g)

    (w4, g4, rc4) = staged(
        third_fields,
        stride,
        [r_late, r_next, u0_low, w_came, q1, t1, both, r1, qa_raw, qa, fa],
        [field, field, square],
        9,
    )
    w4_came = moved(w4, [(2, 4), (3, 5)])

    def second_through(k, t, gt_came, gt2_came, t2):
        @pl.when(k > 5)
        def _():
            t2[...] = product(product(t[...], gt_came[...]), gt2_came[...])

    (t2,) = staged(second_through, stride, [t, gt_came, gt2_came], [square], 2)

    def last_fields(k, r_late, r_next, u3, total_came, q2, f2, g6, rc6):
        @pl.when(k == 2)
        def _():
            rc6[...] = r_late[...] + product(u3[...], total_came[...])

        @pl.when(k == 3)
        def _():
            rc6[...] = r_next[...] + total_came[...]

        @pl.when((k == 2) | (k == 3))
        def _():
            g6[...] = summed(product(q2[...], rc6[...]), f2[...])

    (g6, rc6) = staged(
        last_fields, stride, [r_late, r_next, u0_low, total_came, q2, f2], [field, square], 3
    )
    g6_one = moved(g6, [(2, 6), (3, 7)], 0, 2)
    g6_two = moved(g6, [(2, 6), (3, 7)], 1, 2)

    def passed(value, choose):
        pairs = [(i, i + 1) for i in range(length - 1) if choose(i)]
        return lax.ppermute(value, "sec", pairs)

    half = NODES // 2 * stride
    next_low = passed(f2, lambda i: i < half)

    def all_reflected(
        k, ua, r1, g2, rc4, g4, rc6, g6, hu2, s2, s4, s6
    ):
        @pl.when((k == 2) | (k == 3))
        def _():
            rg2 = product(r1[...], g2[...])
            rg4 = product(rc4[...], g4[...])
            sums = rg2 + product(hu2[...], product(rc6[...], g6[...]))
            value = product(ua[:, : hu2.shape[1]], jnp.concatenate([rg2, rg4, sums], axis=1))
            for i, out in enumerate((s2, s4, s6)):
                out[...] = ua[:, hu2.shape[1] :] + value[:, i * width : (i + 1) * width]

    (s2, s4, s6) = staged(
        all_reflected, stride, [ua, r1, g2, rc4, g4, rc6, g6, hu2], [field] * 3, 3
    )
    s6_came = moved(s6, [(2, 6), (3, 7)])
    s4_came = moved(s4, [(2, 4), (3, 5)])

    def through_mid(k, f2, t1, w4, out):
        @pl.when(k < 4)
        def _():
            out[...] = f2[...]

        @pl.when((k == 4) | (k == 5))
        def _():
            out[...] = product(t1[...], w4[...])

    (mid,) = staged(through_mid, stride, [f2, t1, w4_came], [field], 0.3)
    top = half + half // 2
    next_mid = passed(mid, lambda i: half <= i < top)

    def through_one(d, mid, t2, g6, out):
        late = (d >= top) & (d % 2 == 0)

        @pl.when(late)
        def _():
            out[...] = product(t2[...], g6[...])

        @pl.when(jnp.logical_not(late))
        def _():
            out[...] = mid[...]

    (one,) = staged(through_one, 1, [mid, t2, g6_one], [field], 0.3)
    next_one = passed(one, lambda i: i >= top and i % 2 == 0)

    def through_two(d, t2, g6, out):
        @pl.when((d >= top) & (d % 2 == 1))
        def _():
            out[...] = product(t2[...], g6[...])

    (two,) = staged(through_two, 1, [t2, g6_two], [field], 0.3)
    next_two = passed(two, lambda i: i >= top and i % 2 == 1)

    def depths(d, maps, low, mid, one, two, incident, out):
        came = jnp.where(d % 2 == 1, one[...], two[...])
        came = jnp.where(d <= top, mid[...], came)
        came = jnp.where(d <= half, low[...], came)
        value = right(jnp.where(d == 0, incident[...], came))
        for j in range(depth_maps.shape[1]):
            out[j] = jnp.dot(left(maps[j]), value, preferred_element_type=F32)

    (depth_fields,) = staged(
        depths,
        1,
        [maps, next_low, next_mid, next_one, next_two, incident],
        [depth_maps.shape[1:3] + field[1:]],
        1,
    )

    def fields_out(d, one, two, both, s2, s4, s6, through, reflected):
        k = d // stride
        late = (d >= top) & (d % 2 == 1)

        @pl.when(late)
        def _():
            through[...] = two[...]

        @pl.when(jnp.logical_not(late))
        def _():
            through[...] = one[...]

        @pl.when(k < 2)
        def _():
            reflected[...] = both[:, square[1] :]

        @pl.when((k == 2) | (k == 3))
        def _():
            reflected[...] = s2[...]

        @pl.when((k == 4) | (k == 5))
        def _():
            reflected[...] = s4[...]

        @pl.when(k > 5)
        def _():
            reflected[...] = s6[...]

    (through_field, reflected) = staged(
        fields_out, 1, [one, two, both, s2, s4_came, s6_came], [field] * 2, 0.1
    )
    return (through_field[None], reflected[None], depth_fields[None])


def solution(mesh):
    in_specs = (
        P("sec", None, None),
        P("sec", None, None),
        P("sec", None, None),
        P("sec", None, None),
        P("sec", None, None, None),
        P(),
    )
    out_specs = (P("sec", None, None), P("sec", None, None), P("sec", None, None, None))

    return jax.shard_map(
        per_device, mesh=mesh, in_specs=in_specs, out_specs=out_specs, check_vma=False
    )
```

```python
import jax
import jax.numpy as jnp
from jax import lax
from jax.experimental import pallas as pl
from jax.experimental.pallas import tpu as pltpu
from jax.sharding import PartitionSpec as P

SEGMENTS = 3
NODES = 2**SEGMENTS
F32 = jnp.float32


def split(value):
    high = value.astype(jnp.bfloat16)
    return high, (value - high.astype(F32)).astype(jnp.bfloat16)


def left(value):
    high, low = split(value)
    return jnp.concatenate([high, high, low], axis=1)


def right(value):
    high, low = split(value)
    return jnp.concatenate([high, low, high], axis=0)


def product(former, latter):
    return jnp.dot(left(former), right(latter), preferred_element_type=F32)


def summed(bounce, value):
    side = bounce.shape[1]
    both = product(bounce, jnp.concatenate([bounce, value], axis=1))
    total = value + both[:, side:]
    return total + product(both[:, :side], total)


def rolled_sum(bounce, value):
    factor = left(bounce)

    def step(_, total):
        return value + jnp.dot(factor, right(total), preferred_element_type=F32)

    return lax.fori_loop(0, 3, step, value)


def staged(body, stride, inputs, outputs, products, dtype=F32):
    def kernel(*refs):
        body(lax.axis_index("sec") // stride, *refs)

    vmem = pl.BlockSpec(memory_space=pltpu.VMEM)
    side = inputs[0].shape[-1]
    moved_bytes = 4 * side * side * (len(inputs) + len(outputs))
    return pl.pallas_call(
        kernel,
        out_shape=[jax.ShapeDtypeStruct(shape, dtype) for shape in outputs],
        in_specs=[vmem] * len(inputs),
        out_specs=[vmem] * len(outputs),
        compiler_params=pltpu.CompilerParams(vmem_limit_bytes=24 * 2**20),
        cost_estimate=pl.CostEstimate(
            flops=int(products * 6 * side**3), bytes_accessed=moved_bytes, transcendentals=0
        ),
    )(*inputs)


def per_device(front_reflect, front_through, back_reflect, back_through, depth_maps, incident):
    length = lax.axis_size("sec")
    stride = length // NODES
    square, field = front_reflect.shape[1:], incident.shape

    def moved(value, routes, start=0, step=1):
        pairs = [
            (a * stride + i, b * stride + i)
            for a, b in routes
            for i in range(start, stride, step)
        ]
        return lax.ppermute(value, "sec", pairs)

    r, t, q, u = front_reflect[0], front_through[0], back_reflect[0], back_through[0]
    width = field[1]
    fields = (field[0], 2 * width)
    low = [(0, 2), (1, 3)]
    back = [(4, 2), (5, 3)]
    middle = [(2, 3), (3, 4), (4, 5)]

    swapped = moved(r, [(7, 6), (6, 7), (1, 0)])
    r2_down = moved(r, [(2, 0)])
    q0 = moved(q, [(0, 1), (1, 2)] + middle)
    t0 = moved(t, [(1, 2)] + middle)
    u1_over = moved(u, [(1, 0)])
    u0 = moved(u, [(3, 4), (4, 5)])
    u0_low = moved(u, [(0, 1), (2, 3)])
    qa_raw = moved(q, [(0, 2)])
    r_late = moved(r, [(3, 2)])
    r_next = moved(r, [(4, 3)])

    def load(k, r, t, q, u, incident, *out):
        for i, ref in enumerate((r, t, q, u)):
            out[i][...] = ref[...]

        @pl.when(k == 0)
        def _():
            value = right(incident[...])
            out[4][:, :width] = jnp.dot(left(t[...]), value, preferred_element_type=F32)
            out[4][:, width:] = jnp.dot(left(r[...]), value, preferred_element_type=F32)

    r, t, q, u, first = staged(load, stride, [r, t, q, u, incident], [square] * 4 + [fields], 1)
    first_came = moved(first, [(0, 1)])

    def pair_reflect(at):
        def body(k, came, r, t, q, u, *rest):
            out, gt_out = rest[-2:]

            @pl.when(k == at)
            def _():
                gt = rolled_sum(product(q[...], came[...]), t[...])
                gt_out[...] = gt
                out[...] = r[...] + product(u[...], product(came[...], gt))

            @pl.when(k != at)
            def _():
                out[...] = came[...]
                if len(rest) == 3:
                    gt_out[...] = rest[0][...]

        return body

    (relay, gt) = staged(pair_reflect(6), stride, [swapped, r, t, q, u], [square] * 2, 6)
    hopped = moved(relay, [(6, 7), (7, 5), (0, 2)])
    r2_over = moved(r2_down, [(0, 1)])
    u1_up = moved(u1_over, [(0, 2)])
    r2_up = moved(r2_over, [(1, 3)])

    def forward_q(k, q0, r, t, q, u, q1, hu_out):
        @pl.when(k == 0)
        def _():
            q1[...] = q[...]

        @pl.when((k > 0) & (k < 6))
        def _():
            hu = rolled_sum(product(r[...], q0[...]), u[...])
            hu_out[...] = hu
            q1[...] = q[...] + product(t[...], product(q0[...], hu))

    (q1, hu) = staged(forward_q, stride, [q0, r, t, q, u], [square] * 2, 6)
    qa = moved(q1, [(1, 3)])

    maps = depth_maps[0]

    def forward_t(k, q0, t0, r, t, t1, rgt):
        @pl.when((k > 1) & (k < 6))
        def _():
            gt = rolled_sum(product(q0[...], r[...]), t0[...])
            rgt[...] = product(r[...], gt)
            t1[...] = product(t[...], gt)

    (t1, rgt) = staged(forward_t, stride, [q0, t0, r, t], [square] * 2, 6)

    (relay, gt) = staged(pair_reflect(5), stride, [hopped, r, t, q, u, gt], [square] * 2, 6)
    bounced = moved(relay, [(5, 4)])
    bounced_s = moved(hopped, [(7, 5)])
    gt_came = moved(gt, [(5, 6), (6, 7)])

    def forward_u(k, u0, hu, rgt, u1, w):
        @pl.when((k == 4) | (k == 5))
        def _():
            factor = left(u0[...])
            w[...] = jnp.dot(factor, right(rgt[...]), preferred_element_type=F32)
            u1[...] = jnp.dot(factor, right(hu[...]), preferred_element_type=F32)

    (u1, w) = staged(forward_u, stride, [u0, hu, rgt], [square] * 2, 2)
    w_came = moved(w, back)

    def low_fields(k, first, came, q0, r, t, f1, rg):
        @pl.when(k == 0)
        def _():
            f1[...] = first[:, :width]

        @pl.when(k == 1)
        def _():
            g = rolled_sum(product(q0[...], r[...]), came[:, :width])
            f1[...] = product(t[...], g)
            rg[...] = product(r[...], g)

    (f1, rg) = staged(low_fields, stride, [first, first_came, q0, r, t], [field] * 2, 2)
    fa = moved(f1, low)

    def second_reflect(k, bounced, bounced_s, q1, t1, u1, w, total, gt_out):
        @pl.when((k == 4) | (k == 5))
        def _():
            came = jnp.where(k == 4, bounced[...], bounced_s[...])
            gt = summed(product(q1[...], came), t1[...])
            gt_out[...] = gt
            total[...] = w[...] + product(u1[...], product(came, gt))

    (total, gt2) = staged(second_reflect, stride, [bounced, bounced_s, q1, t1, u1, w], [square] * 2, 6
    )
    total_came = moved(total, back)
    gt2_came = moved(gt2, [(4, 6), (5, 7)])

    def low_u(k, u0, u1_up, u, hu, rgt, rg, first, came, both, w):
        side = u.shape[1]

        @pl.when(k == 0)
        def _():
            both[:, :side] = u[...]
            both[:, side:] = first[:, width:]

        @pl.when((k > 0) & (k < 4))
        def _():
            factor = left(jnp.where(k == 2, u1_up[...], u0[...]))
            both[:, :side] = jnp.dot(factor, right(hu[...]), preferred_element_type=F32)

            @pl.when(k == 1)
            def _():
                both[:, side:] = came[:, width:] + jnp.dot(
                    factor, right(rg[...]), preferred_element_type=F32
                )

            @pl.when(k > 1)
            def _():
                w[...] = jnp.dot(factor, right(rgt[...]), preferred_element_type=F32)

    (both, w_low) = staged(
        low_u,
        stride,
        [u0_low, u1_up, u, hu, rgt, rg, first, first_came],
        [(square[0], square[1] + width), square],
        2,
    )
    ua = moved(both, low)

    def own_fields(k, r2_up, hopped, w, r1):
        @pl.when(k == 2)
        def _():
            r1[...] = hopped[...] + w[...]

        @pl.when(k == 3)
        def _():
            r1[...] = r2_up[...] + w[...]

    (r1,) = staged(own_fields, stride, [r2_up, hopped, w_low], [square], 0.1)

    def second_q(k, r1, qa_raw, qa, q1, t1, both, q2, hu_out):
        @pl.when((k == 2) | (k == 3))
        def _():
            came = jnp.where(k == 2, qa_raw[...], qa[...])
            hu = summed(product(r1[...], came), both[:, : q1.shape[1]])
            hu_out[...] = hu
            q2[...] = q1[...] + product(t1[...], product(came, hu))

    (q2, hu2) = staged(second_q, stride, [r1, qa_raw, qa, q1, t1, both], [square] * 2, 6)

    def second_fields(k, f1, qa_raw, qa, fa, r1, t1, f2, g2):
        @pl.when(k < 2)
        def _():
            f2[...] = f1[...]

        @pl.when((k == 2) | (k == 3))
        def _():
            came = jnp.where(k == 2, qa_raw[...], qa[...])
            g = summed(product(came, r1[...]), fa[...])
            g2[...] = g
            f2[...] = product(t1[...], g)

    (f2, g2) = staged(second_fields, stride, [f1, qa_raw, qa, fa, r1, t1], [field, field], 2)

    def third_fields(k, r_late, r_next, w_came, q1, t1, both, r1, qa_raw, qa, fa, w4, g4, rc4):
        @pl.when((k == 2) | (k == 3))
        def _():
            came = jnp.where(k == 2, r_late[...], r_next[...]) + w_came[...]
            gt = summed(product(q1[...], came), t1[...])
            rc = r1[...] + product(both[:, : q1.shape[1]], product(came, gt))
            rc4[...] = rc
            g = summed(product(jnp.where(k == 2, qa_raw[...], qa[...]), rc), fa[...])
            g4[...] = g
            w4[...] = product(gt, g)

    (w4, g4, rc4) = staged(
        third_fields,
        stride,
        [r_late, r_next, w_came, q1, t1, both, r1, qa_raw, qa, fa],
        [field, field, square],
        9,
    )
    w4_came = moved(w4, [(2, 4), (3, 5)])

    def second_through(k, t, gt_came, gt2_came, t2):
        @pl.when(k > 5)
        def _():
            t2[...] = product(product(t[...], gt_came[...]), gt2_came[...])

    (t2,) = staged(second_through, stride, [t, gt_came, gt2_came], [square], 2)

    def last_fields(k, r_late, r_next, total_came, q2, f2, g6):
        @pl.when((k == 2) | (k == 3))
        def _():
            rc = jnp.where(k == 2, r_late[...], r_next[...]) + total_came[...]
            g6[...] = summed(product(q2[...], rc), f2[...])

    (g6,) = staged(last_fields, stride, [r_late, r_next, total_came, q2, f2], [field], 3)
    g6_odd = moved(g6, [(2, 6), (3, 7)], 1, 2)
    g6_even = moved(g6, [(2, 6), (3, 7)], 0, 2)

    def passed(value, choose):
        pairs = [(i, i + 1) for i in range(length - 1) if choose(i)]
        return lax.ppermute(value, "sec", pairs)

    half = NODES // 2 * stride
    next_low = passed(f2, lambda i: i < half)

    def all_reflected(
        k, ua, r1, g2, rc4, g4, r_late, r_next, total_came, g6, hu2, s2, s4, s6
    ):
        @pl.when((k == 2) | (k == 3))
        def _():
            rc = jnp.where(k == 2, r_late[...], r_next[...]) + total_came[...]
            rg2 = product(r1[...], g2[...])
            rg4 = product(rc4[...], g4[...])
            sums = rg2 + product(hu2[...], product(rc, g6[...]))
            value = product(ua[:, : hu2.shape[1]], jnp.concatenate([rg2, rg4, sums], axis=1))
            for i, out in enumerate((s2, s4, s6)):
                out[...] = ua[:, hu2.shape[1] :] + value[:, i * width : (i + 1) * width]

    (s2, s4, s6) = staged(
        all_reflected,
        stride,
        [ua, r1, g2, rc4, g4, r_late, r_next, total_came, g6, hu2],
        [field] * 3,
        3,
    )
    s6_came = moved(s6, [(2, 6), (3, 7)])
    s4_came = moved(s4, [(2, 4), (3, 5)])

    def through_mid(k, f2, t1, w4, out):
        @pl.when(k < 4)
        def _():
            out[...] = f2[...]

        @pl.when((k == 4) | (k == 5))
        def _():
            out[...] = product(t1[...], w4[...])

    (mid,) = staged(through_mid, stride, [f2, t1, w4_came], [field], 0.3)
    top = half + half // 2
    next_mid = passed(mid, lambda i: half <= i < top)

    def through_odd(d, mid, t2, g6, out):
        late = (d >= top) & (d % 2 == 1)

        @pl.when(late)
        def _():
            out[...] = product(t2[...], g6[...])

        @pl.when(jnp.logical_not(late))
        def _():
            out[...] = mid[...]

    (odd,) = staged(through_odd, 1, [mid, t2, g6_odd], [field], 0.3)
    next_odd = passed(odd, lambda i: i >= top and i % 2 == 1)

    def through_even(d, t2, g6, out):
        @pl.when((d >= top) & (d % 2 == 0))
        def _():
            out[...] = product(t2[...], g6[...])

    (even,) = staged(through_even, 1, [t2, g6_even], [field], 0.3)
    next_even = passed(even, lambda i: i >= top and i % 2 == 0)

    def depths(d, maps, low, mid, odd, even, incident, out):
        came = jnp.where(d % 2 == 1, even[...], odd[...])
        came = jnp.where(d <= top, mid[...], came)
        came = jnp.where(d <= half, low[...], came)
        value = right(jnp.where(d == 0, incident[...], came))
        for j in range(depth_maps.shape[1]):
            out[j] = jnp.dot(left(maps[j]), value, preferred_element_type=F32)

    (depth_fields,) = staged(
        depths,
        1,
        [maps, next_low, next_mid, next_odd, next_even, incident],
        [depth_maps.shape[1:3] + field[1:]],
        1,
    )

    def fields_out(d, odd, even, both, s2, s4, s6, through, reflected):
        k = d // stride
        late = (d >= top) & (d % 2 == 0)

        @pl.when(late)
        def _():
            through[...] = even[...]

        @pl.when(jnp.logical_not(late))
        def _():
            through[...] = odd[...]

        @pl.when(k < 2)
        def _():
            reflected[...] = both[:, square[1] :]

        @pl.when((k == 2) | (k == 3))
        def _():
            reflected[...] = s2[...]

        @pl.when((k == 4) | (k == 5))
        def _():
            reflected[...] = s4[...]

        @pl.when(k > 5)
        def _():
            reflected[...] = s6[...]

    (through_field, reflected) = staged(
        fields_out, 1, [odd, even, both, s2, s4_came, s6_came], [field] * 2, 0.1
    )
    return (through_field[None], reflected[None], depth_fields[None])


def solution(mesh):
    in_specs = (
        P("sec", None, None),
        P("sec", None, None),
        P("sec", None, None),
        P("sec", None, None),
        P("sec", None, None, None),
        P(),
    )
    out_specs = (P("sec", None, None), P("sec", None, None), P("sec", None, None, None))

    return jax.shard_map(
        per_device, mesh=mesh, in_specs=in_specs, out_specs=out_specs, check_vma=False
    )
```
